256 devices in a mesh: segment: 2 (over z_lo), tm: 4 (over x), space: 32 (over z_hi, y, core).
Axes of the slice: x: 4, y: 4, z: 8 (z_hi: 4, z_lo: 2; z = z_hi * 2 + z_lo), core: 2. Of those that a mesh axis runs over, the one named last changes fastest.
Arguments:
- video_clips: float32 [2, 8, 128, 32, 128], P(None, 'tm', 'space'), may hold values from -6 to 6
- conv_weights: float32 [2, 3456, 128], P('segment'), may hold values from -0.109375 to 0.109375
Outputs:
- weight_grads: float32 [2, 3456, 128], P('segment')
The draws below stay inside these ranges and needn't reach their ends.
All inputs are finite; a program needn't handle non-finite values.
Results may differ from the reference program's by a relative error of at most 0.000091.
Values sent between devices are 32-bit elements; how exact they have to be, the bound alone decides.
A program may use at most 64 MiB of HBM per device.

```python
import jax
import jax.numpy as jnp
from jax import lax

C = 128
CLIPS = 2
COLS = 32
FRAMES = 8
ROWS = 128


def levels(stream_key, dims, shards, least, largest):
    loudness = 1.0
    for dim, shards_of in shards:
        steps = jax.random.uniform(jax.random.fold_in(jax.random.fold_in(stream_key, 6), dim), (shards_of,), jnp.float32, least / len(shards), largest / len(shards))
        loudness = loudness * jnp.repeat(jnp.exp(steps), dims[dim] // shards_of).reshape((-1,) + (1,) * (len(dims) - 1 - dim))
    return loudness


def normal_values(rng, dims, width, bound, split=(), kind=jnp.bfloat16):
    array = jax.random.normal(rng, dims, jnp.float32) * width
    if len(split) > 0:
        array = levels(rng, dims, split, -0.22, 0.18) * array
    return jnp.clip(array, min=-bound, max=bound).astype(kind)


def setup_inputs(seed: int = 0) -> dict:
    streams_of = jax.random.split(jax.random.key(seed), 3)
    return {
        "video_clips": normal_values(streams_of[0], (CLIPS, FRAMES, ROWS, COLS, C), 1.0, 6.0, ((1, 4), (2, 32)), jnp.float32),
        "conv_weights": normal_values(streams_of[1], (2, 27 * C, C), (27 * C) ** -0.5, 0.109375, ((0, 2),), jnp.float32),
    }


def convolve(field_in, weight):
    kernel = weight.reshape(3, 3, 3, C, C)
    return lax.conv_general_dilated(field_in, kernel, (1, 1, 1), ((2, 0), (1, 1), (1, 1)), dimension_numbers=('NDHWC', 'DHWIO', 'NDHWC'), precision=lax.Precision.HIGHEST)

def reference(video_clips, conv_weights):
    factor = float(CLIPS * FRAMES * ROWS * COLS) ** (-0.5)

    def forward(encoder, decoder):
        return convolve(jax.nn.silu(convolve(video_clips, encoder)), decoder)
    decoded, pullback = jax.vjp(forward, conv_weights[0], conv_weights[1])
    cotangent = (decoded - video_clips) * factor
    grad_encoder, grad_decoder = pullback(cotangent)
    return jnp.stack([grad_encoder, grad_decoder])
```

```python
import functools

import jax
import jax.numpy as jnp
from jax import lax
from jax.experimental import pallas as pl
from jax.experimental.pallas import tpu as pltpu
from jax.sharding import Mesh
from jax.sharding import PartitionSpec as P

MESH = pl.DeviceIdType.MESH
AXES = ("segment", "tm", "zh", "y", "core")
F32 = jnp.float32
BF16 = jnp.bfloat16
TAPS = 27
PAD = 28
GROUPS = 16
QUARTER = 288


def kernel(
    vid_ref, w_ref, out_ref,
    vext, lext, cext,
    pvh, pvl, plh, pll, pch, pcl,
    wboth, wc0, wc1, wct,
    acc, slope, gcat,
    g0, g1, ra0, ra1, rb, sb, rc, tt, rd, re, uu,
    local_sem, send_sem, recv_sem,
):
    seg = lax.axis_index("segment")
    x = lax.axis_index("tm")
    zh = lax.axis_index("zh")
    y = lax.axis_index("y")
    c = lax.axis_index("core")
    s = zh * 8 + y * 2 + c
    counter = [0]

    def spot(index, **others):
        index = lax.rem(index + 32, 32)
        return {"zh": index // 8, "y": lax.rem(index // 2, 4), "core": lax.rem(index, 2), **others}

    def ring(value, step):
        return lax.rem(value + step + 4, 4)

    other = 1 - seg
    link_b = ring(zh, 2 * seg - 1)

    def remote(src, dst, device):
        slot = counter[0]
        counter[0] += 1
        return pltpu.make_async_remote_copy(
            src_ref=src,
            dst_ref=dst,
            send_sem=send_sem.at[slot],
            recv_sem=recv_sem.at[slot],
            device_id=device,
            device_id_type=MESH,
        )

    own_w = pltpu.make_async_copy(w_ref.at[0], wboth.at[seg], local_sem.at[0])
    own_w.start()
    for ext in (vext, lext, cext):
        ext[...] = jnp.zeros_like(ext)
    vext[2:4, 1:5] = vid_ref[seg]
    for g in (g0, g1):
        g[:, TAPS] = jnp.zeros((GROUPS, 8, 128), F32)

    barrier = pltpu.get_barrier_semaphore()
    greet = [{"tm": ring(x, d)} for d in (1, 2, 3)]
    greet += [{"y": ring(y, d)} for d in (1, 2, 3)]
    greet += [{"zh": ring(zh, d)} for d in (1, 2, 3)]
    greet += [{"core": 1 - c}, {"segment": other}, {"segment": other, "zh": link_b}]
    greet += [spot(s + 1), spot(s - 1)]
    greet += [spot(s + dy, tm=ring(x, dx)) for dy in (1, -1) for dx in (1, -1)]
    for device in greet:
        pl.semaphore_signal(barrier, inc=1, device_id=device, device_id_type=MESH)
    pl.semaphore_wait(barrier, len(greet))

    def quarter(step, part, core):
        return pl.ds(step * 1152 + (part * 2 + core) * QUARTER, QUARTER)

    w_copies = {}
    w_relays = {}
    for step in range(3):
        for part in range(2):
            rows = quarter(step, part, c)
            device = {"segment": other} if part == 0 else {"segment": other, "zh": link_b}
            w_copies[step, part] = remote(w_ref.at[0, rows], wboth.at[seg, rows], device)
            w_relays[step, part] = remote(
                wboth.at[other, rows], wboth.at[other, rows], {"core": 1 - c}
            )

    def halo(ext, own, far, shift):
        ahead = {"tm": ring(x, shift)}
        sends_x = (x < 3) if shift == 1 else (x > 0)
        gets_x = (x > 0) if shift == 1 else (x < 3)
        moves = [
            (remote(ext.at[own:own + 2, 1:5], ext.at[far:far + 2, 1:5], ahead), sends_x, gets_x)
        ]
        for dy in (1, -1):
            src_row, dst_row = (4, 0) if dy == 1 else (1, 5)
            sends = (s < 31) if dy == 1 else (s > 0)
            gets = (s > 0) if dy == 1 else (s < 31)
            row = ext.at[own:own + 2, src_row]
            moves.append(
                (
                    remote(row, ext.at[far:far + 2, dst_row], spot(s + dy, **ahead)),
                    jnp.logical_and(sends, sends_x),
                    jnp.logical_and(gets, gets_x),
                )
            )
            moves.append((remote(row, ext.at[own:own + 2, dst_row], spot(s + dy)), sends, gets))
        return moves

    def start_halo(moves):
        for copy, sends, _ in moves:
            pl.when(sends)(copy.start)

    def finish_halo(moves):
        for copy, sends, gets in moves:
            pl.when(gets)(copy.wait_recv)
            pl.when(sends)(copy.wait_send)

    for step in range(3):
        for part in range(2):
            w_copies[step, part].start()
    video_halo = halo(vext, 2, 0, 1)
    start_halo(video_halo)

    column = lax.broadcasted_iota(jnp.int32, (32, 128), 0)

    def build(ext, high, low):
        @pl.loop(0, 4)
        def _(frame):
            base = pl.multiple_of(frame * 128, 128)
            for line in range(6):
                value = ext[frame, line]
                for e in range(3):
                    if e == 0:
                        moved = jnp.where(column == 0, 0.0, pltpu.roll(value, 1, 0))
                    elif e == 2:
                        moved = jnp.where(column == 31, 0.0, pltpu.roll(value, 31, 0))
                    else:
                        moved = value
                    top = moved.astype(BF16)
                    rest = (moved - top.astype(F32)).astype(BF16)
                    for b in range(3):
                        r = line - b
                        if 0 <= r < 4:
                            lanes = slice((b * 3 + e) * 128, (b * 3 + e + 1) * 128)
                            high[pl.ds(base + r * 32, 32), lanes] = top
                            low[pl.ds(base + r * 32, 32), lanes] = rest

    def split(value):
        top = value.astype(BF16)
        return top, (value - top.astype(F32)).astype(BF16)

    def conv_step(high, low, weight, step, first):
        rows = pl.ds(step * 128, 256)
        lines = pl.ds(step * 1152, 1152)
        both = jnp.dot(high[rows, :], weight[lines, :], preferred_element_type=F32)
        rest = jnp.dot(low[rows, :], weight[lines, 0:128], preferred_element_type=F32)
        total = both[:, 0:128] + both[:, 128:256] + rest
        if first:
            acc[...] = total
        else:
            acc[...] += total

    def weight_grad(high, low, g):
        @pl.loop(0, 3)
        def _(step):
            rows = pl.ds(pl.multiple_of(step * 128, 128), 256)
            dims = (((0,), (0,)), ((), ()))
            both = lax.dot_general(high[rows, :], gcat[...], dims, preferred_element_type=F32)
            rest = lax.dot_general(
                low[rows, :], gcat[:, 0:128], dims, preferred_element_type=F32
            )
            total = both[:, 0:128] + both[:, 128:256] + rest
            for k in range(9):
                g[:, step * 9 + k] = total[k * 128:(k + 1) * 128].reshape(GROUPS, 8, 128)

    finish_halo(video_halo)
    build(vext, pvh, pvl)
    own_w.wait()

    for index, step in enumerate((2, 1, 0)):
        for part in range(2):
            w_copies[step, part].wait_recv()
            w_relays[step, part].start()
        for part in range(2):
            w_relays[step, part].wait_recv()

        @pl.loop(step * 9, step * 9 + 9)
        def _(tap):
            rows = pl.ds(pl.multiple_of(tap * 128, 128), 128)
            flipped = pl.ds(pl.multiple_of((TAPS - 1 - tap) * 128, 128), 128)
            first = wboth[0, rows]
            second = wboth[1, rows]
            for value, ref, place in ((first, wc0, rows), (second, wc1, rows), (second.T, wct, flipped)):
                top, rest = split(value)
                ref[place, 0:128] = top
                ref[place, 128:256] = rest

        conv_step(pvh, pvl, wc0, step, index == 0)

    hidden = acc[...]
    sigmoid = 1.0 / (1.0 + jnp.exp(-hidden))
    slope[...] = sigmoid * (1.0 + hidden * (1.0 - sigmoid))
    lext[2:4, 1:5] = (hidden / (1.0 + jnp.exp(-hidden))).reshape(2, 4, 32, 128)
    latent_halo = halo(lext, 2, 0, 1)
    start_halo(latent_halo)
    finish_halo(latent_halo)
    build(lext, plh, pll)
    for step in range(3):
        conv_step(plh, pll, wc1, step, step == 0)
    cot = (acc[...] - vext[2:4, 1:5].reshape(256, 128)) * (65536.0 ** -0.5)
    cext[0:2, 1:5] = cot.reshape(2, 4, 32, 128)
    cot_halo = halo(cext, 0, 2, -1)
    start_halo(cot_halo)
    top, rest = split(cot)
    gcat[:, 0:128] = top
    gcat[:, 128:256] = rest
    weight_grad(plh, pll, g1)

    class Sum:
        def __init__(self, sec, g, ra):
            self.sec, self.g, self.ra = sec, g, ra
            self.mine = seg == sec

        def start_pair(self):
            self.pair = remote(self.g.at[pl.ds((1 - c) * 8, 8)], self.ra, {"core": 1 - c})
            self.pair.start()

        def start_first(self):
            self.pair.wait()
            g, ra = self.g, self.ra
            half = pl.ds(c * 8, 8)
            g[half] += ra[...]
            self.first = []
            for h, (axis, place) in enumerate((("tm", x), ("y", y))):
                for d in (2, 1, 3):
                    peer = ring(place, d)
                    copy = remote(
                        g.at[c * 8 + h * 4 + peer], rb.at[self.sec, h, d - 1], {axis: peer}
                    )
                    copy.start()
                    self.first.append(copy)

        def start_second(self):
            for copy in self.first:
                copy.wait()
            sec = self.sec
            self.second = []
            for h, place in enumerate((x, y)):
                sb[sec, h] = (
                    self.g[c * 8 + h * 4 + place] + rb[sec, h, 0] + rb[sec, h, 1] + rb[sec, h, 2]
                )
            for h, (axis, place) in enumerate((("y", y), ("tm", x))):
                for d in (2, 1, 3):
                    peer = ring(place, d)
                    copy = remote(
                        sb.at[sec, h, pl.ds(peer * 7, 7)], rc.at[sec, h, d - 1], {axis: peer}
                    )
                    copy.start()
                    self.second.append(copy)

        def start_third(self):
            for copy in self.second:
                copy.wait()
            sec = self.sec
            for h, place in enumerate((y, x)):
                tt[sec, h] = (
                    sb[sec, h, pl.ds(place * 7, 7)] + rc[sec, h, 0] + rc[sec, h, 1] + rc[sec, h, 2]
                )
            self.cross = remote(tt.at[sec], rd, {"segment": other})
            pl.when(jnp.logical_not(self.mine))(self.cross.start)

        def start_fourth(self):
            pl.when(jnp.logical_not(self.mine))(self.cross.wait_send)
            self.fourth = [
                remote(tt.at[self.sec], re.at[d - 1], {"zh": ring(zh, d)}) for d in (2, 1, 3)
            ]

            @pl.when(self.mine)
            def _():
                self.cross.wait_recv()
                tt[self.sec] += rd[...]
                for copy in self.fourth:
                    copy.start()

        def rest(self):
            self.fifth = []
            self.sixth = []
            for h, (axis, place, axis2, place2) in enumerate((("y", y, "tm", x), ("tm", x, "y", y))):
                group = c * 8 + h * 4 + place2
                taps = pl.ds(place * 7, 7)
                for d in (2, 1, 3):
                    self.fifth.append(
                        remote(uu.at[h], out_ref.at[taps, group], {axis: ring(place, d)})
                    )
                for d in (2, 1, 3):
                    self.sixth.append(
                        remote(
                            out_ref.at[:, group], out_ref.at[:, group], {axis2: ring(place2, d)}
                        )
                    )
            half = out_ref.at[:, pl.ds(c * 8, 8)]
            self.last = remote(half, half, {"core": 1 - c})

            @pl.when(self.mine)
            def _():
                for copy in self.fourth:
                    copy.wait()
                uu[...] = tt[self.sec] + re[0] + re[1] + re[2]
                for copy in self.fifth:
                    copy.start()
                for h, (place, place2) in enumerate(((y, x), (x, y))):
                    out_ref[pl.ds(place * 7, 7), c * 8 + h * 4 + place2] = uu[h]
                for copy in self.fifth:
                    copy.wait()
                for copy in self.sixth:
                    copy.start()
                for copy in self.sixth:
                    copy.wait()
                self.last.start()
                self.last.wait()

    decoder = Sum(1, g1, ra1)
    encoder = Sum(0, g0, ra0)
    decoder.start_pair()
    decoder.start_first()

    finish_halo(cot_halo)
    build(cext, pch, pcl)
    for step in range(3):
        conv_step(pch, pcl, wct, step, step == 0)
    top, rest = split(acc[...] * slope[...])
    gcat[:, 0:128] = top
    gcat[:, 128:256] = rest
    weight_grad(pvh, pvl, g0)
    encoder.start_pair()
    decoder.start_second()
    encoder.start_first()
    decoder.start_third()
    decoder.start_fourth()
    encoder.start_second()
    encoder.start_third()
    encoder.start_fourth()
    decoder.rest()
    encoder.rest()

    for step in range(3):
        for part in range(2):
            w_copies[step, part].wait_send()
            w_relays[step, part].wait_send()


def local(video_clips, conv_weights):
    vm = pltpu.VMEM
    ext = vm((4, 6, 32, 128), F32)
    patches = vm((512, 1152), BF16)
    wcat = vm((3456, 256), BF16)
    grads = vm((GROUPS, PAD, 8, 128), F32)
    half = vm((8, PAD, 8, 128), F32)
    summed = pl.pallas_call(
        kernel,
        out_shape=jax.ShapeDtypeStruct((PAD, GROUPS, 8, 128), F32),
        in_specs=[pl.BlockSpec(memory_space=pltpu.VMEM)] * 2,
        out_specs=pl.BlockSpec(memory_space=pltpu.VMEM),
        scratch_shapes=[
            ext, ext, ext,
            patches, patches, patches, patches, patches, patches,
            vm((2, 3456, 128), F32), wcat, wcat, wcat,
            vm((256, 128), F32), vm((256, 128), F32), vm((256, 256), BF16),
            grads, grads, half, half,
            vm((2, 2, 3, PAD, 8, 128), F32),
            vm((2, 2, PAD, 8, 128), F32),
            vm((2, 2, 3, 7, 8, 128), F32),
            vm((2, 2, 7, 8, 128), F32),
            vm((2, 7, 8, 128), F32),
            vm((3, 2, 7, 8, 128), F32),
            vm((2, 7, 8, 128), F32),
            pltpu.SemaphoreType.DMA((1,)),
            pltpu.SemaphoreType.DMA((96,)),
            pltpu.SemaphoreType.DMA((96,)),
        ],
        compiler_params=pltpu.CompilerParams(
            collective_id=0, has_side_effects=True, vmem_limit_bytes=60 * 1024 * 1024
        ),
        name="step",
    )(video_clips, conv_weights)
    return summed[:TAPS].reshape(1, TAPS * 128, 128)


def solution(mesh):
    finer = Mesh(
        mesh.devices.reshape(mesh.shape["segment"], mesh.shape["tm"], 4, 4, 2), AXES
    )
    in_specs = (P(None, "tm", ("zh", "y", "core"), None, None), P("segment", None, None))
    return jax.shard_map(
        local, mesh=finer, in_specs=in_specs, out_specs=P("segment", None, None), check_vma=False
    )
```

```python
import jax
import jax.numpy as jnp
from jax import lax
from jax.experimental import pallas as pl
from jax.experimental.pallas import tpu as pltpu
from jax.sharding import Mesh
from jax.sharding import PartitionSpec as P

MESH = pl.DeviceIdType.MESH
AXES = ("segment", "tm", "zh", "y", "core")
F32 = jnp.float32
BF16 = jnp.bfloat16
TAPS = 27
PAD = 28
GROUPS = 16
QUARTER = 288


def kernel(
    vid_ref, w_ref, out_ref,
    vext, lext, cext,
    pvh, pvl, plh, pll, pch, pcl,
    wboth, wc0, wc1, wct,
    acc, slope, gcat,
    g0, g1, ra0, ra1, rb, sb, rc, tt, rd, re, uu, full,
    local_sem, send_sem, recv_sem,
):
    seg = lax.axis_index("segment")
    x = lax.axis_index("tm")
    zh = lax.axis_index("zh")
    y = lax.axis_index("y")
    c = lax.axis_index("core")
    s = zh * 8 + y * 2 + c
    counter = [0]

    def spot(index, **others):
        index = lax.rem(index + 32, 32)
        return {"zh": index // 8, "y": lax.rem(index // 2, 4), "core": lax.rem(index, 2), **others}

    def ring(value, step):
        return lax.rem(value + step + 4, 4)

    other = 1 - seg
    link_b = ring(zh, 2 * seg - 1)

    def remote(src, dst, device):
        slot = counter[0]
        counter[0] += 1
        return pltpu.make_async_remote_copy(
            src_ref=src,
            dst_ref=dst,
            send_sem=send_sem.at[slot],
            recv_sem=recv_sem.at[slot],
            device_id=device,
            device_id_type=MESH,
        )

    own_w = pltpu.make_async_copy(w_ref.at[0], wboth.at[seg], local_sem.at[0])
    own_v = pltpu.make_async_copy(vid_ref.at[seg], vext.at[2:4, 1:5], local_sem.at[1])
    own_v.start()
    own_w.start()
    for ext, edge, far in ((vext, x == 0, 0), (lext, x == 0, 0), (cext, x == 3, 2)):
        @pl.when(edge)
        def _():
            ext[far:far + 2] = jnp.zeros((2, 6, 32, 128), F32)

        for rim, line in ((s == 0, 0), (s == 31, 5)):
            @pl.when(rim)
            def _():
                ext[:, line] = jnp.zeros((4, 32, 128), F32)

    for g in (g0, g1):
        g[:, TAPS] = jnp.zeros((GROUPS, 8, 128), F32)

    barrier = pltpu.get_barrier_semaphore()
    greet = [{"tm": ring(x, d)} for d in (1, 2, 3)]
    greet += [{"y": ring(y, d)} for d in (1, 2, 3)]
    greet += [{"zh": ring(zh, d)} for d in (1, 2, 3)]
    greet += [{"core": 1 - c}, {"segment": other}, {"segment": other, "zh": link_b}]
    greet += [spot(s + 1), spot(s - 1)]
    greet += [spot(s + dy, tm=ring(x, dx)) for dy in (1, -1) for dx in (1, -1)]
    for device in greet:
        pl.semaphore_signal(barrier, inc=1, device_id=device, device_id_type=MESH)
    pl.semaphore_wait(barrier, len(greet))

    def quarter(step, part, core):
        return pl.ds(step * 1152 + (part * 2 + core) * QUARTER, QUARTER)

    w_copies = {}
    w_relays = {}
    for step in range(3):
        for part in range(2):
            rows = quarter(step, part, c)
            device = {"segment": other} if part == 0 else {"segment": other, "zh": link_b}
            w_copies[step, part] = remote(w_ref.at[0, rows], wboth.at[seg, rows], device)
            w_relays[step, part] = remote(
                wboth.at[other, rows], wboth.at[other, rows], {"core": 1 - c}
            )

    def halo(ext, own, far, shift):
        ahead = {"tm": ring(x, shift)}
        sends_x = (x < 3) if shift == 1 else (x > 0)
        gets_x = (x > 0) if shift == 1 else (x < 3)
        moves = [
            (remote(ext.at[own:own + 2, 1:5], ext.at[far:far + 2, 1:5], ahead), sends_x, gets_x)
        ]
        for dy in (1, -1):
            src_row, dst_row = (4, 0) if dy == 1 else (1, 5)
            sends = (s < 31) if dy == 1 else (s > 0)
            gets = (s > 0) if dy == 1 else (s < 31)
            row = ext.at[own:own + 2, src_row]
            moves.append(
                (
                    remote(row, ext.at[far:far + 2, dst_row], spot(s + dy, **ahead)),
                    jnp.logical_and(sends, sends_x),
                    jnp.logical_and(gets, gets_x),
                )
            )
            moves.append((remote(row, ext.at[own:own + 2, dst_row], spot(s + dy)), sends, gets))
        return moves

    def start_halo(moves):
        for copy, sends, _ in moves:
            pl.when(sends)(copy.start)

    def finish_halo(moves):
        for copy, sends, gets in moves:
            pl.when(gets)(copy.wait_recv)
            pl.when(sends)(copy.wait_send)

    for step in (2, 1, 0):
        for part in range(2):
            w_copies[step, part].start()
    own_v.wait()
    video_halo = halo(vext, 2, 0, 1)
    start_halo(video_halo)

    column = lax.broadcasted_iota(jnp.int32, (32, 128), 0)

    def build(ext, high, low):
        @pl.loop(0, 4)
        def _(frame):
            base = pl.multiple_of(frame * 128, 128)
            for line in range(6):
                value = ext[frame, line]
                for e in range(3):
                    if e == 0:
                        moved = jnp.where(column == 0, 0.0, pltpu.roll(value, 1, 0))
                    elif e == 2:
                        moved = jnp.where(column == 31, 0.0, pltpu.roll(value, 31, 0))
                    else:
                        moved = value
                    top = moved.astype(BF16)
                    rest = (moved - top.astype(F32)).astype(BF16)
                    for b in range(3):
                        r = line - b
                        if 0 <= r < 4:
                            lanes = slice((b * 3 + e) * 128, (b * 3 + e + 1) * 128)
                            high[pl.ds(base + r * 32, 32), lanes] = top
                            low[pl.ds(base + r * 32, 32), lanes] = rest

    def split(value):
        top = value.astype(BF16)
        return top, (value - top.astype(F32)).astype(BF16)

    def conv_step(high, low, weight, step, first):
        rows = pl.ds(step * 128, 256)
        lines = pl.ds(step * 1152, 1152)
        both = jnp.dot(high[rows, :], weight[lines, :], preferred_element_type=F32)
        rest = jnp.dot(low[rows, :], weight[lines, 0:128], preferred_element_type=F32)
        total = both[:, 0:128] + both[:, 128:256] + rest
        if first:
            acc[...] = total
        else:
            acc[...] += total

    def weight_grad(high, low, g):
        @pl.loop(0, 3)
        def _(step):
            rows = pl.ds(pl.multiple_of(step * 128, 128), 256)
            dims = (((0,), (0,)), ((), ()))
            both = lax.dot_general(high[rows, :], gcat[...], dims, preferred_element_type=F32)
            rest = lax.dot_general(
                low[rows, :], gcat[:, 0:128], dims, preferred_element_type=F32
            )
            total = both[:, 0:128] + both[:, 128:256] + rest
            for k in range(9):
                g[:, step * 9 + k] = total[k * 128:(k + 1) * 128].reshape(GROUPS, 8, 128)

    def prepare(start, stop, section):
        @pl.loop(start, stop)
        def _(tap):
            rows = pl.ds(pl.multiple_of(tap * 128, 128), 128)
            value = wboth[section, rows]
            places = [(value, (wc0, wc1)[section], rows)]
            if section == 1:
                flipped = pl.ds(pl.multiple_of((TAPS - 1 - tap) * 128, 128), 128)
                places.append((value.T, wct, flipped))
            for part, ref, place in places:
                top, rest = split(part)
                ref[place, 0:128] = top
                ref[place, 128:256] = rest

    own_w.wait()
    pl.when(seg == 0)(lambda: prepare(0, TAPS, 0))
    pl.when(seg == 1)(lambda: prepare(0, TAPS, 1))
    finish_halo(video_halo)
    build(vext, pvh, pvl)

    for index, step in enumerate((2, 1, 0)):
        for part in range(2):
            w_copies[step, part].wait_recv()
            w_relays[step, part].start()
        for part in range(2):
            w_relays[step, part].wait_recv()
        pl.when(seg == 1)(lambda: prepare(step * 9, step * 9 + 9, 0))
        pl.when(seg == 0)(lambda: prepare(step * 9, step * 9 + 9, 1))
        conv_step(pvh, pvl, wc0, step, index == 0)

    hidden = acc[...]
    sigmoid = 1.0 / (1.0 + jnp.exp(-hidden))
    slope[...] = sigmoid * (1.0 + hidden * (1.0 - sigmoid))
    lext[2:4, 1:5] = (hidden / (1.0 + jnp.exp(-hidden))).reshape(2, 4, 32, 128)
    latent_halo = halo(lext, 2, 0, 1)
    start_halo(latent_halo)
    finish_halo(latent_halo)
    build(lext, plh, pll)
    for step in range(3):
        conv_step(plh, pll, wc1, step, step == 0)
    cot = (acc[...] - vext[2:4, 1:5].reshape(256, 128)) * (65536.0 ** -0.5)
    cext[0:2, 1:5] = cot.reshape(2, 4, 32, 128)
    cot_halo = halo(cext, 0, 2, -1)
    start_halo(cot_halo)
    top, rest = split(cot)
    gcat[:, 0:128] = top
    gcat[:, 128:256] = rest
    weight_grad(plh, pll, g1)

    near = (("tm", x), ("y", y))
    wide = (("y", y), ("tm", x))
    order = (2, 1, 3, 0)

    def block(h, step):
        return pl.ds(ring(wide[h][1], step) * 7, 7)

    class Sum:
        def __init__(self, sec, g, ra):
            self.sec, self.g, self.ra = sec, g, ra
            self.mine = seg == sec
            self.pair, self.first, self.second = {}, {}, {}
            self.cross, self.fourth = {}, {}

        def start_pair(self):
            for j, step in enumerate(order):
                for h in range(2):
                    rows = pl.ds((1 - c) * 8 + h * 4, 4)
                    copy = remote(
                        self.g.at[rows, block(h, step)], self.ra.at[h, j], {"core": 1 - c}
                    )
                    copy.start()
                    self.pair[h, j] = copy

        def start_first(self):
            for j, step in enumerate(order):
                for h in range(2):
                    self.pair[h, j].wait()
                    taps = block(h, step)
                    base = c * 8 + h * 4
                    self.g[pl.ds(base, 4), taps] += self.ra[h, j]
                    axis, place = near[h]
                    for d in (2, 1, 3):
                        peer = ring(place, d)
                        copy = remote(
                            self.g.at[base + peer, taps], rb.at[self.sec, h, j, d - 1], {axis: peer}
                        )
                        copy.start()
                        self.first[h, j, d] = copy

        def start_second(self, j):
            step = order[j]
            for h in range(2):
                for d in (1, 2, 3):
                    self.first[h, j, d].wait()
                got = rb.at[self.sec, h, j]
                total = self.g[c * 8 + h * 4 + near[h][1], block(h, step)]
                total += got[0] + got[1] + got[2]
                if step == 0:
                    tt[self.sec, h] = total
                else:
                    sb[self.sec, h, j] = total
                    axis, place = wide[h]
                    copy = remote(
                        sb.at[self.sec, h, j], rc.at[self.sec, h, j], {axis: ring(place, step)}
                    )
                    copy.start()
                    self.second[h, j] = copy

        def start_third(self):
            sec = self.sec
            for h in range(2):
                for j in range(3):
                    self.second[h, j].wait()
                tt[sec, h] += rc[sec, h, 0] + rc[sec, h, 1] + rc[sec, h, 2]
                self.cross[h] = remote(tt.at[sec, h], rd.at[h], {"segment": other})
                pl.when(jnp.logical_not(self.mine))(self.cross[h].start)

        def start_fourth(self):
            for h in range(2):
                for d in (2, 1, 3):
                    self.fourth[h, d] = remote(
                        tt.at[self.sec, h], re.at[h, d - 1], {"zh": ring(zh, d)}
                    )

            @pl.when(jnp.logical_not(self.mine))
            def _():
                for h in range(2):
                    self.cross[h].wait_send()

            @pl.when(self.mine)
            def _():
                for h in range(2):
                    self.cross[h].wait_recv()
                    tt[self.sec, h] += rd[h]
                    for d in (2, 1, 3):
                        self.fourth[h, d].start()

        def finish(self):
            fifth, sixth, pair, write = {}, {}, {}, {}
            for h in range(2):
                axis, place = wide[h]
                axis1, place1 = near[h]
                group = c * 8 + h * 4 + place1
                for d in (2, 1, 3):
                    fifth[h, d] = remote(
                        uu.at[h], full.at[block(h, 0), group], {axis: ring(place, d)}
                    )
                for d in (0, 1, 3, 2):
                    for e in (2, 1, 3):
                        spot_ = full.at[block(h, -d), group]
                        source = uu.at[h] if d == 0 else spot_
                        sixth[h, d, e] = remote(source, spot_, {axis1: ring(place1, e)})
                for e in range(4):
                    column_ = full.at[:, c * 8 + h * 4 + ring(place1, -e)]
                    pair[h, e] = remote(column_, column_, {"core": 1 - c})
                    for far, core in enumerate((c, 1 - c)):
                        index = core * 8 + h * 4 + ring(place1, -e)
                        write[h, e, far] = pltpu.make_async_copy(
                            full.at[0:TAPS, index],
                            out_ref.at[:, index],
                            local_sem.at[2 + (h * 4 + e) * 2 + far],
                        )

            @pl.when(self.mine)
            def _():
                for h in range(2):
                    for d in (1, 2, 3):
                        self.fourth[h, d].wait()
                    uu[h] = tt[self.sec, h] + re[h, 0] + re[h, 1] + re[h, 2]
                    for d in (2, 1, 3):
                        fifth[h, d].start()
                    for e in (2, 1, 3):
                        sixth[h, 0, e].start()
                    full[block(h, 0), c * 8 + h * 4 + near[h][1]] = uu[h]
                for d in (1, 3, 2):
                    for h in range(2):
                        fifth[h, d].wait_recv()
                        for e in (2, 1, 3):
                            sixth[h, d, e].start()
                for e in (0, 1, 3, 2):
                    for h in range(2):
                        if e > 0:
                            for d in range(4):
                                sixth[h, d, e].wait_recv()
                        pair[h, e].start()
                        write[h, e, 0].start()
                for e in (0, 1, 3, 2):
                    for h in range(2):
                        pair[h, e].wait_recv()
                        write[h, e, 1].start()
                for h in range(2):
                    for d in (1, 2, 3):
                        fifth[h, d].wait_send()
                        for e in range(4):
                            sixth[h, e, d].wait_send()
                    for e in range(4):
                        pair[h, e].wait_send()
                        for far in range(2):
                            write[h, e, far].wait()

    decoder = Sum(1, g1, ra1)
    encoder = Sum(0, g0, ra0)
    decoder.start_pair()
    decoder.start_first()

    finish_halo(cot_halo)
    build(cext, pch, pcl)
    for step in range(3):
        conv_step(pch, pcl, wct, step, step == 0)
    top, rest = split(acc[...] * slope[...])
    gcat[:, 0:128] = top
    gcat[:, 128:256] = rest
    weight_grad(pvh, pvl, g0)
    encoder.start_pair()
    for j in range(4):
        decoder.start_second(j)
    encoder.start_first()
    decoder.start_third()
    encoder.start_second(0)
    encoder.start_second(1)
    decoder.start_fourth()
    encoder.start_second(2)
    encoder.start_second(3)
    encoder.start_third()
    encoder.start_fourth()
    decoder.finish()
    encoder.finish()

    for step in range(3):
        for part in range(2):
            w_copies[step, part].wait_send()
            w_relays[step, part].wait_send()


def local(video_clips, conv_weights):
    vm = pltpu.VMEM
    ext = vm((4, 6, 32, 128), F32)
    patches = vm((512, 1152), BF16)
    wcat = vm((3456, 256), BF16)
    grads = vm((GROUPS, PAD, 8, 128), F32)
    quarters = vm((2, 4, 4, 7, 8, 128), F32)
    summed = pl.pallas_call(
        kernel,
        out_shape=jax.ShapeDtypeStruct((TAPS, GROUPS, 8, 128), F32),
        in_specs=[pl.BlockSpec(memory_space=pl.ANY)] * 2,
        out_specs=pl.BlockSpec(memory_space=pl.ANY),
        scratch_shapes=[
            ext, ext, ext,
            patches, patches, patches, patches, patches, patches,
            vm((2, 3456, 128), F32), wcat, wcat, wcat,
            vm((256, 128), F32), vm((256, 128), F32), vm((256, 256), BF16),
            grads, grads, quarters, quarters,
            vm((2, 2, 4, 3, 7, 8, 128), F32),
            vm((2, 2, 3, 7, 8, 128), F32),
            vm((2, 2, 3, 7, 8, 128), F32),
            vm((2, 2, 7, 8, 128), F32),
            vm((2, 7, 8, 128), F32),
            vm((2, 3, 7, 8, 128), F32),
            vm((2, 7, 8, 128), F32),
            vm((PAD, GROUPS, 8, 128), F32),
            pltpu.SemaphoreType.DMA((20,)),
            pltpu.SemaphoreType.DMA((200,)),
            pltpu.SemaphoreType.DMA((200,)),
        ],
        compiler_params=pltpu.CompilerParams(
            collective_id=0, has_side_effects=True, vmem_limit_bytes=60 * 1024 * 1024
        ),
        name="step",
    )(video_clips, conv_weights)
    return summed.reshape(1, TAPS * 128, 128)


def solution(mesh):
    finer = Mesh(
        mesh.devices.reshape(mesh.shape["segment"], mesh.shape["tm"], 4, 4, 2), AXES
    )
    in_specs = (P(None, "tm", ("zh", "y", "core"), None, None), P("segment", None, None))
    return jax.shard_map(
        local, mesh=finer, in_specs=in_specs, out_specs=P("segment", None, None), check_vma=False
    )
```

```python
import jax
import jax.numpy as jnp
from jax import lax
from jax.experimental import pallas as pl
from jax.experimental.pallas import tpu as pltpu
from jax.sharding import Mesh
from jax.sharding import PartitionSpec as P

MESH = pl.DeviceIdType.MESH
AXES = ("segment", "tm", "zh", "y", "core")
F32 = jnp.float32
BF16 = jnp.bfloat16
TAPS = 27
PAD = 28
GROUPS = 16
QUARTER = 288


def kernel(
    vid_ref, w_ref, full,
    vext, lext, cext,
    pvh, pvl, plh, pll, pch, pcl,
    wboth, wc0, wc1, wct,
    acc, slope, gcat,
    g0, g1, ra0, ra1, rb, sb, rc, tt, rd, re, uu,
    local_sem, send_sem, recv_sem,
):
    seg = lax.axis_index("segment")
    x = lax.axis_index("tm")
    zh = lax.axis_index("zh")
    y = lax.axis_index("y")
    c = lax.axis_index("core")
    s = zh * 8 + y * 2 + c
    counter = [0]

    def spot(index, **others):
        index = lax.rem(index + 32, 32)
        return {"zh": index // 8, "y": lax.rem(index // 2, 4), "core": lax.rem(index, 2), **others}

    def ring(value, step):
        return lax.rem(value + step + 4, 4)

    other = 1 - seg
    link_b = ring(zh, 2 * seg - 1)

    def remote(src, dst, device):
        slot = counter[0]
        counter[0] += 1
        return pltpu.make_async_remote_copy(
            src_ref=src,
            dst_ref=dst,
            send_sem=send_sem.at[slot],
            recv_sem=recv_sem.at[slot],
            device_id=device,
            device_id_type=MESH,
        )

    own_w = pltpu.make_async_copy(w_ref.at[0], wboth.at[seg], local_sem.at[0])
    own_v = pltpu.make_async_copy(vid_ref.at[seg], vext.at[2:4, 1:5], local_sem.at[1])
    own_v.start()
    own_w.start()
    for ext, edge, far in ((vext, x == 0, 0), (lext, x == 0, 0), (cext, x == 3, 2)):
        @pl.when(edge)
        def _():
            ext[far:far + 2] = jnp.zeros((2, 6, 32, 128), F32)

        for rim, line in ((s == 0, 0), (s == 31, 5)):
            @pl.when(rim)
            def _():
                ext[:, line] = jnp.zeros((4, 32, 128), F32)

    for g in (g0, g1):
        g[:, TAPS] = jnp.zeros((GROUPS, 8, 128), F32)

    barrier = pltpu.get_barrier_semaphore()
    greet = [{"tm": ring(x, d)} for d in (1, 2, 3)]
    greet += [{"y": ring(y, d)} for d in (1, 2, 3)]
    greet += [{"zh": ring(zh, d)} for d in (1, 2, 3)]
    greet += [{"core": 1 - c}, {"segment": other}, {"segment": other, "zh": link_b}]
    greet += [spot(s + 1), spot(s - 1)]
    greet += [spot(s + dy, tm=ring(x, dx)) for dy in (1, -1) for dx in (1, -1)]
    for device in greet:
        pl.semaphore_signal(barrier, inc=1, device_id=device, device_id_type=MESH)
    pl.semaphore_wait(barrier, len(greet))

    def quarter(step, part, core):
        return pl.ds(step * 1152 + (part * 2 + core) * QUARTER, QUARTER)

    w_copies = {}
    w_relays = {}
    for step in range(3):
        for part in range(2):
            rows = quarter(step, part, c)
            device = {"segment": other} if part == 0 else {"segment": other, "zh": link_b}
            w_copies[step, part] = remote(w_ref.at[0, rows], wboth.at[seg, rows], device)
            w_relays[step, part] = remote(
                wboth.at[other, rows], wboth.at[other, rows], {"core": 1 - c}
            )

    def halo(ext, own, far, shift):
        ahead = {"tm": ring(x, shift)}
        sends_x = (x < 3) if shift == 1 else (x > 0)
        gets_x = (x > 0) if shift == 1 else (x < 3)
        moves = [
            (remote(ext.at[own:own + 2, 1:5], ext.at[far:far + 2, 1:5], ahead), sends_x, gets_x)
        ]
        for dy in (1, -1):
            src_row, dst_row = (4, 0) if dy == 1 else (1, 5)
            sends = (s < 31) if dy == 1 else (s > 0)
            gets = (s > 0) if dy == 1 else (s < 31)
            row = ext.at[own:own + 2, src_row]
            moves.append(
                (
                    remote(row, ext.at[far:far + 2, dst_row], spot(s + dy, **ahead)),
                    jnp.logical_and(sends, sends_x),
                    jnp.logical_and(gets, gets_x),
                )
            )
            moves.append((remote(row, ext.at[own:own + 2, dst_row], spot(s + dy)), sends, gets))
        return moves

    def start_halo(moves):
        for copy, sends, _ in moves:
            pl.when(sends)(copy.start)

    def finish_halo(moves):
        for copy, sends, gets in moves:
            pl.when(gets)(copy.wait_recv)
            pl.when(sends)(copy.wait_send)

    for step in (2, 1, 0):
        for part in range(2):
            w_copies[step, part].start()
    own_v.wait()
    video_halo = halo(vext, 2, 0, 1)
    start_halo(video_halo)

    column = lax.broadcasted_iota(jnp.int32, (32, 128), 0)

    def build(ext, high, low):
        @pl.loop(0, 4)
        def _(frame):
            base = pl.multiple_of(frame * 128, 128)
            for line in range(6):
                value = ext[frame, line]
                for e in range(3):
                    if e == 0:
                        moved = jnp.where(column == 0, 0.0, pltpu.roll(value, 1, 0))
                    elif e == 2:
                        moved = jnp.where(column == 31, 0.0, pltpu.roll(value, 31, 0))
                    else:
                        moved = value
                    top = moved.astype(BF16)
                    rest = (moved - top.astype(F32)).astype(BF16)
                    for b in range(3):
                        r = line - b
                        if 0 <= r < 4:
                            lanes = slice((b * 3 + e) * 128, (b * 3 + e + 1) * 128)
                            high[pl.ds(base + r * 32, 32), lanes] = top
                            low[pl.ds(base + r * 32, 32), lanes] = rest

    def split(value):
        top = value.astype(BF16)
        return top, (value - top.astype(F32)).astype(BF16)

    def conv_step(high, low, weight, step, first):
        rows = pl.ds(step * 128, 256)
        lines = pl.ds(step * 1152, 1152)
        both = jnp.dot(high[rows, :], weight[lines, :], preferred_element_type=F32)
        rest = jnp.dot(low[rows, :], weight[lines, 0:128], preferred_element_type=F32)
        total = both[:, 0:128] + both[:, 128:256] + rest
        if first:
            acc[...] = total
        else:
            acc[...] += total

    def weight_grad(high, low, g):
        @pl.loop(0, 3)
        def _(step):
            rows = pl.ds(pl.multiple_of(step * 128, 128), 256)
            dims = (((0,), (0,)), ((), ()))
            both = lax.dot_general(high[rows, :], gcat[...], dims, preferred_element_type=F32)
            rest = lax.dot_general(
                low[rows, :], gcat[:, 0:128], dims, preferred_element_type=F32
            )
            total = both[:, 0:128] + both[:, 128:256] + rest
            for k in range(9):
                g[:, step * 9 + k] = total[k * 128:(k + 1) * 128].reshape(GROUPS, 8, 128)

    def prepare(start, stop, section):
        @pl.loop(start, stop)
        def _(tap):
            rows = pl.ds(pl.multiple_of(tap * 128, 128), 128)
            value = wboth[section, rows]
            places = [(value, (wc0, wc1)[section], rows)]
            if section == 1:
                flipped = pl.ds(pl.multiple_of((TAPS - 1 - tap) * 128, 128), 128)
                places.append((value.T, wct, flipped))
            for part, ref, place in places:
                top, rest = split(part)
                ref[place, 0:128] = top
                ref[place, 128:256] = rest

    own_w.wait()
    pl.when(seg == 0)(lambda: prepare(0, TAPS, 0))
    pl.when(seg == 1)(lambda: prepare(0, TAPS, 1))
    finish_halo(video_halo)
    build(vext, pvh, pvl)

    for index, step in enumerate((2, 1, 0)):
        for part in range(2):
            w_copies[step, part].wait_recv()
            w_relays[step, part].start()
        for part in range(2):
            w_relays[step, part].wait_recv()
        pl.when(seg == 1)(lambda: prepare(step * 9, step * 9 + 9, 0))
        pl.when(seg == 0)(lambda: prepare(step * 9, step * 9 + 9, 1))
        conv_step(pvh, pvl, wc0, step, index == 0)

    hidden = acc[...]
    sigmoid = 1.0 / (1.0 + jnp.exp(-hidden))
    slope[...] = sigmoid * (1.0 + hidden * (1.0 - sigmoid))
    lext[2:4, 1:5] = (hidden / (1.0 + jnp.exp(-hidden))).reshape(2, 4, 32, 128)
    latent_halo = halo(lext, 2, 0, 1)
    start_halo(latent_halo)
    finish_halo(latent_halo)
    build(lext, plh, pll)
    for step in range(3):
        conv_step(plh, pll, wc1, step, step == 0)
    cot = (acc[...] - vext[2:4, 1:5].reshape(256, 128)) * (65536.0 ** -0.5)
    cext[0:2, 1:5] = cot.reshape(2, 4, 32, 128)
    cot_halo = halo(cext, 0, 2, -1)
    start_halo(cot_halo)
    top, rest = split(cot)
    gcat[:, 0:128] = top
    gcat[:, 128:256] = rest
    weight_grad(plh, pll, g1)

    near = (("tm", x), ("y", y))
    wide = (("y", y), ("tm", x))
    order = (2, 1, 3, 0)

    def block(h, step):
        return pl.ds(ring(wide[h][1], step) * 7, 7)

    class Sum:
        def __init__(self, sec, g, ra):
            self.sec, self.g, self.ra = sec, g, ra
            self.mine = seg == sec
            self.pair, self.first, self.second = {}, {}, {}
            self.cross, self.fourth = {}, {}

        def start_pair(self):
            for j, step in enumerate(order):
                for h in range(2):
                    rows = pl.ds((1 - c) * 8 + h * 4, 4)
                    copy = remote(
                        self.g.at[rows, block(h, step)], self.ra.at[h, j], {"core": 1 - c}
                    )
                    copy.start()
                    self.pair[h, j] = copy

        def start_first(self):
            for j, step in enumerate(order):
                for h in range(2):
                    self.pair[h, j].wait()
                    taps = block(h, step)
                    base = c * 8 + h * 4
                    self.g[pl.ds(base, 4), taps] += self.ra[h, j]
                    axis, place = near[h]
                    for d in (2, 1, 3):
                        peer = ring(place, d)
                        copy = remote(
                            self.g.at[base + peer, taps], rb.at[self.sec, h, j, d - 1], {axis: peer}
                        )
                        copy.start()
                        self.first[h, j, d] = copy

        def start_second(self, j):
            step = order[j]
            for h in range(2):
                for d in (1, 2, 3):
                    self.first[h, j, d].wait()
                got = rb.at[self.sec, h, j]
                total = self.g[c * 8 + h * 4 + near[h][1], block(h, step)]
                total += got[0] + got[1] + got[2]
                if step == 0:
                    tt[self.sec, h] = total
                else:
                    sb[self.sec, h, j] = total
                    axis, place = wide[h]
                    copy = remote(
                        sb.at[self.sec, h, j], rc.at[self.sec, h, j], {axis: ring(place, step)}
                    )
                    copy.start()
                    self.second[h, j] = copy

        def start_third(self):
            sec = self.sec
            for h in range(2):
                for j in range(3):
                    self.second[h, j].wait()
                tt[sec, h] += rc[sec, h, 0] + rc[sec, h, 1] + rc[sec, h, 2]
                self.cross[h] = remote(tt.at[sec, h], rd.at[h], {"segment": other})
                pl.when(jnp.logical_not(self.mine))(self.cross[h].start)

        def start_fourth(self):
            for h in range(2):
                for d in (2, 1, 3):
                    self.fourth[h, d] = remote(
                        tt.at[self.sec, h], re.at[h, d - 1], {"zh": ring(zh, d)}
                    )

            @pl.when(jnp.logical_not(self.mine))
            def _():
                for h in range(2):
                    self.cross[h].wait_send()

            @pl.when(self.mine)
            def _():
                for h in range(2):
                    self.cross[h].wait_recv()
                    tt[self.sec, h] += rd[h]
                    for d in (2, 1, 3):
                        self.fourth[h, d].start()

        def finish(self):
            fifth, sixth, pair = {}, {}, {}
            for h in range(2):
                axis, place = wide[h]
                axis1, place1 = near[h]
                group = c * 8 + h * 4 + place1
                for d in (2, 1, 3):
                    fifth[h, d] = remote(
                        uu.at[h], full.at[block(h, 0), group], {axis: ring(place, d)}
                    )
                for d in (0, 1, 3, 2):
                    for e in (2, 1, 3):
                        spot_ = full.at[block(h, -d), group]
                        source = uu.at[h] if d == 0 else spot_
                        sixth[h, d, e] = remote(source, spot_, {axis1: ring(place1, e)})
                for e in range(4):
                    column_ = full.at[:, c * 8 + h * 4 + ring(place1, -e)]
                    pair[h, e] = remote(column_, column_, {"core": 1 - c})

            @pl.when(self.mine)
            def _():
                for h in range(2):
                    for d in (1, 2, 3):
                        self.fourth[h, d].wait()
                    uu[h] = tt[self.sec, h] + re[h, 0] + re[h, 1] + re[h, 2]
                    for d in (2, 1, 3):
                        fifth[h, d].start()
                    for e in (2, 1, 3):
                        sixth[h, 0, e].start()
                    full[block(h, 0), c * 8 + h * 4 + near[h][1]] = uu[h]
                for d in (1, 3, 2):
                    for h in range(2):
                        fifth[h, d].wait_recv()
                        for e in (2, 1, 3):
                            sixth[h, d, e].start()
                for e in (0, 1, 3, 2):
                    for h in range(2):
                        if e > 0:
                            for d in range(4):
                                sixth[h, d, e].wait_recv()
                        pair[h, e].start()
                for h in range(2):
                    for d in (1, 2, 3):
                        fifth[h, d].wait_send()
                        for e in range(4):
                            sixth[h, e, d].wait_send()
                    for e in range(4):
                        pair[h, e].wait()

    decoder = Sum(1, g1, ra1)
    encoder = Sum(0, g0, ra0)
    decoder.start_pair()
    decoder.start_first()

    finish_halo(cot_halo)
    build(cext, pch, pcl)
    for step in range(3):
        conv_step(pch, pcl, wct, step, step == 0)
    top, rest = split(acc[...] * slope[...])
    gcat[:, 0:128] = top
    gcat[:, 128:256] = rest
    weight_grad(pvh, pvl, g0)
    encoder.start_pair()
    encoder.start_first()
    for j in range(4):
        decoder.start_second(j)
    encoder.start_second(0)
    encoder.start_second(1)
    decoder.start_third()
    encoder.start_second(2)
    encoder.start_second(3)
    encoder.start_third()
    decoder.start_fourth()
    encoder.start_fourth()
    decoder.finish()
    encoder.finish()

    for step in range(3):
        for part in range(2):
            w_copies[step, part].wait_send()
            w_relays[step, part].wait_send()


def local(video_clips, conv_weights):
    vm = pltpu.VMEM
    ext = vm((4, 6, 32, 128), F32)
    patches = vm((512, 1152), BF16)
    wcat = vm((3456, 256), BF16)
    grads = vm((GROUPS, PAD, 8, 128), F32)
    quarters = vm((2, 4, 4, 7, 8, 128), F32)
    summed = pl.pallas_call(
        kernel,
        out_shape=pltpu.VMEM((PAD, GROUPS, 8, 128), F32),
        in_specs=[pl.BlockSpec(memory_space=pl.ANY)] * 2,
        out_specs=pl.BlockSpec(memory_space=pltpu.VMEM),
        scratch_shapes=[
            ext, ext, ext,
            patches, patches, patches, patches, patches, patches,
            vm((2, 3456, 128), F32), wcat, wcat, wcat,
            vm((256, 128), F32), vm((256, 128), F32), vm((256, 256), BF16),
            grads, grads, quarters, quarters,
            vm((2, 2, 4, 3, 7, 8, 128), F32),
            vm((2, 2, 3, 7, 8, 128), F32),
            vm((2, 2, 3, 7, 8, 128), F32),
            vm((2, 2, 7, 8, 128), F32),
            vm((2, 7, 8, 128), F32),
            vm((2, 3, 7, 8, 128), F32),
            vm((2, 7, 8, 128), F32),
            pltpu.SemaphoreType.DMA((2,)),
            pltpu.SemaphoreType.DMA((200,)),
            pltpu.SemaphoreType.DMA((200,)),
        ],
        compiler_params=pltpu.CompilerParams(
            collective_id=0, has_side_effects=True, vmem_limit_bytes=60 * 1024 * 1024
        ),
        name="step",
    )(video_clips, conv_weights)
    return summed[:TAPS].reshape(1, TAPS * 128, 128)


def solution(mesh):
    finer = Mesh(
        mesh.devices.reshape(mesh.shape["segment"], mesh.shape["tm"], 4, 4, 2), AXES
    )
    in_specs = (P(None, "tm", ("zh", "y", "core"), None, None), P("segment", None, None))
    return jax.shard_map(
        local, mesh=finer, in_specs=in_specs, out_specs=P("segment", None, None), check_vma=False
    )
```

```python
import jax
import jax.numpy as jnp
from jax import lax
from jax.experimental import pallas as pl
from jax.experimental.pallas import tpu as pltpu
from jax.sharding import Mesh
from jax.sharding import PartitionSpec as P

MESH = pl.DeviceIdType.MESH
AXES = ("segment", "tm", "zh", "y", "core")
F32 = jnp.float32
BF16 = jnp.bfloat16
TAPS = 27
PAD = 28
GROUPS = 16
QUARTER = 288
SENDS = 30
RECEIPTS = 73


def kernel(
    vid_ref, w_ref, full,
    vext, lext, cext,
    pvh, pvl, plh, pll, pch, pcl,
    wboth, wc0, wc1, wct,
    acc, slope, gcat,
    g0, g1, ra0, ra1, rb, sb, rc, tt, rd, re, uu,
    local_sem, send_sem, recv_sem,
):
    seg = lax.axis_index("segment")
    x = lax.axis_index("tm")
    zh = lax.axis_index("zh")
    y = lax.axis_index("y")
    c = lax.axis_index("core")
    s = zh * 8 + y * 2 + c
    sends, receipts = [0], [0]

    def new(counter, count=1):
        counter[0] += count
        return counter[0] - count

    def spot(index, **others):
        index = lax.rem(index + 32, 32)
        return {"zh": index // 8, "y": lax.rem(index // 2, 4), "core": lax.rem(index, 2), **others}

    def ring(value, step):
        return lax.rem(value + step + 4, 4)

    other = 1 - seg
    link_b = ring(zh, 2 * seg - 1)

    def remote(src, dst, device, sent=None, received=None):
        sent = new(sends) if sent is None else sent
        received = new(receipts) if received is None else received
        return pltpu.make_async_remote_copy(
            src_ref=src,
            dst_ref=dst,
            send_sem=send_sem.at[sent],
            recv_sem=recv_sem.at[received],
            device_id=device,
            device_id_type=MESH,
        )

    def await_sent(slot, like):
        pltpu.make_async_copy(like, like, send_sem.at[slot]).wait()

    def await_received(slot, like):
        pltpu.make_async_copy(like, like, recv_sem.at[slot]).wait()

    own_w = pltpu.make_async_copy(w_ref.at[0], wboth.at[seg], local_sem.at[0])
    own_v = pltpu.make_async_copy(vid_ref.at[seg], vext.at[2:4, 1:5], local_sem.at[1])
    own_v.start()
    own_w.start()
    for ext, edge, far in ((vext, x == 0, 0), (lext, x == 0, 0), (cext, x == 3, 2)):
        @pl.when(edge)
        def _():
            ext[far:far + 2] = jnp.zeros((2, 6, 32, 128), F32)

        for rim, line in ((s == 0, 0), (s == 31, 5)):
            @pl.when(rim)
            def _():
                ext[:, line] = jnp.zeros((4, 32, 128), F32)

    for g in (g0, g1):
        g[:, TAPS] = jnp.zeros((GROUPS, 8, 128), F32)

    barrier = pltpu.get_barrier_semaphore()
    greet = [{"tm": ring(x, d)} for d in (1, 2, 3)]
    greet += [{"y": ring(y, d)} for d in (1, 2, 3)]
    greet += [{"zh": ring(zh, d)} for d in (1, 2, 3)]
    greet += [{"core": 1 - c}, {"segment": other}, {"segment": other, "zh": link_b}]
    greet += [spot(s + 1), spot(s - 1)]
    greet += [spot(s + dy, tm=ring(x, dx)) for dy in (1, -1) for dx in (1, -1)]
    for device in greet:
        pl.semaphore_signal(barrier, inc=1, device_id=device, device_id_type=MESH)
    pl.semaphore_wait(barrier, len(greet))

    def quarter(step, part, core):
        return pl.ds(step * 1152 + (part * 2 + core) * QUARTER, QUARTER)

    w_copies = {}
    w_relays = {}
    w_sent, w_passed = new(sends), new(sends)
    w_got, w_shared = new(receipts, 3), new(receipts, 3)
    for step in range(3):
        for part in range(2):
            rows = quarter(step, part, c)
            device = {"segment": other} if part == 0 else {"segment": other, "zh": link_b}
            w_copies[step, part] = remote(
                w_ref.at[0, rows], wboth.at[seg, rows], device, w_sent, w_got + step
            )
            w_relays[step, part] = remote(
                wboth.at[other, rows], wboth.at[other, rows], {"core": 1 - c},
                w_passed, w_shared + step,
            )

    def halo(ext, own, far, shift):
        ahead = {"tm": ring(x, shift)}
        sends_x = (x < 3) if shift == 1 else (x > 0)
        gets_x = (x > 0) if shift == 1 else (x < 3)
        moves = [
            (remote(ext.at[own:own + 2, 1:5], ext.at[far:far + 2, 1:5], ahead), sends_x, gets_x)
        ]
        for dy in (1, -1):
            src_row, dst_row = (4, 0) if dy == 1 else (1, 5)
            gives = (s < 31) if dy == 1 else (s > 0)
            gets = (s > 0) if dy == 1 else (s < 31)
            row = ext.at[own:own + 2, src_row]
            moves.append(
                (
                    remote(row, ext.at[far:far + 2, dst_row], spot(s + dy, **ahead)),
                    jnp.logical_and(gives, sends_x),
                    jnp.logical_and(gets, gets_x),
                )
            )
            moves.append((remote(row, ext.at[own:own + 2, dst_row], spot(s + dy)), gives, gets))
        return moves

    def start_halo(moves):
        for copy, sends, _ in moves:
            pl.when(sends)(copy.start)

    def finish_halo(moves):
        for copy, sends, gets in moves:
            pl.when(gets)(copy.wait_recv)
            pl.when(sends)(copy.wait_send)

    for step in (2, 1, 0):
        for part in range(2):
            w_copies[step, part].start()
    own_v.wait()
    video_halo = halo(vext, 2, 0, 1)
    start_halo(video_halo)

    column = lax.broadcasted_iota(jnp.int32, (32, 128), 0)

    def build(ext, high, low):
        @pl.loop(0, 4)
        def _(frame):
            base = pl.multiple_of(frame * 128, 128)
            for line in range(6):
                value = ext[frame, line]
                for e in range(3):
                    if e == 0:
                        moved = jnp.where(column == 0, 0.0, pltpu.roll(value, 1, 0))
                    elif e == 2:
                        moved = jnp.where(column == 31, 0.0, pltpu.roll(value, 31, 0))
                    else:
                        moved = value
                    top = moved.astype(BF16)
                    rest = (moved - top.astype(F32)).astype(BF16)
                    for b in range(3):
                        r = line - b
                        if 0 <= r < 4:
                            lanes = slice((b * 3 + e) * 128, (b * 3 + e + 1) * 128)
                            high[pl.ds(base + r * 32, 32), lanes] = top
                            low[pl.ds(base + r * 32, 32), lanes] = rest

    def split(value):
        top = value.astype(BF16)
        return top, (value - top.astype(F32)).astype(BF16)

    def conv_step(high, low, weight, step, first):
        rows = pl.ds(step * 128, 256)
        lines = pl.ds(step * 1152, 1152)
        both = jnp.dot(high[rows, :], weight[lines, :], preferred_element_type=F32)
        rest = jnp.dot(low[rows, :], weight[lines, 0:128], preferred_element_type=F32)
        total = both[:, 0:128] + both[:, 128:256] + rest
        if first:
            acc[...] = total
        else:
            acc[...] += total

    def weight_grad(high, low, g):
        @pl.loop(0, 3)
        def _(step):
            rows = pl.ds(pl.multiple_of(step * 128, 128), 256)
            dims = (((0,), (0,)), ((), ()))
            both = lax.dot_general(high[rows, :], gcat[...], dims, preferred_element_type=F32)
            rest = lax.dot_general(
                low[rows, :], gcat[:, 0:128], dims, preferred_element_type=F32
            )
            total = both[:, 0:128] + both[:, 128:256] + rest
            for k in range(9):
                g[:, step * 9 + k] = total[k * 128:(k + 1) * 128].reshape(GROUPS, 8, 128)

    def prepare(start, stop, section):
        @pl.loop(start, stop)
        def _(tap):
            rows = pl.ds(pl.multiple_of(tap * 128, 128), 128)
            value = wboth[section, rows]
            places = [(value, (wc0, wc1)[section], rows)]
            if section == 1:
                flipped = pl.ds(pl.multiple_of((TAPS - 1 - tap) * 128, 128), 128)
                places.append((value.T, wct, flipped))
            for part, ref, place in places:
                top, rest = split(part)
                ref[place, 0:128] = top
                ref[place, 128:256] = rest

    own_w.wait()
    pl.when(seg == 0)(lambda: prepare(0, TAPS, 0))
    pl.when(seg == 1)(lambda: prepare(0, TAPS, 1))
    finish_halo(video_halo)
    build(vext, pvh, pvl)

    for index, step in enumerate((2, 1, 0)):
        await_received(w_got + step, wboth.at[other, 0:2 * QUARTER])
        for part in range(2):
            w_relays[step, part].start()
        await_received(w_shared + step, wboth.at[other, 0:2 * QUARTER])
        pl.when(seg == 1)(lambda: prepare(step * 9, step * 9 + 9, 0))
        pl.when(seg == 0)(lambda: prepare(step * 9, step * 9 + 9, 1))
        conv_step(pvh, pvl, wc0, step, index == 0)

    hidden = acc[...]
    sigmoid = 1.0 / (1.0 + jnp.exp(-hidden))
    slope[...] = sigmoid * (1.0 + hidden * (1.0 - sigmoid))
    lext[2:4, 1:5] = (hidden / (1.0 + jnp.exp(-hidden))).reshape(2, 4, 32, 128)
    latent_halo = halo(lext, 2, 0, 1)
    start_halo(latent_halo)
    finish_halo(latent_halo)
    build(lext, plh, pll)
    for step in range(3):
        conv_step(plh, pll, wc1, step, step == 0)
    cot = (acc[...] - vext[2:4, 1:5].reshape(256, 128)) * (65536.0 ** -0.5)
    cext[0:2, 1:5] = cot.reshape(2, 4, 32, 128)
    cot_halo = halo(cext, 0, 2, -1)
    start_halo(cot_halo)
    top, rest = split(cot)
    gcat[:, 0:128] = top
    gcat[:, 128:256] = rest
    weight_grad(plh, pll, g1)

    near = (("tm", x), ("y", y))
    wide = (("y", y), ("tm", x))
    order = (2, 1, 3, 0)
    parts = (slice(0, 4), slice(4, 7))

    def block(h, step, u):
        cut = parts[u]
        return pl.ds(ring(wide[h][1], step) * 7 + cut.start, cut.stop - cut.start)

    class Sum:
        def __init__(self, sec, g, ra):
            self.sec, self.g, self.ra = sec, g, ra
            self.sent = new(sends, 4)
            self.paired = new(receipts, 8)
            self.summed = new(receipts, 8)
            self.widened = new(receipts, 2)

        def start_pair(self):
            for u in range(2):
                for j, step in enumerate(order):
                    for h in range(2):
                        rows = pl.ds((1 - c) * 8 + h * 4, 4)
                        remote(
                            self.g.at[rows, block(h, step, u)],
                            self.ra.at[h, j, :, parts[u]],
                            {"core": 1 - c}, self.sent, self.paired + u * 4 + j,
                        ).start()

        def start_first(self, u):
            cut = parts[u]
            for j, step in enumerate(order):
                await_received(self.paired + u * 4 + j, self.ra.at[:, j, :, cut])
                for h in range(2):
                    taps = block(h, step, u)
                    base = c * 8 + h * 4
                    self.g[pl.ds(base, 4), taps] += self.ra[h, j, :, cut]
                    axis, place = near[h]
                    for d in (2, 1, 3):
                        peer = ring(place, d)
                        remote(
                            self.g.at[base + peer, taps],
                            rb.at[self.sec, h, j, d - 1, cut],
                            {axis: peer}, self.sent + 1, self.summed + u * 4 + j,
                        ).start()

        def start_second(self, u):
            cut = parts[u]
            sec = self.sec
            for j, step in enumerate(order):
                await_received(self.summed + u * 4 + j, rb.at[sec, :, j, :, cut])
                for h in range(2):
                    total = self.g[c * 8 + h * 4 + near[h][1], block(h, step, u)]
                    total += rb[sec, h, j, 0, cut] + rb[sec, h, j, 1, cut] + rb[sec, h, j, 2, cut]
                    if step == 0:
                        tt[sec, h, cut] = total
                    else:
                        sb[sec, h, j, cut] = total
                        axis, place = wide[h]
                        remote(
                            sb.at[sec, h, j, cut], rc.at[sec, h, j, cut],
                            {axis: ring(place, step)}, self.sent + 2, self.widened + u,
                        ).start()

        def start_third(self, u):
            cut = parts[u]
            sec = self.sec
            await_received(self.widened + u, rc.at[sec, :, :, cut])
            for h in range(2):
                tt[sec, h, cut] += rc[sec, h, 0, cut] + rc[sec, h, 1, cut] + rc[sec, h, 2, cut]

            @pl.when(seg != sec)
            def _():
                remote(
                    tt.at[sec, :, cut], rd.at[:, cut], {"segment": other},
                    crossing, crossed + u,
                ).start()

        def start_fourth(self, u):
            cut = parts[u]

            @pl.when(seg == self.sec)
            def _():
                await_received(crossed + u, rd.at[:, cut])
                tt[self.sec, :, cut] += rd[:, cut]
                for d in (2, 1, 3):
                    remote(
                        tt.at[self.sec, :, cut], re.at[d - 1, :, cut], {"zh": ring(zh, d)},
                        stacking, stacked + u,
                    ).start()

        def finish(self):
            await_sent(self.sent, self.ra)
            await_sent(self.sent + 1, rb.at[self.sec])
            await_sent(self.sent + 2, sb.at[self.sec])

    crossing, stacking, crossed, stacked = new(sends), new(sends), new(receipts, 2), new(receipts, 2)
    decoder = Sum(1, g1, ra1)
    encoder = Sum(0, g0, ra0)
    decoder.start_pair()
    decoder.start_first(0)
    decoder.start_first(1)

    finish_halo(cot_halo)
    build(cext, pch, pcl)
    for step in range(3):
        conv_step(pch, pcl, wct, step, step == 0)
    top, rest = split(acc[...] * slope[...])
    gcat[:, 0:128] = top
    gcat[:, 128:256] = rest
    weight_grad(pvh, pvl, g0)
    encoder.start_pair()
    encoder.start_first(0)
    encoder.start_first(1)
    decoder.start_second(0)
    decoder.start_second(1)
    encoder.start_second(0)
    decoder.start_third(0)
    decoder.start_third(1)
    encoder.start_second(1)
    encoder.start_third(0)
    decoder.start_fourth(0)
    encoder.start_fourth(0)
    encoder.start_third(1)
    decoder.start_fourth(1)
    encoder.start_fourth(1)

    spreading, passing, sharing = new(sends), new(sends), new(sends)
    spread, passed, shared = new(receipts, 6), new(receipts, 3), new(receipts)

    def group(h, e):
        return c * 8 + h * 4 + ring(near[h][1], e)

    def pass_on(h, u, d):
        for e in (2, 1, 3):
            piece = full.at[block(h, -d, u), group(h, 0)]
            axis, place = near[h]
            remote(
                uu.at[h, parts[u]] if d == 0 else piece, piece,
                {axis: ring(place, e)}, passing, passed + e - 1,
            ).start()

    for u, cut in enumerate(parts):
        await_received(stacked + u, re.at[:, :, cut])
        for h in range(2):
            total = tt[seg, h, cut] + re[0, h, cut] + re[1, h, cut] + re[2, h, cut]
            uu[h, cut] = total
            full[block(h, 0, u), group(h, 0)] = total
            axis, place = wide[h]
            for d in (2, 1, 3):
                remote(
                    uu.at[h, cut], full.at[block(h, 0, u), group(h, 0)],
                    {axis: ring(place, d)}, spreading, spread + u * 3 + d - 1,
                ).start()
            pass_on(h, u, 0)
    for u, cut in enumerate(parts):
        for d in (1, 3, 2):
            await_received(spread + u * 3 + d - 1, uu.at[:, cut])
            for h in range(2):
                pass_on(h, u, d)
    for e in (0, 1, 3, 2):
        if e > 0:
            await_received(passed + e - 1, full.at[:, 0:2])
        for h in range(2):
            whole = full.at[:, group(h, -e)]
            remote(whole, whole, {"core": 1 - c}, sharing, shared).start()
    await_received(shared, ra0)

    decoder.finish()
    encoder.finish()
    await_sent(crossing, rd)
    await_sent(stacking, re)
    await_sent(spreading, re)
    await_sent(passing, rb.at[0])
    await_sent(sharing, ra0)
    await_sent(w_sent, wboth.at[0, 0:6 * QUARTER])
    await_sent(w_passed, wboth.at[0, 0:6 * QUARTER])
    assert sends[0] <= SENDS and receipts[0] <= RECEIPTS, (sends, receipts)


def local(video_clips, conv_weights):
    vm = pltpu.VMEM
    ext = vm((4, 6, 32, 128), F32)
    patches = vm((512, 1152), BF16)
    wcat = vm((3456, 256), BF16)
    grads = vm((GROUPS, PAD, 8, 128), F32)
    quarters = vm((2, 4, 4, 7, 8, 128), F32)
    summed = pl.pallas_call(
        kernel,
        out_shape=pltpu.VMEM((PAD, GROUPS, 8, 128), F32),
        in_specs=[pl.BlockSpec(memory_space=pl.ANY)] * 2,
        out_specs=pl.BlockSpec(memory_space=pltpu.VMEM),
        scratch_shapes=[
            ext, ext, ext,
            patches, patches, patches, patches, patches, patches,
            vm((2, 3456, 128), F32), wcat, wcat, wcat,
            vm((256, 128), F32), vm((256, 128), F32), vm((256, 256), BF16),
            grads, grads, quarters, quarters,
            vm((2, 2, 4, 3, 7, 8, 128), F32),
            vm((2, 2, 3, 7, 8, 128), F32),
            vm((2, 2, 3, 7, 8, 128), F32),
            vm((2, 2, 7, 8, 128), F32),
            vm((2, 7, 8, 128), F32),
            vm((3, 2, 7, 8, 128), F32),
            vm((2, 7, 8, 128), F32),
            pltpu.SemaphoreType.DMA((2,)),
            pltpu.SemaphoreType.DMA((SENDS,)),
            pltpu.SemaphoreType.DMA((RECEIPTS,)),
        ],
        compiler_params=pltpu.CompilerParams(
            collective_id=0, has_side_effects=True, vmem_limit_bytes=60 * 1024 * 1024
        ),
        name="step",
    )(video_clips, conv_weights)
    return summed[:TAPS].reshape(1, TAPS * 128, 128)


def solution(mesh):
    finer = Mesh(
        mesh.devices.reshape(mesh.shape["segment"], mesh.shape["tm"], 4, 4, 2), AXES
    )
    in_specs = (P(None, "tm", ("zh", "y", "core"), None, None), P("segment", None, None))
    return jax.shard_map(
        local, mesh=finer, in_specs=in_specs, out_specs=P("segment", None, None), check_vma=False
    )
```

```python
import jax
import jax.numpy as jnp
from jax import lax
from jax.experimental import pallas as pl
from jax.experimental.pallas import tpu as pltpu
from jax.sharding import Mesh
from jax.sharding import PartitionSpec as P

MESH = pl.DeviceIdType.MESH
AXES = ("segment", "tm", "zh", "y", "core")
F32 = jnp.float32
BF16 = jnp.bfloat16
TAPS = 27
PAD = 28
GROUPS = 16
QUARTER = 288
SENDS = 31
RECEIPTS = 96


def kernel(
    vid_ref, w_ref, full,
    vext, lext, cext,
    pvh, pvl, plh, pll, pch, pcl,
    wboth, wc0, wc1, wct,
    acc, slope, gcat,
    g0, g1, ra0, ra1, rb, rl, sb, rc, tt, rd, re, uu,
    local_sem, send_sem, recv_sem,
):
    seg = lax.axis_index("segment")
    x = lax.axis_index("tm")
    zh = lax.axis_index("zh")
    y = lax.axis_index("y")
    c = lax.axis_index("core")
    s = zh * 8 + y * 2 + c
    sends, receipts = [0], [0]

    def new(counter, count=1):
        counter[0] += count
        return counter[0] - count

    def spot(index, **others):
        index = lax.rem(index + 32, 32)
        return {"zh": index // 8, "y": lax.rem(index // 2, 4), "core": lax.rem(index, 2), **others}

    def ring(value, step):
        return lax.rem(value + step + 4, 4)

    other = 1 - seg
    link_b = ring(zh, 2 * seg - 1)

    def remote(src, dst, device, sent=None, received=None):
        sent = new(sends) if sent is None else sent
        received = new(receipts) if received is None else received
        return pltpu.make_async_remote_copy(
            src_ref=src,
            dst_ref=dst,
            send_sem=send_sem.at[sent],
            recv_sem=recv_sem.at[received],
            device_id=device,
            device_id_type=MESH,
        )

    def await_sent(slot, like):
        pltpu.make_async_copy(like, like, send_sem.at[slot]).wait()

    def await_received(slot, like):
        pltpu.make_async_copy(like, like, recv_sem.at[slot]).wait()

    own_w = pltpu.make_async_copy(w_ref.at[0], wboth.at[seg], local_sem.at[0])
    own_v = pltpu.make_async_copy(vid_ref.at[seg], vext.at[2:4, 1:5], local_sem.at[1])
    own_v.start()
    own_w.start()
    for ext, edge, far in ((vext, x == 0, 0), (lext, x == 0, 0), (cext, x == 3, 2)):
        @pl.when(edge)
        def _():
            ext[far:far + 2] = jnp.zeros((2, 6, 32, 128), F32)

        for rim, line in ((s == 0, 0), (s == 31, 5)):
            @pl.when(rim)
            def _():
                ext[:, line] = jnp.zeros((4, 32, 128), F32)

    for g in (g0, g1):
        g[:, TAPS] = jnp.zeros((GROUPS, 8, 128), F32)

    barrier = pltpu.get_barrier_semaphore()
    greet = [{"tm": ring(x, d)} for d in (1, 2, 3)]
    greet += [{"y": ring(y, d)} for d in (1, 2, 3)]
    greet += [{"zh": ring(zh, d)} for d in (1, 2, 3)]
    greet += [{"core": 1 - c}, {"segment": other}, {"segment": other, "zh": link_b}]
    greet += [spot(s + 1), spot(s - 1)]
    greet += [spot(s + dy, tm=ring(x, dx)) for dy in (1, -1) for dx in (1, -1)]
    for device in greet:
        pl.semaphore_signal(barrier, inc=1, device_id=device, device_id_type=MESH)
    pl.semaphore_wait(barrier, len(greet))

    def quarter(step, part, core):
        return pl.ds(step * 1152 + (part * 2 + core) * QUARTER, QUARTER)

    w_copies = {}
    w_relays = {}
    w_sent, w_passed = new(sends), new(sends)
    w_got, w_shared = new(receipts, 3), new(receipts, 3)
    for step in range(3):
        for part in range(2):
            rows = quarter(step, part, c)
            device = {"segment": other} if part == 0 else {"segment": other, "zh": link_b}
            w_copies[step, part] = remote(
                w_ref.at[0, rows], wboth.at[seg, rows], device, w_sent, w_got + step
            )
            w_relays[step, part] = remote(
                wboth.at[other, rows], wboth.at[other, rows], {"core": 1 - c},
                w_passed, w_shared + step,
            )

    def halo(ext, own, far, shift):
        ahead = {"tm": ring(x, shift)}
        sends_x = (x < 3) if shift == 1 else (x > 0)
        gets_x = (x > 0) if shift == 1 else (x < 3)
        moves = [
            (remote(ext.at[own:own + 2, 1:5], ext.at[far:far + 2, 1:5], ahead), sends_x, gets_x)
        ]
        for dy in (1, -1):
            src_row, dst_row = (4, 0) if dy == 1 else (1, 5)
            gives = (s < 31) if dy == 1 else (s > 0)
            gets = (s > 0) if dy == 1 else (s < 31)
            row = ext.at[own:own + 2, src_row]
            moves.append(
                (
                    remote(row, ext.at[far:far + 2, dst_row], spot(s + dy, **ahead)),
                    jnp.logical_and(gives, sends_x),
                    jnp.logical_and(gets, gets_x),
                )
            )
            moves.append((remote(row, ext.at[own:own + 2, dst_row], spot(s + dy)), gives, gets))
        return moves

    def start_halo(moves):
        for copy, sends, _ in moves:
            pl.when(sends)(copy.start)

    def finish_halo(moves):
        for copy, sends, gets in moves:
            pl.when(gets)(copy.wait_recv)
            pl.when(sends)(copy.wait_send)

    own_v.wait()
    video_halo = halo(vext, 2, 0, 1)
    start_halo(video_halo)
    for step in (2, 1, 0):
        for part in range(2):
            w_copies[step, part].start()

    column = lax.broadcasted_iota(jnp.int32, (32, 128), 0)

    def build(ext, high, low):
        @pl.loop(0, 4)
        def _(frame):
            base = pl.multiple_of(frame * 128, 128)
            for line in range(6):
                value = ext[frame, line]
                for e in range(3):
                    if e == 0:
                        moved = jnp.where(column == 0, 0.0, pltpu.roll(value, 1, 0))
                    elif e == 2:
                        moved = jnp.where(column == 31, 0.0, pltpu.roll(value, 31, 0))
                    else:
                        moved = value
                    top = moved.astype(BF16)
                    rest = (moved - top.astype(F32)).astype(BF16)
                    for b in range(3):
                        r = line - b
                        if 0 <= r < 4:
                            lanes = slice((b * 3 + e) * 128, (b * 3 + e + 1) * 128)
                            high[pl.ds(base + r * 32, 32), lanes] = top
                            low[pl.ds(base + r * 32, 32), lanes] = rest

    def split(value):
        top = value.astype(BF16)
        return top, (value - top.astype(F32)).astype(BF16)

    def conv_step(high, low, weight, step, first):
        rows = pl.ds(step * 128, 256)
        lines = pl.ds(step * 1152, 1152)
        both = jnp.dot(high[rows, :], weight[lines, :], preferred_element_type=F32)
        rest = jnp.dot(low[rows, :], weight[lines, 0:128], preferred_element_type=F32)
        total = both[:, 0:128] + both[:, 128:256] + rest
        if first:
            acc[...] = total
        else:
            acc[...] += total

    def weight_grad(high, low, g):
        @pl.loop(0, 3)
        def _(step):
            rows = pl.ds(pl.multiple_of(step * 128, 128), 256)
            dims = (((0,), (0,)), ((), ()))
            both = lax.dot_general(high[rows, :], gcat[...], dims, preferred_element_type=F32)
            rest = lax.dot_general(
                low[rows, :], gcat[:, 0:128], dims, preferred_element_type=F32
            )
            total = both[:, 0:128] + both[:, 128:256] + rest
            for k in range(9):
                g[:, step * 9 + k] = total[k * 128:(k + 1) * 128].reshape(GROUPS, 8, 128)

    def prepare(start, stop, section):
        @pl.loop(start, stop)
        def _(tap):
            rows = pl.ds(pl.multiple_of(tap * 128, 128), 128)
            value = wboth[section, rows]
            places = [(value, (wc0, wc1)[section], rows)]
            if section == 1:
                flipped = pl.ds(pl.multiple_of((TAPS - 1 - tap) * 128, 128), 128)
                places.append((value.T, wct, flipped))
            for part, ref, place in places:
                top, rest = split(part)
                ref[place, 0:128] = top
                ref[place, 128:256] = rest

    own_w.wait()
    pl.when(seg == 0)(lambda: prepare(0, TAPS, 0))
    pl.when(seg == 1)(lambda: prepare(0, TAPS, 1))
    finish_halo(video_halo)
    build(vext, pvh, pvl)

    for index, step in enumerate((2, 1, 0)):
        await_received(w_got + step, wboth.at[other, 0:2 * QUARTER])
        for part in range(2):
            w_relays[step, part].start()
        await_received(w_shared + step, wboth.at[other, 0:2 * QUARTER])
        pl.when(seg == 1)(lambda: prepare(step * 9, step * 9 + 9, 0))
        pl.when(seg == 0)(lambda: prepare(step * 9, step * 9 + 9, 1))
        conv_step(pvh, pvl, wc0, step, index == 0)

    hidden = acc[...]
    sigmoid = 1.0 / (1.0 + jnp.exp(-hidden))
    slope[...] = sigmoid * (1.0 + hidden * (1.0 - sigmoid))
    lext[2:4, 1:5] = (hidden / (1.0 + jnp.exp(-hidden))).reshape(2, 4, 32, 128)
    latent_halo = halo(lext, 2, 0, 1)
    start_halo(latent_halo)
    finish_halo(latent_halo)
    build(lext, plh, pll)
    for step in range(3):
        conv_step(plh, pll, wc1, step, step == 0)
    cot = (acc[...] - vext[2:4, 1:5].reshape(256, 128)) * (65536.0 ** -0.5)
    cext[0:2, 1:5] = cot.reshape(2, 4, 32, 128)
    cot_halo = halo(cext, 0, 2, -1)
    start_halo(cot_halo)
    top, rest = split(cot)
    gcat[:, 0:128] = top
    gcat[:, 128:256] = rest
    weight_grad(plh, pll, g1)

    near = (("tm", x), ("y", y))
    wide = (("y", y), ("tm", x))
    order = (2, 1, 3, 0)
    parts = (slice(0, 4), slice(4, 7))
    side = (1, -1)

    def block(h, step, u):
        cut = parts[u]
        return pl.ds(ring(wide[h][1], step) * 7 + cut.start, cut.stop - cut.start)

    class Sum:
        def __init__(self, sec, g, ra):
            self.sec, self.g, self.ra = sec, g, ra
            self.sent = new(sends, 4)
            self.paired = new(receipts, 8)
            self.summed = new(receipts, 8)
            self.relayed = new(receipts, 8)
            self.widened = new(receipts, 2)

        def start_pair(self):
            for u in range(2):
                for j, step in enumerate(order):
                    for h in range(2):
                        rows = pl.ds((1 - c) * 8 + h * 4, 4)
                        remote(
                            self.g.at[rows, block(h, step, u)],
                            self.ra.at[h, j, :, parts[u]],
                            {"core": 1 - c}, self.sent, self.paired + u * 4 + j,
                        ).start()

        def start_first(self, u):
            cut = parts[u]
            for j, step in enumerate(order):
                await_received(self.paired + u * 4 + j, self.ra.at[:, j, :, cut])
                for h in range(2):
                    taps = block(h, step, u)
                    base = c * 8 + h * 4
                    self.g[pl.ds(base, 4), taps] += self.ra[h, j, :, cut]
                    axis, place = near[h]
                    f = side[u]
                    remote(
                        self.g.at[base + ring(place, 2), taps],
                        rl.at[self.sec, h, j, cut],
                        {axis: ring(place, f)}, self.sent + 1, self.relayed + u * 4 + j,
                    ).start()
                    remote(
                        self.g.at[base + ring(place, -f), taps],
                        rb.at[self.sec, h, j, 1, cut],
                        {axis: ring(place, -f)}, self.sent + 1, self.summed + u * 4 + j,
                    ).start()

        def relay_first(self, u):
            cut = parts[u]
            for j, step in enumerate(order):
                await_received(self.relayed + u * 4 + j, rl.at[self.sec, :, j, cut])
                for h in range(2):
                    axis, place = near[h]
                    peer = ring(place, side[u])
                    taps = block(h, step, u)
                    index = c * 8 + h * 4 + peer
                    self.g[index, taps] += rl[self.sec, h, j, cut]
                    remote(
                        self.g.at[index, taps], rb.at[self.sec, h, j, 0, cut],
                        {axis: peer}, self.sent + 3, self.summed + u * 4 + j,
                    ).start()

        def start_second(self, u):
            cut = parts[u]
            sec = self.sec
            for j, step in enumerate(order):
                await_received(self.summed + u * 4 + j, rb.at[sec, :, j, :, cut])
                for h in range(2):
                    total = self.g[c * 8 + h * 4 + near[h][1], block(h, step, u)]
                    total += rb[sec, h, j, 0, cut] + rb[sec, h, j, 1, cut]
                    if step == 0:
                        tt[sec, h, cut] = total
                    else:
                        sb[sec, h, j, cut] = total
                        axis, place = wide[h]
                        remote(
                            sb.at[sec, h, j, cut], rc.at[sec, h, j, cut],
                            {axis: ring(place, step)}, self.sent + 2, self.widened + u,
                        ).start()

        def start_third(self, u):
            cut = parts[u]
            sec = self.sec
            await_received(self.widened + u, rc.at[sec, :, :, cut])
            for h in range(2):
                tt[sec, h, cut] += rc[sec, h, 0, cut] + rc[sec, h, 1, cut] + rc[sec, h, 2, cut]

            @pl.when(seg != sec)
            def _():
                remote(
                    tt.at[sec, :, cut], rd.at[:, cut], {"segment": other},
                    crossing, crossed + u,
                ).start()

        def start_fourth(self, u):
            cut = parts[u]

            @pl.when(seg == self.sec)
            def _():
                await_received(crossed + u, rd.at[:, cut])
                tt[self.sec, :, cut] += rd[:, cut]
                for d in (2, 1, 3):
                    remote(
                        tt.at[self.sec, :, cut], re.at[d - 1, :, cut], {"zh": ring(zh, d)},
                        stacking, stacked + u,
                    ).start()

        def finish(self):
            await_sent(self.sent, self.ra)
            await_sent(self.sent + 1, rb.at[self.sec])
            await_sent(self.sent + 2, sb.at[self.sec])
            await_sent(self.sent + 3, rl.at[self.sec])

    crossing, stacking, crossed, stacked = new(sends), new(sends), new(receipts, 2), new(receipts, 2)
    decoder = Sum(1, g1, ra1)
    encoder = Sum(0, g0, ra0)
    decoder.start_pair()
    decoder.start_first(0)
    decoder.start_first(1)

    finish_halo(cot_halo)
    build(cext, pch, pcl)
    for step in range(3):
        conv_step(pch, pcl, wct, step, step == 0)
    top, rest = split(acc[...] * slope[...])
    gcat[:, 0:128] = top
    gcat[:, 128:256] = rest
    weight_grad(pvh, pvl, g0)
    encoder.start_pair()
    decoder.relay_first(0)
    decoder.relay_first(1)
    encoder.start_first(0)
    encoder.start_first(1)
    encoder.relay_first(0)
    decoder.start_second(0)
    encoder.relay_first(1)
    decoder.start_second(1)
    encoder.start_second(0)
    encoder.start_second(1)
    decoder.start_third(0)
    decoder.start_third(1)
    encoder.start_third(0)
    encoder.start_third(1)
    decoder.start_fourth(0)
    encoder.start_fourth(0)
    decoder.start_fourth(1)
    encoder.start_fourth(1)

    spreading, passing, forwarding, sharing = new(sends), new(sends), new(sends), new(sends)
    spread, chained = new(receipts, 6), new(receipts, 8)
    ended, forwarded, shared = new(receipts, 2), new(receipts, 2), new(receipts)

    def group(h, e):
        return c * 8 + h * 4 + ring(near[h][1], e)

    def pass_on(h, u, d):
        for e in (1, -1):
            piece = full.at[block(h, -d, u), group(h, 0)]
            axis, place = near[h]
            remote(
                uu.at[h, parts[u]] if d == 0 else piece, piece,
                {axis: ring(place, e)}, passing,
                chained + u * 4 + d if e == side[u] else ended + u,
            ).start()

    def forward(d):
        for u, cut in enumerate(parts):
            await_received(chained + u * 4 + d, uu.at[:, cut])
            for h in range(2):
                piece = full.at[block(h, -d, u), group(h, -side[u])]
                axis, place = near[h]
                remote(
                    piece, piece, {axis: ring(place, side[u])}, forwarding, forwarded + u
                ).start()

    def pass_block(d):
        for u, cut in enumerate(parts):
            await_received(spread + u * 3 + d - 1, uu.at[:, cut])
            for h in range(2):
                pass_on(h, u, d)

    def share(e):
        for h in range(2):
            whole = full.at[:, group(h, e)]
            remote(whole, whole, {"core": 1 - c}, sharing, shared).start()

    for u, cut in enumerate(parts):
        await_received(stacked + u, re.at[:, :, cut])
        for h in range(2):
            total = tt[seg, h, cut] + re[0, h, cut] + re[1, h, cut] + re[2, h, cut]
            uu[h, cut] = total
            full[block(h, 0, u), group(h, 0)] = total
            axis, place = wide[h]
            for d in (2, 1, 3):
                remote(
                    uu.at[h, cut], full.at[block(h, 0, u), group(h, 0)],
                    {axis: ring(place, d)}, spreading, spread + u * 3 + d - 1,
                ).start()
            pass_on(h, u, 0)
    pass_block(1)
    pass_block(3)
    forward(0)
    pass_block(2)
    share(0)
    forward(1)
    forward(3)
    forward(2)
    for u, cut in enumerate(parts):
        await_received(ended + u, ra0.at[:, :, 0, cut])
    share(1)
    share(-1)
    for u, cut in enumerate(parts):
        await_received(forwarded + u, ra0.at[:, :, 0, cut])
    share(2)
    await_received(shared, ra0)

    decoder.finish()
    encoder.finish()
    await_sent(crossing, rd)
    await_sent(stacking, re)
    await_sent(spreading, re)
    await_sent(passing, rb.at[0])
    await_sent(forwarding, rl.at[0])
    await_sent(sharing, ra0)
    await_sent(w_sent, wboth.at[0, 0:6 * QUARTER])
    await_sent(w_passed, wboth.at[0, 0:6 * QUARTER])
    assert sends[0] <= SENDS and receipts[0] <= RECEIPTS, (sends, receipts)


def local(video_clips, conv_weights):
    vm = pltpu.VMEM
    ext = vm((4, 6, 32, 128), F32)
    patches = vm((512, 1152), BF16)
    wcat = vm((3456, 256), BF16)
    grads = vm((GROUPS, PAD, 8, 128), F32)
    quarters = vm((2, 4, 4, 7, 8, 128), F32)
    summed = pl.pallas_call(
        kernel,
        out_shape=pltpu.VMEM((PAD, GROUPS, 8, 128), F32),
        in_specs=[pl.BlockSpec(memory_space=pl.ANY)] * 2,
        out_specs=pl.BlockSpec(memory_space=pltpu.VMEM),
        scratch_shapes=[
            ext, ext, ext,
            patches, patches, patches, patches, patches, patches,
            vm((2, 3456, 128), F32), wcat, wcat, wcat,
            vm((256, 128), F32), vm((256, 128), F32), vm((256, 256), BF16),
            grads, grads, quarters, quarters,
            vm((2, 2, 4, 2, 7, 8, 128), F32),
            vm((2, 2, 4, 7, 8, 128), F32),
            vm((2, 2, 3, 7, 8, 128), F32),
            vm((2, 2, 3, 7, 8, 128), F32),
            vm((2, 2, 7, 8, 128), F32),
            vm((2, 7, 8, 128), F32),
            vm((3, 2, 7, 8, 128), F32),
            vm((2, 7, 8, 128), F32),
            pltpu.SemaphoreType.DMA((2,)),
            pltpu.SemaphoreType.DMA((SENDS,)),
            pltpu.SemaphoreType.DMA((RECEIPTS,)),
        ],
        compiler_params=pltpu.CompilerParams(
            collective_id=0, has_side_effects=True, vmem_limit_bytes=60 * 1024 * 1024
        ),
        name="step",
    )(video_clips, conv_weights)
    return summed[:TAPS].reshape(1, TAPS * 128, 128)


def solution(mesh):
    finer = Mesh(
        mesh.devices.reshape(mesh.shape["segment"], mesh.shape["tm"], 4, 4, 2), AXES
    )
    in_specs = (P(None, "tm", ("zh", "y", "core"), None, None), P("segment", None, None))
    return jax.shard_map(
        local, mesh=finer, in_specs=in_specs, out_specs=P("segment", None, None), check_vma=False
    )
```

```python
import jax
import jax.numpy as jnp
from jax import lax
from jax.experimental import pallas as pl
from jax.experimental.pallas import tpu as pltpu
from jax.sharding import Mesh
from jax.sharding import PartitionSpec as P

MESH = pl.DeviceIdType.MESH
AXES = ("segment", "tm", "zh", "y", "core")
F32 = jnp.float32
BF16 = jnp.bfloat16
TAPS = 27
PAD = 28
GROUPS = 16
NEAR_ROWS = 224
FAR_ROWS = 352
SENDS = 34
RECEIPTS = 79


def kernel(
    vid_ref, w_ref, full,
    vext, lext, cext, uext, mix, part_sum,
    pvh, pvl, plh, pll, pch, pcl,
    wboth, wc0, wc1, wct,
    acc, slope, gcat,
    g0, g1, ra0, ra1, rb, sb, rc, tt, rd, re, uu,
    local_sem, send_sem, recv_sem,
):
    seg = lax.axis_index("segment")
    x = lax.axis_index("tm")
    zh = lax.axis_index("zh")
    y = lax.axis_index("y")
    c = lax.axis_index("core")
    s = zh * 8 + y * 2 + c
    sends, receipts = [0], [0]

    def new(counter, count=1):
        counter[0] += count
        return counter[0] - count

    def spot(index, **others):
        index = lax.rem(index + 32, 32)
        return {"zh": index // 8, "y": lax.rem(index // 2, 4), "core": lax.rem(index, 2), **others}

    def ring(value, step):
        return lax.rem(value + step + 4, 4)

    other = 1 - seg
    link_b = ring(zh, 2 * seg - 1)

    def remote(src, dst, device, sent=None, received=None):
        sent = new(sends) if sent is None else sent
        received = new(receipts) if received is None else received
        return pltpu.make_async_remote_copy(
            src_ref=src,
            dst_ref=dst,
            send_sem=send_sem.at[sent],
            recv_sem=recv_sem.at[received],
            device_id=device,
            device_id_type=MESH,
        )

    def await_sent(slot, like):
        pltpu.make_async_copy(like, like, send_sem.at[slot]).wait()

    def await_received(slot, like):
        pltpu.make_async_copy(like, like, recv_sem.at[slot]).wait()

    own_w = pltpu.make_async_copy(w_ref.at[0], wboth.at[seg], local_sem.at[0])
    own_v = pltpu.make_async_copy(vid_ref.at[seg], vext.at[2:4, 1:5], local_sem.at[1])
    helped = pltpu.make_async_copy(vid_ref.at[1], uext.at[:, 1:5], local_sem.at[2])
    pl.when(seg == 0)(helped.start)
    own_v.start()
    own_w.start()
    for rim, line in ((s == 0, 0), (s == 31, 5)):
        @pl.when(rim)
        def _():
            uext[:, line] = jnp.zeros((2, 32, 128), F32)

    for ext, edge, far in ((vext, x == 0, 0), (lext, x == 0, 0), (cext, x == 3, 2)):
        @pl.when(edge)
        def _():
            ext[far:far + 2] = jnp.zeros((2, 6, 32, 128), F32)

        for rim, line in ((s == 0, 0), (s == 31, 5)):
            @pl.when(rim)
            def _():
                ext[:, line] = jnp.zeros((4, 32, 128), F32)

    for g in (g0, g1):
        g[:, TAPS] = jnp.zeros((GROUPS, 8, 128), F32)

    barrier = pltpu.get_barrier_semaphore()
    greet = [{"tm": ring(x, d)} for d in (1, 2, 3)]
    greet += [{"y": ring(y, d)} for d in (1, 2, 3)]
    greet += [{"zh": ring(zh, d)} for d in (1, 2, 3)]
    greet += [{"core": 1 - c}, {"segment": other}, {"segment": other, "zh": link_b}]
    greet += [spot(s + 1), spot(s - 1)]
    greet += [spot(s + dy, tm=ring(x, dx)) for dy in (1, -1) for dx in (1, -1)]
    for device in greet:
        pl.semaphore_signal(barrier, inc=1, device_id=device, device_id_type=MESH)
    pl.semaphore_wait(barrier, len(greet))

    def quarter(step, part, core):
        count = (NEAR_ROWS, FAR_ROWS)[part]
        return pl.ds(step * 1152 + part * 2 * NEAR_ROWS + core * count, count)

    w_copies = {}
    w_relays = {}
    w_sent, w_passed = new(sends), new(sends)
    w_got, w_shared = new(receipts, 3), new(receipts, 3)
    for step in range(3):
        for part in range(2):
            rows = quarter(step, part, c)
            device = {"segment": other} if part == 0 else {"segment": other, "zh": link_b}
            w_copies[step, part] = remote(
                w_ref.at[0, rows], wboth.at[seg, rows], device, w_sent, w_got + step
            )
            w_relays[step, part] = remote(
                wboth.at[other, rows], wboth.at[other, rows], {"core": 1 - c},
                w_passed, w_shared + step,
            )

    def halo(ext, own, far, shift):
        ahead = {"tm": ring(x, shift)}
        sends_x = (x < 3) if shift == 1 else (x > 0)
        gets_x = (x > 0) if shift == 1 else (x < 3)
        frames, beyond = slice(own, own + 2), slice(far, far + 2)
        inner, outer = 4 - 3 * c, 1 + 3 * c
        up, down = (s < 31), (s > 0)
        edge = jnp.logical_or(jnp.logical_and(c == 1, up), jnp.logical_and(c == 0, down))
        corner = remote(
            ext.at[frames, outer], ext.at[beyond, 5 - 5 * c], spot(s + 2 * c - 1, **ahead)
        )
        rest = pl.ds(1 + c, 3)
        moves = {
            "first": (remote(ext.at[frames, inner], ext.at[beyond, inner], ahead), sends_x, gets_x),
            "next": (remote(ext.at[frames, 4], ext.at[frames, 0], spot(s + 1)), up, down),
            "last": (remote(ext.at[frames, 1], ext.at[frames, 5], spot(s - 1)), down, up),
            "corner": (corner, jnp.logical_and(edge, sends_x), jnp.logical_and(edge, gets_x)),
            "rest": (remote(ext.at[frames, rest], ext.at[beyond, rest], ahead), sends_x, gets_x),
            "pass": (
                remote(ext.at[beyond, inner], ext.at[beyond, 5 * c], {"core": 1 - c}),
                gets_x, gets_x,
            ),
        }
        return moves

    def start_halo(moves):
        for name, (copy, gives, _) in moves.items():
            if name != "pass":
                pl.when(gives)(copy.start)

    def finish_halo(moves):
        first, _, gets = moves["first"]

        @pl.when(gets)
        def _():
            first.wait_recv()
            moves["pass"][0].start()

        for name, (copy, gives, gets) in moves.items():
            if name != "first":
                pl.when(gets)(copy.wait_recv)
            pl.when(gives)(copy.wait_send)

    help_rows = (
        (remote(uext.at[:, 4], uext.at[:, 0], spot(s + 1)), s < 31, s > 0),
        (remote(uext.at[:, 1], uext.at[:, 5], spot(s - 1)), s > 0, s < 31),
    )
    help_sum = remote(mix, part_sum, {"segment": other})

    @pl.when(seg == 0)
    def _():
        helped.wait()
        for copy, gives, _ in help_rows:
            pl.when(gives)(copy.start)

    own_v.wait()
    video_halo = halo(vext, 2, 0, 1)
    start_halo(video_halo)
    for step in (2, 1, 0):
        for part in range(2):
            if step == 2:
                pl.when(seg == 1)(w_copies[step, part].start)
            else:
                w_copies[step, part].start()

    column = lax.broadcasted_iota(jnp.int32, (32, 128), 0)

    def build(ext, high, low, frames=4):
        @pl.loop(0, frames)
        def _(frame):
            base = pl.multiple_of(frame * 128, 128)
            for line in range(6):
                value = ext[frame, line]
                for e in range(3):
                    if e == 0:
                        moved = jnp.where(column == 0, 0.0, pltpu.roll(value, 1, 0))
                    elif e == 2:
                        moved = jnp.where(column == 31, 0.0, pltpu.roll(value, 31, 0))
                    else:
                        moved = value
                    top = moved.astype(BF16)
                    rest = (moved - top.astype(F32)).astype(BF16)
                    for b in range(3):
                        r = line - b
                        if 0 <= r < 4:
                            lanes = slice((b * 3 + e) * 128, (b * 3 + e + 1) * 128)
                            high[pl.ds(base + r * 32, 32), lanes] = top
                            low[pl.ds(base + r * 32, 32), lanes] = rest

    def split(value):
        top = value.astype(BF16)
        return top, (value - top.astype(F32)).astype(BF16)

    def product(high, low, weight, first, step):
        rows = pl.ds(first * 128, 256)
        lines = pl.ds(step * 1152, 1152)
        both = jnp.dot(high[rows, :], weight[lines, :], preferred_element_type=F32)
        rest = jnp.dot(low[rows, :], weight[lines, 0:128], preferred_element_type=F32)
        return both[:, 0:128] + both[:, 128:256] + rest

    def conv_step(high, low, weight, step, first):
        total = product(high, low, weight, step, step)
        if first:
            acc[...] = total
        else:
            acc[...] += total

    def weight_grad(high, low, g):
        @pl.loop(0, 3)
        def _(step):
            rows = pl.ds(pl.multiple_of(step * 128, 128), 256)
            dims = (((0,), (0,)), ((), ()))
            both = lax.dot_general(high[rows, :], gcat[...], dims, preferred_element_type=F32)
            rest = lax.dot_general(
                low[rows, :], gcat[:, 0:128], dims, preferred_element_type=F32
            )
            total = both[:, 0:128] + both[:, 128:256] + rest
            for k in range(9):
                g[:, step * 9 + k] = total[k * 128:(k + 1) * 128].reshape(GROUPS, 8, 128)

    def prepare(start, stop, section):
        @pl.loop(start, stop)
        def _(tap):
            rows = pl.ds(pl.multiple_of(tap * 128, 128), 128)
            value = wboth[section, rows]
            places = [(value, (wc0, wc1)[section], rows)]
            if section == 1:
                flipped = pl.ds(pl.multiple_of((TAPS - 1 - tap) * 128, 128), 128)
                places.append((value.T, wct, flipped))
            for part, ref, place in places:
                top, rest = split(part)
                ref[place, 0:128] = top
                ref[place, 128:256] = rest

    own_w.wait()
    pl.when(seg == 0)(lambda: prepare(0, TAPS, 0))
    pl.when(seg == 1)(lambda: prepare(0, TAPS, 1))

    @pl.when(seg == 0)
    def _():
        for copy, _, gets in help_rows:
            pl.when(gets)(copy.wait_recv)
        build(uext, plh, pll, 2)
        mix[...] = product(plh, pll, wc0, 0, 2)
        help_sum.start()

    finish_halo(video_halo)
    build(vext, pvh, pvl)

    latent_halo = halo(lext, 2, 0, 1)

    def encode():
        hidden = acc[...]
        sigmoid = 1.0 / (1.0 + jnp.exp(-hidden))
        slope[...] = sigmoid * (1.0 + hidden * (1.0 - sigmoid))
        lext[2:4, 1:5] = (hidden / (1.0 + jnp.exp(-hidden))).reshape(2, 4, 32, 128)
        start_halo(latent_halo)

    @pl.when(seg == 0)
    def _():
        for step in range(3):
            conv_step(pvh, pvl, wc0, step, step == 0)
        encode()

    def take(step):
        await_received(w_got + step, wboth.at[other, 0:576])
        for part in range(2):
            w_relays[step, part].start()
        await_received(w_shared + step, wboth.at[other, 0:576])

    @pl.when(seg == 0)
    def _():
        for step in (2, 1, 0):
            take(step)
            prepare(step * 9, step * 9 + 9, 1)

    @pl.when(seg == 1)
    def _():
        for step in (1, 0):
            take(step)
            prepare(step * 9, step * 9 + 9, 0)
            conv_step(pvh, pvl, wc0, step, step == 1)
        help_sum.wait_recv()
        acc[...] += part_sum[...]
        encode()

    finish_halo(latent_halo)
    build(lext, plh, pll)
    for step in range(3):
        conv_step(plh, pll, wc1, step, step == 0)
    cot = (acc[...] - vext[2:4, 1:5].reshape(256, 128)) * (65536.0 ** -0.5)
    cext[0:2, 1:5] = cot.reshape(2, 4, 32, 128)
    cot_halo = halo(cext, 0, 2, -1)
    start_halo(cot_halo)
    top, rest = split(cot)
    gcat[:, 0:128] = top
    gcat[:, 128:256] = rest
    weight_grad(plh, pll, g1)

    near = (("tm", x), ("y", y))
    wide = (("y", y), ("tm", x))
    order = (2, 1, 3, 0)
    parts = (slice(0, 4), slice(4, 7))

    def block(h, step, u):
        cut = parts[u]
        return pl.ds(ring(wide[h][1], step) * 7 + cut.start, cut.stop - cut.start)

    class Sum:
        def __init__(self, sec, g, ra):
            self.sec, self.g, self.ra = sec, g, ra
            self.sent = new(sends, 3)
            self.paired = new(receipts, 8)
            self.summed = new(receipts, 8)
            self.widened = new(receipts, 2)

        def start_pair(self):
            for u in range(2):
                for j, step in enumerate(order):
                    for h in range(2):
                        rows = pl.ds((1 - c) * 8 + h * 4, 4)
                        remote(
                            self.g.at[rows, block(h, step, u)],
                            self.ra.at[h, j, :, parts[u]],
                            {"core": 1 - c}, self.sent, self.paired + u * 4 + j,
                        ).start()

        def start_first(self, u):
            cut = parts[u]
            for j, step in enumerate(order):
                await_received(self.paired + u * 4 + j, self.ra.at[:, j, :, cut])
                for h in range(2):
                    taps = block(h, step, u)
                    base = c * 8 + h * 4
                    self.g[pl.ds(base, 4), taps] += self.ra[h, j, :, cut]
                    axis, place = near[h]
                    for d in (2, 1, 3):
                        peer = ring(place, d)
                        remote(
                            self.g.at[base + peer, taps],
                            rb.at[self.sec, h, j, d - 1, cut],
                            {axis: peer}, self.sent + 1, self.summed + u * 4 + j,
                        ).start()

        def start_second(self, u):
            cut = parts[u]
            sec = self.sec
            for j, step in enumerate(order):
                await_received(self.summed + u * 4 + j, rb.at[sec, :, j, :, cut])
                for h in range(2):
                    total = self.g[c * 8 + h * 4 + near[h][1], block(h, step, u)]
                    total += rb[sec, h, j, 0, cut] + rb[sec, h, j, 1, cut] + rb[sec, h, j, 2, cut]
                    if step == 0:
                        tt[sec, h, cut] = total
                    else:
                        sb[sec, h, j, cut] = total
                        axis, place = wide[h]
                        remote(
                            sb.at[sec, h, j, cut], rc.at[sec, h, j, cut],
                            {axis: ring(place, step)}, self.sent + 2, self.widened + u,
                        ).start()

        def start_third(self, u):
            cut = parts[u]
            sec = self.sec
            await_received(self.widened + u, rc.at[sec, :, :, cut])
            for h in range(2):
                tt[sec, h, cut] += rc[sec, h, 0, cut] + rc[sec, h, 1, cut] + rc[sec, h, 2, cut]

            @pl.when(seg != sec)
            def _():
                remote(
                    tt.at[sec, :, cut], rd.at[:, cut], {"segment": other},
                    crossing, crossed + u,
                ).start()

        def start_fourth(self, u):
            cut = parts[u]

            @pl.when(seg == self.sec)
            def _():
                await_received(crossed + u, rd.at[:, cut])
                tt[self.sec, :, cut] += rd[:, cut]
                for d in (2, 1, 3):
                    remote(
                        tt.at[self.sec, :, cut], re.at[d - 1, :, cut], {"zh": ring(zh, d)},
                        stacking, stacked + u,
                    ).start()

        def finish(self):
            await_sent(self.sent, self.ra)
            await_sent(self.sent + 1, rb.at[self.sec])
            await_sent(self.sent + 2, sb.at[self.sec])

    crossing, stacking, crossed, stacked = new(sends), new(sends), new(receipts, 2), new(receipts, 2)
    decoder = Sum(1, g1, ra1)
    encoder = Sum(0, g0, ra0)
    decoder.start_pair()
    decoder.start_first(0)
    decoder.start_first(1)

    finish_halo(cot_halo)
    build(cext, pch, pcl)
    for step in range(3):
        conv_step(pch, pcl, wct, step, step == 0)
    top, rest = split(acc[...] * slope[...])
    gcat[:, 0:128] = top
    gcat[:, 128:256] = rest
    weight_grad(pvh, pvl, g0)
    encoder.start_pair()
    encoder.start_first(0)
    encoder.start_first(1)
    decoder.start_second(0)
    decoder.start_second(1)
    encoder.start_second(0)
    encoder.start_second(1)
    decoder.start_third(0)
    decoder.start_third(1)
    encoder.start_third(0)
    encoder.start_third(1)
    decoder.start_fourth(0)
    decoder.start_fourth(1)
    encoder.start_fourth(0)
    encoder.start_fourth(1)

    spreading, passing, sharing = new(sends), new(sends), new(sends)
    spread, passed, shared = new(receipts, 6), new(receipts, 3), new(receipts)

    def group(h, e):
        return c * 8 + h * 4 + ring(near[h][1], e)

    def pass_on(h, u, d):
        for e in (2, 1, 3):
            piece = full.at[block(h, -d, u), group(h, 0)]
            axis, place = near[h]
            remote(
                uu.at[h, parts[u]] if d == 0 else piece, piece,
                {axis: ring(place, e)}, passing, passed + e - 1,
            ).start()

    for u, cut in enumerate(parts):
        await_received(stacked + u, re.at[:, :, cut])
        for h in range(2):
            total = tt[seg, h, cut] + re[0, h, cut] + re[1, h, cut] + re[2, h, cut]
            uu[h, cut] = total
            full[block(h, 0, u), group(h, 0)] = total
            axis, place = wide[h]
            for d in (2, 1, 3):
                remote(
                    uu.at[h, cut], full.at[block(h, 0, u), group(h, 0)],
                    {axis: ring(place, d)}, spreading, spread + u * 3 + d - 1,
                ).start()
            pass_on(h, u, 0)
    for u, cut in enumerate(parts):
        for d in (1, 3, 2):
            await_received(spread + u * 3 + d - 1, uu.at[:, cut])
            for h in range(2):
                pass_on(h, u, d)
    for e in (0, 1, 3, 2):
        if e > 0:
            await_received(passed + e - 1, full.at[:, 0:2])
        for h in range(2):
            whole = full.at[:, group(h, -e)]
            remote(whole, whole, {"core": 1 - c}, sharing, shared).start()
    await_received(shared, ra0)

    decoder.finish()
    encoder.finish()
    await_sent(crossing, rd)
    await_sent(stacking, re)
    await_sent(spreading, re)
    await_sent(passing, rb.at[0])
    await_sent(sharing, ra0)

    @pl.when(seg == 0)
    def _():
        await_sent(w_sent, wboth.at[0, 0:4 * 288])
        await_sent(w_passed, wboth.at[0, 0:6 * 288])
        for copy, gives, _ in help_rows:
            pl.when(gives)(copy.wait_send)
        help_sum.wait_send()

    @pl.when(seg == 1)
    def _():
        await_sent(w_sent, wboth.at[0, 0:6 * 288])
        await_sent(w_passed, wboth.at[0, 0:4 * 288])

    assert sends[0] <= SENDS and receipts[0] <= RECEIPTS, (sends, receipts)


def local(video_clips, conv_weights):
    vm = pltpu.VMEM
    ext = vm((4, 6, 32, 128), F32)
    patches = vm((512, 1152), BF16)
    wcat = vm((3456, 256), BF16)
    grads = vm((GROUPS, PAD, 8, 128), F32)
    quarters = vm((2, 4, 4, 7, 8, 128), F32)
    summed = pl.pallas_call(
        kernel,
        out_shape=pltpu.VMEM((PAD, GROUPS, 8, 128), F32),
        in_specs=[pl.BlockSpec(memory_space=pl.ANY)] * 2,
        out_specs=pl.BlockSpec(memory_space=pltpu.VMEM),
        scratch_shapes=[
            ext, ext, ext, vm((2, 6, 32, 128), F32), vm((256, 128), F32), vm((256, 128), F32),
            patches, patches, patches, patches, patches, patches,
            vm((2, 3456, 128), F32), wcat, wcat, wcat,
            vm((256, 128), F32), vm((256, 128), F32), vm((256, 256), BF16),
            grads, grads, quarters, quarters,
            vm((2, 2, 4, 3, 7, 8, 128), F32),
            vm((2, 2, 3, 7, 8, 128), F32),
            vm((2, 2, 3, 7, 8, 128), F32),
            vm((2, 2, 7, 8, 128), F32),
            vm((2, 7, 8, 128), F32),
            vm((3, 2, 7, 8, 128), F32),
            vm((2, 7, 8, 128), F32),
            pltpu.SemaphoreType.DMA((3,)),
            pltpu.SemaphoreType.DMA((SENDS,)),
            pltpu.SemaphoreType.DMA((RECEIPTS,)),
        ],
        compiler_params=pltpu.CompilerParams(
            collective_id=0, has_side_effects=True, vmem_limit_bytes=60 * 1024 * 1024
        ),
        name="step",
    )(video_clips, conv_weights)
    return summed[:TAPS].reshape(1, TAPS * 128, 128)


def solution(mesh):
    finer = Mesh(
        mesh.devices.reshape(mesh.shape["segment"], mesh.shape["tm"], 4, 4, 2), AXES
    )
    in_specs = (P(None, "tm", ("zh", "y", "core"), None, None), P("segment", None, None))
    return jax.shard_map(
        local, mesh=finer, in_specs=in_specs, out_specs=P("segment", None, None), check_vma=False
    )
```

```python
import jax
import jax.numpy as jnp
from jax import lax
from jax.experimental import pallas as pl
from jax.experimental.pallas import tpu as pltpu
from jax.sharding import Mesh
from jax.sharding import PartitionSpec as P

MESH = pl.DeviceIdType.MESH
AXES = ("segment", "tm", "zh", "y", "core")
F32 = jnp.float32
BF16 = jnp.bfloat16
TAPS = 27
PAD = 28
GROUPS = 16
NEAR_ROWS = 224
FAR_ROWS = 352
SENDS = 34
RECEIPTS = 79


def kernel(
    vid_ref, w_ref, full,
    vext, lext, cext, uext, mix, part_sum,
    pvh, pvl, plh, pll, pch, pcl, pth, ptl,
    wboth, wc0, wc1, wct,
    acc, slope, gcat,
    g0, g1, ra0, ra1, rb, sb, rc, tt, rd, re, uu,
    local_sem, send_sem, recv_sem,
):
    seg = lax.axis_index("segment")
    x = lax.axis_index("tm")
    zh = lax.axis_index("zh")
    y = lax.axis_index("y")
    c = lax.axis_index("core")
    s = zh * 8 + y * 2 + c
    sends, receipts = [0], [0]

    def new(counter, count=1):
        counter[0] += count
        return counter[0] - count

    def spot(index, **others):
        index = lax.rem(index + 32, 32)
        return {"zh": index // 8, "y": lax.rem(index // 2, 4), "core": lax.rem(index, 2), **others}

    def ring(value, step):
        return lax.rem(value + step + 4, 4)

    other = 1 - seg
    link_b = ring(zh, 2 * seg - 1)

    def remote(src, dst, device, sent=None, received=None):
        sent = new(sends) if sent is None else sent
        received = new(receipts) if received is None else received
        return pltpu.make_async_remote_copy(
            src_ref=src,
            dst_ref=dst,
            send_sem=send_sem.at[sent],
            recv_sem=recv_sem.at[received],
            device_id=device,
            device_id_type=MESH,
        )

    def await_sent(slot, like):
        pltpu.make_async_copy(like, like, send_sem.at[slot]).wait()

    def await_received(slot, like):
        pltpu.make_async_copy(like, like, recv_sem.at[slot]).wait()

    own_w = pltpu.make_async_copy(w_ref.at[0], wboth.at[seg], local_sem.at[0])
    own_v = pltpu.make_async_copy(vid_ref.at[seg], vext.at[2:4, 1:5], local_sem.at[1])
    helped = pltpu.make_async_copy(vid_ref.at[1], uext.at[:, 1:5], local_sem.at[2])
    pl.when(seg == 0)(helped.start)
    own_v.start()
    own_w.start()
    for rim, line in ((s == 0, 0), (s == 31, 5)):
        @pl.when(rim)
        def _():
            uext[:, line] = jnp.zeros((2, 32, 128), F32)

    for ext, edge, far in ((vext, x == 0, 0), (lext, x == 0, 0), (cext, x == 3, 2)):
        @pl.when(edge)
        def _():
            ext[far:far + 2] = jnp.zeros((2, 6, 32, 128), F32)

        for rim, line in ((s == 0, 0), (s == 31, 5)):
            @pl.when(rim)
            def _():
                ext[:, line] = jnp.zeros((4, 32, 128), F32)

    for g in (g0, g1):
        g[:, TAPS] = jnp.zeros((GROUPS, 8, 128), F32)

    barrier = pltpu.get_barrier_semaphore()
    greet = [{"tm": ring(x, d)} for d in (1, 2, 3)]
    greet += [{"y": ring(y, d)} for d in (1, 2, 3)]
    greet += [{"zh": ring(zh, d)} for d in (1, 2, 3)]
    greet += [{"core": 1 - c}, {"segment": other}, {"segment": other, "zh": link_b}]
    greet += [spot(s + 1), spot(s - 1)]
    greet += [spot(s + dy, tm=ring(x, dx)) for dy in (1, -1) for dx in (1, -1)]
    for device in greet:
        pl.semaphore_signal(barrier, inc=1, device_id=device, device_id_type=MESH)
    pl.semaphore_wait(barrier, len(greet))

    def quarter(step, part, core):
        count = (NEAR_ROWS, FAR_ROWS)[part]
        return pl.ds(step * 1152 + part * 2 * NEAR_ROWS + core * count, count)

    w_copies = {}
    w_relays = {}
    w_sent, w_passed = new(sends), new(sends)
    w_got, w_shared = new(receipts, 3), new(receipts, 3)
    for step in range(3):
        for part in range(2):
            rows = quarter(step, part, c)
            device = {"segment": other} if part == 0 else {"segment": other, "zh": link_b}
            w_copies[step, part] = remote(
                w_ref.at[0, rows], wboth.at[seg, rows], device, w_sent, w_got + step
            )
            w_relays[step, part] = remote(
                wboth.at[other, rows], wboth.at[other, rows], {"core": 1 - c},
                w_passed, w_shared + step,
            )

    def halo(ext, own, far, shift):
        ahead = {"tm": ring(x, shift)}
        sends_x = (x < 3) if shift == 1 else (x > 0)
        gets_x = (x > 0) if shift == 1 else (x < 3)
        frames, beyond = slice(own, own + 2), slice(far, far + 2)
        inner, outer = 4 - 3 * c, 1 + 3 * c
        up, down = (s < 31), (s > 0)
        edge = jnp.logical_or(jnp.logical_and(c == 1, up), jnp.logical_and(c == 0, down))
        corner = remote(
            ext.at[frames, outer], ext.at[beyond, 5 - 5 * c], spot(s + 2 * c - 1, **ahead)
        )
        rest = pl.ds(1 + c, 3)
        moves = {
            "first": (remote(ext.at[frames, inner], ext.at[beyond, inner], ahead), sends_x, gets_x),
            "next": (remote(ext.at[frames, 4], ext.at[frames, 0], spot(s + 1)), up, down),
            "last": (remote(ext.at[frames, 1], ext.at[frames, 5], spot(s - 1)), down, up),
            "corner": (corner, jnp.logical_and(edge, sends_x), jnp.logical_and(edge, gets_x)),
            "rest": (remote(ext.at[frames, rest], ext.at[beyond, rest], ahead), sends_x, gets_x),
            "pass": (
                remote(ext.at[beyond, inner], ext.at[beyond, 5 * c], {"core": 1 - c}),
                gets_x, gets_x,
            ),
        }
        return moves

    def start_halo(moves):
        for name, (copy, gives, _) in moves.items():
            if name != "pass":
                pl.when(gives)(copy.start)

    def take_rows(moves):
        for name in ("next", "last"):
            copy, _, gets = moves[name]
            pl.when(gets)(copy.wait_recv)
        first, _, gets = moves["first"]

        @pl.when(gets)
        def _():
            first.wait_recv()
            moves["pass"][0].start()

    def take_frames(moves):
        for name in ("corner", "rest", "pass"):
            copy, _, gets = moves[name]
            pl.when(gets)(copy.wait_recv)
        for copy, gives, _ in moves.values():
            pl.when(gives)(copy.wait_send)

    help_rows = (
        (remote(uext.at[:, 4], uext.at[:, 0], spot(s + 1)), s < 31, s > 0),
        (remote(uext.at[:, 1], uext.at[:, 5], spot(s - 1)), s > 0, s < 31),
    )
    help_sum = remote(mix, part_sum, {"segment": other})

    @pl.when(seg == 0)
    def _():
        helped.wait()
        for copy, gives, _ in help_rows:
            pl.when(gives)(copy.start)

    own_v.wait()
    video_halo = halo(vext, 2, 0, 1)
    start_halo(video_halo)
    for step in (2, 1, 0):
        for part in range(2):
            if step == 2:
                pl.when(seg == 1)(w_copies[step, part].start)
            else:
                w_copies[step, part].start()

    column = lax.broadcasted_iota(jnp.int32, (32, 128), 0)

    def build(ext, high, low, start, stop):
        @pl.loop(start, stop)
        def _(frame):
            base = pl.multiple_of(frame * 128, 128)
            for line in range(6):
                value = ext[frame, line]
                for e in range(3):
                    if e == 0:
                        moved = jnp.where(column == 0, 0.0, pltpu.roll(value, 1, 0))
                    elif e == 2:
                        moved = jnp.where(column == 31, 0.0, pltpu.roll(value, 31, 0))
                    else:
                        moved = value
                    top = moved.astype(BF16)
                    rest = (moved - top.astype(F32)).astype(BF16)
                    for b in range(3):
                        r = line - b
                        if 0 <= r < 4:
                            lanes = slice((b * 3 + e) * 128, (b * 3 + e + 1) * 128)
                            high[pl.ds(base + r * 32, 32), lanes] = top
                            low[pl.ds(base + r * 32, 32), lanes] = rest

    def split(value):
        top = value.astype(BF16)
        return top, (value - top.astype(F32)).astype(BF16)

    def product(high, low, weight, first, step):
        rows = pl.ds(first * 128, 256)
        lines = pl.ds(step * 1152, 1152)
        both = jnp.dot(high[rows, :], weight[lines, :], preferred_element_type=F32)
        rest = jnp.dot(low[rows, :], weight[lines, 0:128], preferred_element_type=F32)
        return both[:, 0:128] + both[:, 128:256] + rest

    def conv_step(high, low, weight, step, first):
        total = product(high, low, weight, step, step)
        if first:
            acc[...] = total
        else:
            acc[...] += total

    def place_grad(g, step, both, rest):
        total = both[:, 0:128] + both[:, 128:256] + rest
        for k in range(9):
            g[:, step * 9 + k] = total[k * 128:(k + 1) * 128].reshape(GROUPS, 8, 128)

    def weight_grad(high, low, g):
        @pl.loop(0, 3)
        def _(step):
            rows = pl.ds(pl.multiple_of(step * 128, 128), 256)
            dims = (((0,), (0,)), ((), ()))
            both = lax.dot_general(high[rows, :], gcat[...], dims, preferred_element_type=F32)
            rest = lax.dot_general(
                low[rows, :], gcat[:, 0:128], dims, preferred_element_type=F32
            )
            place_grad(g, step, both, rest)

    def weight_grad_turned(high, low, g):
        @pl.loop(0, 3)
        def _(step):
            cells = pl.ds(pl.multiple_of(step * 128, 128), 256)
            both = jnp.dot(high[:, cells], gcat[...], preferred_element_type=F32)
            rest = jnp.dot(low[:, cells], gcat[:, 0:128], preferred_element_type=F32)
            place_grad(g, step, both, rest)

    def prepare(start, stop, section):
        @pl.loop(start, stop)
        def _(tap):
            rows = pl.ds(pl.multiple_of(tap * 128, 128), 128)
            value = wboth[section, rows]
            places = [(value, (wc0, wc1)[section], rows)]
            if section == 1:
                flipped = pl.ds(pl.multiple_of((TAPS - 1 - tap) * 128, 128), 128)
                places.append((value.T, wct, flipped))
            for part, ref, place in places:
                top, rest = split(part)
                ref[place, 0:128] = top
                ref[place, 128:256] = rest

    own_w.wait()
    pl.when(seg == 0)(lambda: prepare(0, TAPS, 0))
    pl.when(seg == 1)(lambda: prepare(0, TAPS, 1))

    @pl.when(seg == 0)
    def _():
        for copy, _, gets in help_rows:
            pl.when(gets)(copy.wait_recv)
        build(uext, plh, pll, 0, 2)
        mix[...] = product(plh, pll, wc0, 0, 2)
        help_sum.start()

    take_rows(video_halo)
    take_frames(video_halo)
    build(vext, pvh, pvl, 0, 4)

    latent_halo = halo(lext, 2, 0, 1)

    def encode():
        hidden = acc[...]
        sigmoid = 1.0 / (1.0 + jnp.exp(-hidden))
        slope[...] = sigmoid * (1.0 + hidden * (1.0 - sigmoid))
        lext[2:4, 1:5] = (hidden / (1.0 + jnp.exp(-hidden))).reshape(2, 4, 32, 128)
        start_halo(latent_halo)

    @pl.when(seg == 0)
    def _():
        for step in range(3):
            conv_step(pvh, pvl, wc0, step, step == 0)
        encode()

    @pl.loop(0, 9)
    def _(k):
        lanes = pl.ds(pl.multiple_of(k * 128, 128), 128)
        for source, turned in ((pvh, pth), (pvl, ptl)):
            turned[lanes, :] = source[:, lanes].T

    def take(step):
        await_received(w_got + step, wboth.at[other, 0:576])
        for part in range(2):
            w_relays[step, part].start()
        await_received(w_shared + step, wboth.at[other, 0:576])

    @pl.when(seg == 0)
    def _():
        for step in (2, 1, 0):
            take(step)
            prepare(step * 9, step * 9 + 9, 1)

    @pl.when(seg == 1)
    def _():
        for step in (1, 0):
            take(step)
            prepare(step * 9, step * 9 + 9, 0)
            conv_step(pvh, pvl, wc0, step, step == 1)
        help_sum.wait_recv()
        acc[...] += part_sum[...]
        encode()

    take_rows(latent_halo)
    build(lext, plh, pll, 2, 4)
    conv_step(plh, pll, wc1, 2, True)
    take_frames(latent_halo)
    build(lext, plh, pll, 0, 2)
    for step in (1, 0):
        conv_step(plh, pll, wc1, step, False)
    cot = (acc[...] - vext[2:4, 1:5].reshape(256, 128)) * (65536.0 ** -0.5)
    cext[0:2, 1:5] = cot.reshape(2, 4, 32, 128)
    cot_halo = halo(cext, 0, 2, -1)
    start_halo(cot_halo)
    top, rest = split(cot)
    gcat[:, 0:128] = top
    gcat[:, 128:256] = rest
    weight_grad(plh, pll, g1)

    near = (("tm", x), ("y", y))
    wide = (("y", y), ("tm", x))
    order = (2, 1, 3, 0)
    parts = (slice(0, 4), slice(4, 7))

    def block(h, step, u):
        cut = parts[u]
        return pl.ds(ring(wide[h][1], step) * 7 + cut.start, cut.stop - cut.start)

    class Sum:
        def __init__(self, sec, g, ra):
            self.sec, self.g, self.ra = sec, g, ra
            self.sent = new(sends, 3)
            self.paired = new(receipts, 8)
            self.summed = new(receipts, 8)
            self.widened = new(receipts, 2)

        def start_pair(self):
            for u in range(2):
                for j, step in enumerate(order):
                    for h in range(2):
                        rows = pl.ds((1 - c) * 8 + h * 4, 4)
                        remote(
                            self.g.at[rows, block(h, step, u)],
                            self.ra.at[h, j, :, parts[u]],
                            {"core": 1 - c}, self.sent, self.paired + u * 4 + j,
                        ).start()

        def start_first(self, u):
            cut = parts[u]
            for j, step in enumerate(order):
                await_received(self.paired + u * 4 + j, self.ra.at[:, j, :, cut])
                for h in range(2):
                    taps = block(h, step, u)
                    base = c * 8 + h * 4
                    self.g[pl.ds(base, 4), taps] += self.ra[h, j, :, cut]
                    axis, place = near[h]
                    for d in (2, 1, 3):
                        peer = ring(place, d)
                        remote(
                            self.g.at[base + peer, taps],
                            rb.at[self.sec, h, j, d - 1, cut],
                            {axis: peer}, self.sent + 1, self.summed + u * 4 + j,
                        ).start()

        def start_second(self, u):
            cut = parts[u]
            sec = self.sec
            for j, step in enumerate(order):
                await_received(self.summed + u * 4 + j, rb.at[sec, :, j, :, cut])
                for h in range(2):
                    total = self.g[c * 8 + h * 4 + near[h][1], block(h, step, u)]
                    total += rb[sec, h, j, 0, cut] + rb[sec, h, j, 1, cut] + rb[sec, h, j, 2, cut]
                    if step == 0:
                        tt[sec, h, cut] = total
                    else:
                        sb[sec, h, j, cut] = total
                        axis, place = wide[h]
                        remote(
                            sb.at[sec, h, j, cut], rc.at[sec, h, j, cut],
                            {axis: ring(place, step)}, self.sent + 2, self.widened + u,
                        ).start()

        def start_third(self, u):
            cut = parts[u]
            sec = self.sec
            await_received(self.widened + u, rc.at[sec, :, :, cut])
            for h in range(2):
                tt[sec, h, cut] += rc[sec, h, 0, cut] + rc[sec, h, 1, cut] + rc[sec, h, 2, cut]

            @pl.when(seg != sec)
            def _():
                remote(
                    tt.at[sec, :, cut], rd.at[:, cut], {"segment": other},
                    crossing, crossed + u,
                ).start()

        def start_fourth(self, u):
            cut = parts[u]

            @pl.when(seg == self.sec)
            def _():
                await_received(crossed + u, rd.at[:, cut])
                tt[self.sec, :, cut] += rd[:, cut]
                for d in (2, 1, 3):
                    remote(
                        tt.at[self.sec, :, cut], re.at[d - 1, :, cut], {"zh": ring(zh, d)},
                        stacking, stacked + u,
                    ).start()

        def finish(self):
            await_sent(self.sent, self.ra)
            await_sent(self.sent + 1, rb.at[self.sec])
            await_sent(self.sent + 2, sb.at[self.sec])

    crossing, stacking, crossed, stacked = new(sends), new(sends), new(receipts, 2), new(receipts, 2)
    decoder = Sum(1, g1, ra1)
    encoder = Sum(0, g0, ra0)
    decoder.start_pair()
    decoder.start_first(0)
    decoder.start_first(1)

    take_rows(cot_halo)
    build(cext, pch, pcl, 0, 2)
    conv_step(pch, pcl, wct, 0, True)
    take_frames(cot_halo)
    build(cext, pch, pcl, 2, 4)
    for step in (1, 2):
        conv_step(pch, pcl, wct, step, False)
    top, rest = split(acc[...] * slope[...])
    gcat[:, 0:128] = top
    gcat[:, 128:256] = rest
    weight_grad_turned(pth, ptl, g0)
    encoder.start_pair()
    encoder.start_first(0)
    encoder.start_first(1)
    decoder.start_second(0)
    decoder.start_second(1)
    encoder.start_second(0)
    encoder.start_second(1)
    decoder.start_third(0)
    decoder.start_third(1)
    encoder.start_third(0)
    encoder.start_third(1)
    decoder.start_fourth(0)
    decoder.start_fourth(1)
    encoder.start_fourth(0)
    encoder.start_fourth(1)

    spreading, passing, sharing = new(sends), new(sends), new(sends)
    spread, passed, shared = new(receipts, 6), new(receipts, 3), new(receipts)

    def group(h, e):
        return c * 8 + h * 4 + ring(near[h][1], e)

    def pass_on(h, u, d):
        for e in (2, 1, 3):
            piece = full.at[block(h, -d, u), group(h, 0)]
            axis, place = near[h]
            remote(
                uu.at[h, parts[u]] if d == 0 else piece, piece,
                {axis: ring(place, e)}, passing, passed + e - 1,
            ).start()

    for u, cut in enumerate(parts):
        await_received(stacked + u, re.at[:, :, cut])
        for h in range(2):
            total = tt[seg, h, cut] + re[0, h, cut] + re[1, h, cut] + re[2, h, cut]
            uu[h, cut] = total
            full[block(h, 0, u), group(h, 0)] = total
            axis, place = wide[h]
            for d in (2, 1, 3):
                remote(
                    uu.at[h, cut], full.at[block(h, 0, u), group(h, 0)],
                    {axis: ring(place, d)}, spreading, spread + u * 3 + d - 1,
                ).start()
            pass_on(h, u, 0)
    for u, cut in enumerate(parts):
        for d in (1, 3, 2):
            await_received(spread + u * 3 + d - 1, uu.at[:, cut])
            for h in range(2):
                pass_on(h, u, d)
    for e in (0, 1, 3, 2):
        if e > 0:
            await_received(passed + e - 1, full.at[:, 0:2])
        for h in range(2):
            whole = full.at[:, group(h, -e)]
            remote(whole, whole, {"core": 1 - c}, sharing, shared).start()
    await_received(shared, ra0)

    decoder.finish()
    encoder.finish()
    await_sent(crossing, rd)
    await_sent(stacking, re)
    await_sent(spreading, re)
    await_sent(passing, rb.at[0])
    await_sent(sharing, ra0)

    @pl.when(seg == 0)
    def _():
        await_sent(w_sent, wboth.at[0, 0:4 * 288])
        await_sent(w_passed, wboth.at[0, 0:6 * 288])
        for copy, gives, _ in help_rows:
            pl.when(gives)(copy.wait_send)
        help_sum.wait_send()

    @pl.when(seg == 1)
    def _():
        await_sent(w_sent, wboth.at[0, 0:6 * 288])
        await_sent(w_passed, wboth.at[0, 0:4 * 288])

    assert sends[0] <= SENDS and receipts[0] <= RECEIPTS, (sends, receipts)


def write_out(full, out_ref, sems):
    copies = [
        pltpu.make_async_copy(full.at[pl.ds(k * 9, 9)], out_ref.at[pl.ds(k * 9, 9)], sems.at[k])
        for k in range(3)
    ]
    for copy in copies:
        copy.start()
    for copy in copies:
        copy.wait()


def local(video_clips, conv_weights):
    vm = pltpu.VMEM
    ext = vm((4, 6, 32, 128), F32)
    patches = vm((512, 1152), BF16)
    wcat = vm((3456, 256), BF16)
    grads = vm((GROUPS, PAD, 8, 128), F32)
    quarters = vm((2, 4, 4, 7, 8, 128), F32)
    summed = pl.pallas_call(
        kernel,
        out_shape=pltpu.VMEM((PAD, GROUPS, 8, 128), F32),
        in_specs=[pl.BlockSpec(memory_space=pl.ANY)] * 2,
        out_specs=pl.BlockSpec(memory_space=pltpu.VMEM),
        scratch_shapes=[
            ext, ext, ext, vm((2, 6, 32, 128), F32), vm((256, 128), F32), vm((256, 128), F32),
            patches, patches, patches, patches, patches, patches,
            vm((1152, 512), BF16), vm((1152, 512), BF16),
            vm((2, 3456, 128), F32), wcat, wcat, wcat,
            vm((256, 128), F32), vm((256, 128), F32), vm((256, 256), BF16),
            grads, grads, quarters, quarters,
            vm((2, 2, 4, 3, 7, 8, 128), F32),
            vm((2, 2, 3, 7, 8, 128), F32),
            vm((2, 2, 3, 7, 8, 128), F32),
            vm((2, 2, 7, 8, 128), F32),
            vm((2, 7, 8, 128), F32),
            vm((3, 2, 7, 8, 128), F32),
            vm((2, 7, 8, 128), F32),
            pltpu.SemaphoreType.DMA((3,)),
            pltpu.SemaphoreType.DMA((SENDS,)),
            pltpu.SemaphoreType.DMA((RECEIPTS,)),
        ],
        compiler_params=pltpu.CompilerParams(
            collective_id=0, has_side_effects=True, vmem_limit_bytes=60 * 1024 * 1024
        ),
        name="step",
    )(video_clips, conv_weights)
    copied = pl.pallas_call(
        write_out,
        out_shape=jax.ShapeDtypeStruct((TAPS, GROUPS, 8, 128), F32),
        in_specs=[pl.BlockSpec(memory_space=pltpu.VMEM)],
        out_specs=pl.BlockSpec(memory_space=pl.ANY),
        scratch_shapes=[pltpu.SemaphoreType.DMA((3,))],
        name="write_out",
    )(pltpu.with_memory_space_constraint(summed, pltpu.VMEM))
    return copied.reshape(1, TAPS * 128, 128)


def solution(mesh):
    finer = Mesh(
        mesh.devices.reshape(mesh.shape["segment"], mesh.shape["tm"], 4, 4, 2), AXES
    )
    in_specs = (P(None, "tm", ("zh", "y", "core"), None, None), P("segment", None, None))
    return jax.shard_map(
        local, mesh=finer, in_specs=in_specs, out_specs=P("segment", None, None), check_vma=False
    )
```

```python
import jax
import jax.numpy as jnp
from jax import lax
from jax.experimental import pallas as pl
from jax.experimental.pallas import tpu as pltpu
from jax.sharding import Mesh
from jax.sharding import PartitionSpec as P

MESH = pl.DeviceIdType.MESH
AXES = ("segment", "tm", "zh", "y", "core")
F32 = jnp.float32
BF16 = jnp.bfloat16
TAPS = 27
PAD = 28
GROUPS = 16
NEAR_ROWS = 224
FAR_ROWS = 352
EVEN_ROWS = 288
SENDS = 22
RECEIPTS = 79


def kernel(
    vid_ref, w_ref, full,
    vext, lext, cext, uext, mix, part_sum,
    pvh, pvl, plh, pll, pch, pcl, pth, ptl,
    wboth, wc0, wc1, wct,
    acc, slope, gcat,
    g0, g1, ra0, ra1, rb, sb, rc, tt, rd, re, uu,
    local_sem, send_sem, recv_sem,
):
    seg = lax.axis_index("segment")
    x = lax.axis_index("tm")
    zh = lax.axis_index("zh")
    y = lax.axis_index("y")
    c = lax.axis_index("core")
    s = zh * 8 + y * 2 + c
    sends, receipts = [0], [0]

    def new(counter, count=1):
        counter[0] += count
        return counter[0] - count

    def spot(index, **others):
        index = lax.rem(index + 32, 32)
        return {"zh": index // 8, "y": lax.rem(index // 2, 4), "core": lax.rem(index, 2), **others}

    def ring(value, step):
        return lax.rem(value + step + 4, 4)

    other = 1 - seg
    link_b = ring(zh, 2 * seg - 1)

    def remote(src, dst, device, sent=None, received=None):
        sent = new(sends) if sent is None else sent
        received = new(receipts) if received is None else received
        return pltpu.make_async_remote_copy(
            src_ref=src,
            dst_ref=dst,
            send_sem=send_sem.at[sent],
            recv_sem=recv_sem.at[received],
            device_id=device,
            device_id_type=MESH,
        )

    def await_sent(slot, like):
        pltpu.make_async_copy(like, like, send_sem.at[slot]).wait()

    def await_received(slot, like):
        pltpu.make_async_copy(like, like, recv_sem.at[slot]).wait()

    own_w = pltpu.make_async_copy(w_ref.at[0], wboth.at[seg], local_sem.at[0])
    own_v = pltpu.make_async_copy(vid_ref.at[seg], vext.at[2:4, 1:5], local_sem.at[1])
    helped = pltpu.make_async_copy(vid_ref.at[1], uext.at[:, 1:5], local_sem.at[2])
    pl.when(seg == 0)(helped.start)
    own_v.start()
    own_w.start()
    for rim, line in ((s == 0, 0), (s == 31, 5)):
        @pl.when(rim)
        def _():
            uext[:, line] = jnp.zeros((2, 32, 128), F32)

    for ext, edge, far in ((vext, x == 0, 0), (lext, x == 0, 0), (cext, x == 3, 2)):
        @pl.when(edge)
        def _():
            ext[far:far + 2] = jnp.zeros((2, 6, 32, 128), F32)

        for rim, line in ((s == 0, 0), (s == 31, 5)):
            @pl.when(rim)
            def _():
                ext[:, line] = jnp.zeros((4, 32, 128), F32)

    for g in (g0, g1):
        g[:, TAPS] = jnp.zeros((GROUPS, 8, 128), F32)

    barrier = pltpu.get_barrier_semaphore()
    greet = [{"tm": ring(x, d)} for d in (1, 2, 3)]
    greet += [{"y": ring(y, d)} for d in (1, 2, 3)]
    greet += [{"zh": ring(zh, d)} for d in (1, 2, 3)]
    greet += [{"core": 1 - c}, {"segment": other}, {"segment": other, "zh": link_b}]
    greet += [spot(s + 1), spot(s - 1)]
    greet += [spot(s + dy, tm=ring(x, dx)) for dy in (1, -1) for dx in (1, -1)]
    for device in greet:
        pl.semaphore_signal(barrier, inc=1, device_id=device, device_id_type=MESH)
    pl.semaphore_wait(barrier, len(greet))

    shares = ((NEAR_ROWS, FAR_ROWS), (EVEN_ROWS, EVEN_ROWS))

    def quarter(sender, step, part, core):
        count = shares[sender][part]
        return pl.ds(step * 1152 + part * 2 * shares[sender][0] + core * count, count)

    w_sent, w_passed = new(sends), new(sends)
    w_got, w_shared = new(receipts, 3), new(receipts, 3)

    def send_weights(sender, step, part):
        rows = quarter(sender, step, part, c)
        device = {"segment": other} if part == 0 else {"segment": other, "zh": link_b}
        remote(w_ref.at[0, rows], wboth.at[seg, rows], device, w_sent, w_got + step).start()

    def relay_weights(sender, step, part):
        rows = quarter(sender, step, part, c)
        remote(
            wboth.at[other, rows], wboth.at[other, rows], {"core": 1 - c},
            w_passed, w_shared + step,
        ).start()

    halo_sent = new(sends, 6)

    def halo(ext, own, far, shift):
        ahead = {"tm": ring(x, shift)}
        sends_x = (x < 3) if shift == 1 else (x > 0)
        gets_x = (x > 0) if shift == 1 else (x < 3)
        frames, beyond = slice(own, own + 2), slice(far, far + 2)
        inner, outer = 4 - 3 * c, 1 + 3 * c
        up, down = (s < 31), (s > 0)
        edge = jnp.logical_or(jnp.logical_and(c == 1, up), jnp.logical_and(c == 0, down))
        corner = remote(
            ext.at[frames, outer], ext.at[beyond, 5 - 5 * c], spot(s + 2 * c - 1, **ahead),
            halo_sent,
        )
        rest = pl.ds(1 + c, 3)
        moves = {
            "first": (remote(ext.at[frames, inner], ext.at[beyond, inner], ahead, halo_sent + 1), sends_x, gets_x),
            "next": (remote(ext.at[frames, 4], ext.at[frames, 0], spot(s + 1), halo_sent + 2), up, down),
            "last": (remote(ext.at[frames, 1], ext.at[frames, 5], spot(s - 1), halo_sent + 3), down, up),
            "corner": (corner, jnp.logical_and(edge, sends_x), jnp.logical_and(edge, gets_x)),
            "rest": (remote(ext.at[frames, rest], ext.at[beyond, rest], ahead, halo_sent + 4), sends_x, gets_x),
            "pass": (
                remote(ext.at[beyond, inner], ext.at[beyond, 5 * c], {"core": 1 - c}, halo_sent + 5),
                gets_x, gets_x,
            ),
        }
        return moves

    def start_halo(moves):
        for name, (copy, gives, _) in moves.items():
            if name != "pass":
                pl.when(gives)(copy.start)

    def take_rows(moves):
        for name in ("next", "last"):
            copy, _, gets = moves[name]
            pl.when(gets)(copy.wait_recv)
        first, _, gets = moves["first"]

        @pl.when(gets)
        def _():
            first.wait_recv()
            moves["pass"][0].start()

    def take_frames(moves):
        for name in ("corner", "rest", "pass"):
            copy, _, gets = moves[name]
            pl.when(gets)(copy.wait_recv)
        for copy, gives, _ in moves.values():
            pl.when(gives)(copy.wait_send)

    help_rows = (
        (remote(uext.at[:, 4], uext.at[:, 0], spot(s + 1)), s < 31, s > 0),
        (remote(uext.at[:, 1], uext.at[:, 5], spot(s - 1)), s > 0, s < 31),
    )
    help_sum = remote(mix, part_sum, {"segment": other})

    @pl.when(seg == 0)
    def _():
        helped.wait()
        for copy, gives, _ in help_rows:
            pl.when(gives)(copy.start)

    own_v.wait()
    video_halo = halo(vext, 2, 0, 1)
    start_halo(video_halo)
    for sender, steps in ((0, (1, 0)), (1, (2, 1, 0))):
        @pl.when(seg == sender)
        def _():
            for step in steps:
                for part in range(2):
                    send_weights(sender, step, part)

    column = lax.broadcasted_iota(jnp.int32, (32, 128), 0)

    def build(ext, high, low, start, stop):
        @pl.loop(start, stop)
        def _(frame):
            base = pl.multiple_of(frame * 128, 128)
            for line in range(6):
                value = ext[frame, line]
                for e in range(3):
                    if e == 0:
                        moved = jnp.where(column == 0, 0.0, pltpu.roll(value, 1, 0))
                    elif e == 2:
                        moved = jnp.where(column == 31, 0.0, pltpu.roll(value, 31, 0))
                    else:
                        moved = value
                    top = moved.astype(BF16)
                    rest = (moved - top.astype(F32)).astype(BF16)
                    for b in range(3):
                        r = line - b
                        if 0 <= r < 4:
                            lanes = slice((b * 3 + e) * 128, (b * 3 + e + 1) * 128)
                            high[pl.ds(base + r * 32, 32), lanes] = top
                            low[pl.ds(base + r * 32, 32), lanes] = rest

    def split(value):
        top = value.astype(BF16)
        return top, (value - top.astype(F32)).astype(BF16)

    def product(high, low, weight, first, step):
        rows = pl.ds(first * 128, 256)
        lines = pl.ds(step * 1152, 1152)
        both = jnp.dot(high[rows, :], weight[lines, :], preferred_element_type=F32)
        rest = jnp.dot(low[rows, :], weight[lines, 0:128], preferred_element_type=F32)
        return both[:, 0:128] + both[:, 128:256] + rest

    def conv_step(high, low, weight, step, first):
        total = product(high, low, weight, step, step)
        if first:
            acc[...] = total
        else:
            acc[...] += total

    def place_grad(g, step, both, rest):
        total = both[:, 0:128] + both[:, 128:256] + rest
        for k in range(9):
            g[:, step * 9 + k] = total[k * 128:(k + 1) * 128].reshape(GROUPS, 8, 128)

    def weight_grad(high, low, g):
        @pl.loop(0, 3)
        def _(step):
            rows = pl.ds(pl.multiple_of(step * 128, 128), 256)
            dims = (((0,), (0,)), ((), ()))
            both = lax.dot_general(high[rows, :], gcat[...], dims, preferred_element_type=F32)
            rest = lax.dot_general(
                low[rows, :], gcat[:, 0:128], dims, preferred_element_type=F32
            )
            place_grad(g, step, both, rest)

    def weight_grad_turned(high, low, g):
        @pl.loop(0, 3)
        def _(step):
            cells = pl.ds(pl.multiple_of(step * 128, 128), 256)
            both = jnp.dot(high[:, cells], gcat[...], preferred_element_type=F32)
            rest = jnp.dot(low[:, cells], gcat[:, 0:128], preferred_element_type=F32)
            place_grad(g, step, both, rest)

    def prepare(start, stop, section):
        @pl.loop(start, stop)
        def _(tap):
            rows = pl.ds(pl.multiple_of(tap * 128, 128), 128)
            value = wboth[section, rows]
            places = [(value, (wc0, wc1)[section], rows)]
            if section == 1:
                flipped = pl.ds(pl.multiple_of((TAPS - 1 - tap) * 128, 128), 128)
                places.append((value.T, wct, flipped))
            for part, ref, place in places:
                top, rest = split(part)
                ref[place, 0:128] = top
                ref[place, 128:256] = rest

    own_w.wait()
    pl.when(seg == 0)(lambda: prepare(0, TAPS, 0))
    pl.when(seg == 1)(lambda: prepare(0, TAPS, 1))

    @pl.when(seg == 0)
    def _():
        for copy, _, gets in help_rows:
            pl.when(gets)(copy.wait_recv)
        build(uext, plh, pll, 0, 2)
        mix[...] = product(plh, pll, wc0, 0, 2)
        help_sum.start()

    take_rows(video_halo)
    take_frames(video_halo)
    build(vext, pvh, pvl, 0, 4)

    latent_halo = halo(lext, 2, 0, 1)

    def encode():
        hidden = acc[...]
        sigmoid = 1.0 / (1.0 + jnp.exp(-hidden))
        slope[...] = sigmoid * (1.0 + hidden * (1.0 - sigmoid))
        lext[2:4, 1:5] = (hidden / (1.0 + jnp.exp(-hidden))).reshape(2, 4, 32, 128)
        start_halo(latent_halo)

    @pl.when(seg == 0)
    def _():
        for step in range(3):
            conv_step(pvh, pvl, wc0, step, step == 0)
        encode()

    @pl.loop(0, 9)
    def _(k):
        lanes = pl.ds(pl.multiple_of(k * 128, 128), 128)
        for source, turned in ((pvh, pth), (pvl, ptl)):
            turned[lanes, :] = source[:, lanes].T

    def take(sender, step):
        await_received(w_got + step, wboth.at[other, 0:576])
        for part in range(2):
            relay_weights(sender, step, part)
        await_received(w_shared + step, wboth.at[other, 0:576])

    @pl.when(seg == 0)
    def _():
        for step in (2, 1, 0):
            take(1, step)
            prepare(step * 9, step * 9 + 9, 1)

    @pl.when(seg == 1)
    def _():
        for step in (1, 0):
            take(0, step)
            prepare(step * 9, step * 9 + 9, 0)
            conv_step(pvh, pvl, wc0, step, step == 1)
        help_sum.wait_recv()
        acc[...] += part_sum[...]
        encode()

    take_rows(latent_halo)
    build(lext, plh, pll, 2, 4)
    conv_step(plh, pll, wc1, 2, True)
    take_frames(latent_halo)
    build(lext, plh, pll, 0, 2)
    for step in (1, 0):
        conv_step(plh, pll, wc1, step, False)
    cot = (acc[...] - vext[2:4, 1:5].reshape(256, 128)) * (65536.0 ** -0.5)
    cext[0:2, 1:5] = cot.reshape(2, 4, 32, 128)
    cot_halo = halo(cext, 0, 2, -1)
    start_halo(cot_halo)
    top, rest = split(cot)
    gcat[:, 0:128] = top
    gcat[:, 128:256] = rest
    weight_grad(plh, pll, g1)

    near = (("tm", x), ("y", y))
    wide = (("y", y), ("tm", x))
    order = (2, 1, 3, 0)
    parts = (slice(0, 4), slice(4, 7))

    def block(h, step, u):
        cut = parts[u]
        return pl.ds(ring(wide[h][1], step) * 7 + cut.start, cut.stop - cut.start)

    class Sum:
        def __init__(self, sec, g, ra):
            self.sec, self.g, self.ra = sec, g, ra
            self.sent = new(sends, 3)
            self.paired = new(receipts, 8)
            self.summed = new(receipts, 8)
            self.widened = new(receipts, 2)

        def start_pair(self):
            for u in range(2):
                for j, step in enumerate(order):
                    for h in range(2):
                        rows = pl.ds((1 - c) * 8 + h * 4, 4)
                        remote(
                            self.g.at[rows, block(h, step, u)],
                            self.ra.at[h, j, :, parts[u]],
                            {"core": 1 - c}, self.sent, self.paired + u * 4 + j,
                        ).start()

        def start_first(self, u):
            cut = parts[u]
            for j, step in enumerate(order):
                await_received(self.paired + u * 4 + j, self.ra.at[:, j, :, cut])
                for h in range(2):
                    taps = block(h, step, u)
                    base = c * 8 + h * 4
                    self.g[pl.ds(base, 4), taps] += self.ra[h, j, :, cut]
                    axis, place = near[h]
                    for d in (2, 1, 3):
                        peer = ring(place, d)
                        remote(
                            self.g.at[base + peer, taps],
                            rb.at[self.sec, h, j, d - 1, cut],
                            {axis: peer}, self.sent + 1, self.summed + u * 4 + j,
                        ).start()

        def start_second(self, u):
            cut = parts[u]
            sec = self.sec
            for j, step in enumerate(order):
                await_received(self.summed + u * 4 + j, rb.at[sec, :, j, :, cut])
                for h in range(2):
                    total = self.g[c * 8 + h * 4 + near[h][1], block(h, step, u)]
                    total += rb[sec, h, j, 0, cut] + rb[sec, h, j, 1, cut] + rb[sec, h, j, 2, cut]
                    if step == 0:
                        tt[sec, h, cut] = total
                    else:
                        sb[sec, h, j, cut] = total
                        axis, place = wide[h]
                        remote(
                            sb.at[sec, h, j, cut], rc.at[sec, h, j, cut],
                            {axis: ring(place, step)}, self.sent + 2, self.widened + u,
                        ).start()

        def start_third(self, u):
            cut = parts[u]
            sec = self.sec
            await_received(self.widened + u, rc.at[sec, :, :, cut])
            for h in range(2):
                tt[sec, h, cut] += rc[sec, h, 0, cut] + rc[sec, h, 1, cut] + rc[sec, h, 2, cut]

            @pl.when(seg != sec)
            def _():
                remote(
                    tt.at[sec, :, cut], rd.at[:, cut], {"segment": other},
                    crossing, crossed + u,
                ).start()

        def start_fourth(self, u):
            cut = parts[u]

            @pl.when(seg == self.sec)
            def _():
                await_received(crossed + u, rd.at[:, cut])
                tt[self.sec, :, cut] += rd[:, cut]
                for d in (2, 1, 3):
                    remote(
                        tt.at[self.sec, :, cut], re.at[d - 1, :, cut], {"zh": ring(zh, d)},
                        stacking, stacked + u,
                    ).start()

        def finish(self):
            await_sent(self.sent, self.ra)
            await_sent(self.sent + 1, rb.at[self.sec])
            await_sent(self.sent + 2, sb.at[self.sec])

    crossing, stacking, crossed, stacked = new(sends), new(sends), new(receipts, 2), new(receipts, 2)
    decoder = Sum(1, g1, ra1)
    encoder = Sum(0, g0, ra0)
    decoder.start_pair()
    decoder.start_first(0)
    decoder.start_first(1)

    take_rows(cot_halo)
    build(cext, pch, pcl, 0, 2)
    conv_step(pch, pcl, wct, 0, True)
    take_frames(cot_halo)
    build(cext, pch, pcl, 2, 4)
    for step in (1, 2):
        conv_step(pch, pcl, wct, step, False)
    top, rest = split(acc[...] * slope[...])
    gcat[:, 0:128] = top
    gcat[:, 128:256] = rest
    weight_grad_turned(pth, ptl, g0)
    encoder.start_pair()
    decoder.start_second(0)
    encoder.start_first(0)
    decoder.start_second(1)
    encoder.start_first(1)
    decoder.start_third(0)
    encoder.start_second(0)
    decoder.start_third(1)
    encoder.start_second(1)
    encoder.start_third(0)
    encoder.start_third(1)
    decoder.start_fourth(0)
    decoder.start_fourth(1)
    encoder.start_fourth(0)
    encoder.start_fourth(1)

    spreading, passing, sharing = new(sends), new(sends), new(sends)
    spread, passed, shared = new(receipts, 6), new(receipts, 3), new(receipts)

    def group(h, e):
        return c * 8 + h * 4 + ring(near[h][1], e)

    def pass_on(h, u, d):
        for e in (2, 1, 3):
            piece = full.at[block(h, -d, u), group(h, 0)]
            axis, place = near[h]
            remote(
                uu.at[h, parts[u]] if d == 0 else piece, piece,
                {axis: ring(place, e)}, passing, passed + e - 1,
            ).start()

    for u, cut in enumerate(parts):
        await_received(stacked + u, re.at[:, :, cut])
        for h in range(2):
            total = tt[seg, h, cut] + re[0, h, cut] + re[1, h, cut] + re[2, h, cut]
            uu[h, cut] = total
            axis, place = wide[h]
            for d in (2, 1, 3):
                remote(
                    uu.at[h, cut], full.at[block(h, 0, u), group(h, 0)],
                    {axis: ring(place, d)}, spreading, spread + u * 3 + d - 1,
                ).start()
    for u, cut in enumerate(parts):
        for h in range(2):
            pass_on(h, u, 0)
            full[block(h, 0, u), group(h, 0)] = uu[h, cut]
    for u, cut in enumerate(parts):
        for d in (1, 3, 2):
            await_received(spread + u * 3 + d - 1, uu.at[:, cut])
            for h in range(2):
                pass_on(h, u, d)
    for e in (0, 1, 3, 2):
        if e > 0:
            await_received(passed + e - 1, full.at[:, 0:2])
        for h in range(2):
            whole = full.at[:, group(h, -e)]
            remote(whole, whole, {"core": 1 - c}, sharing, shared).start()
    await_received(shared, ra0)

    decoder.finish()
    encoder.finish()
    await_sent(crossing, rd)
    await_sent(stacking, re)
    await_sent(spreading, re)
    await_sent(passing, rb.at[0])
    await_sent(sharing, ra0)

    @pl.when(seg == 0)
    def _():
        await_sent(w_sent, wboth.at[0, 0:4 * 288])
        await_sent(w_passed, wboth.at[0, 0:6 * 288])
        for copy, gives, _ in help_rows:
            pl.when(gives)(copy.wait_send)
        help_sum.wait_send()

    @pl.when(seg == 1)
    def _():
        await_sent(w_sent, wboth.at[0, 0:6 * 288])
        await_sent(w_passed, wboth.at[0, 0:4 * 288])

    assert sends[0] <= SENDS and receipts[0] <= RECEIPTS, (sends, receipts)


def write_out(full, out_ref, sems):
    copies = [
        pltpu.make_async_copy(full.at[pl.ds(k * 3, 3)], out_ref.at[pl.ds(k * 3, 3)], sems.at[k])
        for k in range(9)
    ]
    for copy in copies:
        copy.start()
    for copy in copies:
        copy.wait()


def local(video_clips, conv_weights):
    vm = pltpu.VMEM
    ext = vm((4, 6, 32, 128), F32)
    patches = vm((512, 1152), BF16)
    wcat = vm((3456, 256), BF16)
    grads = vm((GROUPS, PAD, 8, 128), F32)
    quarters = vm((2, 4, 4, 7, 8, 128), F32)
    summed = pl.pallas_call(
        kernel,
        out_shape=pltpu.VMEM((PAD, GROUPS, 8, 128), F32),
        in_specs=[pl.BlockSpec(memory_space=pl.ANY)] * 2,
        out_specs=pl.BlockSpec(memory_space=pltpu.VMEM),
        scratch_shapes=[
            ext, ext, ext, vm((2, 6, 32, 128), F32), vm((256, 128), F32), vm((256, 128), F32),
            patches, patches, patches, patches, patches, patches,
            vm((1152, 512), BF16), vm((1152, 512), BF16),
            vm((2, 3456, 128), F32), wcat, wcat, wcat,
            vm((256, 128), F32), vm((256, 128), F32), vm((256, 256), BF16),
            grads, grads, quarters, quarters,
            vm((2, 2, 4, 3, 7, 8, 128), F32),
            vm((2, 2, 3, 7, 8, 128), F32),
            vm((2, 2, 3, 7, 8, 128), F32),
            vm((2, 2, 7, 8, 128), F32),
            vm((2, 7, 8, 128), F32),
            vm((3, 2, 7, 8, 128), F32),
            vm((2, 7, 8, 128), F32),
            pltpu.SemaphoreType.DMA((3,)),
            pltpu.SemaphoreType.DMA((SENDS,)),
            pltpu.SemaphoreType.DMA((RECEIPTS,)),
        ],
        compiler_params=pltpu.CompilerParams(
            collective_id=0, has_side_effects=True, vmem_limit_bytes=60 * 1024 * 1024
        ),
        name="step",
    )(video_clips, conv_weights)
    copied = pl.pallas_call(
        write_out,
        out_shape=jax.ShapeDtypeStruct((TAPS, GROUPS, 8, 128), F32),
        in_specs=[pl.BlockSpec(memory_space=pltpu.VMEM)],
        out_specs=pl.BlockSpec(memory_space=pl.ANY),
        scratch_shapes=[pltpu.SemaphoreType.DMA((9,))],
        name="write_out",
    )(pltpu.with_memory_space_constraint(summed, pltpu.VMEM))
    return copied.reshape(1, TAPS * 128, 128)


def solution(mesh):
    finer = Mesh(
        mesh.devices.reshape(mesh.shape["segment"], mesh.shape["tm"], 4, 4, 2), AXES
    )
    in_specs = (P(None, "tm", ("zh", "y", "core"), None, None), P("segment", None, None))
    return jax.shard_map(
        local, mesh=finer, in_specs=in_specs, out_specs=P("segment", None, None), check_vma=False
    )
```

```python
import jax
import jax.numpy as jnp
from jax import lax
from jax.experimental import pallas as pl
from jax.experimental.pallas import tpu as pltpu
from jax.sharding import Mesh
from jax.sharding import PartitionSpec as P

MESH = pl.DeviceIdType.MESH
AXES = ("segment", "tm", "zh", "y", "core")
F32 = jnp.float32
BF16 = jnp.bfloat16
TAPS = 27
PAD = 28
GROUPS = 16
NEAR_ROWS = 224
FAR_ROWS = 352
EVEN_ROWS = 288
SENDS = 22
RECEIPTS = 79


def kernel(
    vid_ref, w_ref, full,
    vext, lext, cext, uext, mix, part_sum,
    pvh, pvl, plh, pll, pch, pcl, pth, ptl,
    wboth, wc0, wc1, wct,
    acc, slope, gcat,
    g0, g1, ra0, ra1, rb, sb, rc, tt, rd, re, uu,
    local_sem, send_sem, recv_sem,
):
    seg = lax.axis_index("segment")
    x = lax.axis_index("tm")
    zh = lax.axis_index("zh")
    y = lax.axis_index("y")
    c = lax.axis_index("core")
    s = zh * 8 + y * 2 + c
    sends, receipts = [0], [0]

    def new(counter, count=1):
        counter[0] += count
        return counter[0] - count

    def spot(index, **others):
        index = lax.rem(index + 32, 32)
        return {"zh": index // 8, "y": lax.rem(index // 2, 4), "core": lax.rem(index, 2), **others}

    def ring(value, step):
        return lax.rem(value + step + 4, 4)

    other = 1 - seg
    link_b = ring(zh, 2 * seg - 1)

    def remote(src, dst, device, sent=None, received=None):
        sent = new(sends) if sent is None else sent
        received = new(receipts) if received is None else received
        return pltpu.make_async_remote_copy(
            src_ref=src,
            dst_ref=dst,
            send_sem=send_sem.at[sent],
            recv_sem=recv_sem.at[received],
            device_id=device,
            device_id_type=MESH,
        )

    def await_sent(slot, like):
        pltpu.make_async_copy(like, like, send_sem.at[slot]).wait()

    def await_received(slot, like):
        pltpu.make_async_copy(like, like, recv_sem.at[slot]).wait()

    own_w = pltpu.make_async_copy(w_ref.at[0], wboth.at[seg], local_sem.at[0])
    own_v = pltpu.make_async_copy(vid_ref.at[seg], vext.at[2:4, 1:5], local_sem.at[1])
    helped = pltpu.make_async_copy(vid_ref.at[1], uext.at[:, 1:5], local_sem.at[2])
    pl.when(seg == 0)(helped.start)
    own_v.start()
    own_w.start()
    for rim, line in ((s == 0, 0), (s == 31, 5)):
        @pl.when(rim)
        def _():
            uext[:, line] = jnp.zeros((2, 32, 128), F32)

    for ext, edge, far in ((vext, x == 0, 0), (lext, x == 0, 0), (cext, x == 3, 2)):
        @pl.when(edge)
        def _():
            ext[far:far + 2] = jnp.zeros((2, 6, 32, 128), F32)

        for rim, line in ((s == 0, 0), (s == 31, 5)):
            @pl.when(rim)
            def _():
                ext[:, line] = jnp.zeros((4, 32, 128), F32)

    for g in (g0, g1):
        g[:, TAPS] = jnp.zeros((GROUPS, 8, 128), F32)

    barrier = pltpu.get_barrier_semaphore()
    greet = [{"tm": ring(x, d)} for d in (1, 2, 3)]
    greet += [{"y": ring(y, d)} for d in (1, 2, 3)]
    greet += [{"zh": ring(zh, d)} for d in (1, 2, 3)]
    greet += [{"core": 1 - c}, {"segment": other}, {"segment": other, "zh": link_b}]
    greet += [spot(s + 1), spot(s - 1)]
    greet += [spot(s + dy, tm=ring(x, dx)) for dy in (1, -1) for dx in (1, -1)]
    for device in greet:
        pl.semaphore_signal(barrier, inc=1, device_id=device, device_id_type=MESH)
    pl.semaphore_wait(barrier, len(greet))

    shares = ((NEAR_ROWS, FAR_ROWS), (EVEN_ROWS, EVEN_ROWS))

    def quarter(sender, step, part, core):
        count = shares[sender][part]
        return pl.ds(step * 1152 + part * 2 * shares[sender][0] + core * count, count)

    w_sent, w_passed = new(sends), new(sends)
    w_got, w_shared = new(receipts, 3), new(receipts, 3)

    def send_weights(sender, step, part):
        rows = quarter(sender, step, part, c)
        device = {"segment": other} if part == 0 else {"segment": other, "zh": link_b}
        remote(w_ref.at[0, rows], wboth.at[seg, rows], device, w_sent, w_got + step).start()

    def relay_weights(sender, step, part):
        rows = quarter(sender, step, part, c)
        remote(
            wboth.at[other, rows], wboth.at[other, rows], {"core": 1 - c},
            w_passed, w_shared + step,
        ).start()

    halo_sent = new(sends, 6)

    def halo(ext, own, far, shift):
        ahead = {"tm": ring(x, shift)}
        sends_x = (x < 3) if shift == 1 else (x > 0)
        gets_x = (x > 0) if shift == 1 else (x < 3)
        frames, beyond = slice(own, own + 2), slice(far, far + 2)
        inner, outer = 4 - 3 * c, 1 + 3 * c
        up, down = (s < 31), (s > 0)
        edge = jnp.logical_or(jnp.logical_and(c == 1, up), jnp.logical_and(c == 0, down))
        corner = remote(
            ext.at[frames, outer], ext.at[beyond, 5 - 5 * c], spot(s + 2 * c - 1, **ahead),
            halo_sent,
        )
        rest = pl.ds(1 + c, 3)
        moves = {
            "first": (remote(ext.at[frames, inner], ext.at[beyond, inner], ahead, halo_sent + 1), sends_x, gets_x),
            "next": (remote(ext.at[frames, 4], ext.at[frames, 0], spot(s + 1), halo_sent + 2), up, down),
            "last": (remote(ext.at[frames, 1], ext.at[frames, 5], spot(s - 1), halo_sent + 3), down, up),
            "corner": (corner, jnp.logical_and(edge, sends_x), jnp.logical_and(edge, gets_x)),
            "rest": (remote(ext.at[frames, rest], ext.at[beyond, rest], ahead, halo_sent + 4), sends_x, gets_x),
            "pass": (
                remote(ext.at[beyond, inner], ext.at[beyond, 5 * c], {"core": 1 - c}, halo_sent + 5),
                gets_x, gets_x,
            ),
        }
        return moves

    def start_halo(moves):
        for name, (copy, gives, _) in moves.items():
            if name != "pass":
                pl.when(gives)(copy.start)

    def take_rows(moves):
        first, _, gets = moves["first"]

        @pl.when(gets)
        def _():
            first.wait_recv()
            moves["pass"][0].start()

        for name in ("next", "last"):
            copy, _, gets = moves[name]
            pl.when(gets)(copy.wait_recv)

    def take_frames(moves):
        for name in ("corner", "rest", "pass"):
            copy, _, gets = moves[name]
            pl.when(gets)(copy.wait_recv)
        for copy, gives, _ in moves.values():
            pl.when(gives)(copy.wait_send)

    help_rows = (
        (remote(uext.at[:, 4], uext.at[:, 0], spot(s + 1)), s < 31, s > 0),
        (remote(uext.at[:, 1], uext.at[:, 5], spot(s - 1)), s > 0, s < 31),
    )
    help_sum = remote(mix, part_sum, {"segment": other})

    @pl.when(seg == 0)
    def _():
        helped.wait()
        for copy, gives, _ in help_rows:
            pl.when(gives)(copy.start)

    own_v.wait()
    video_halo = halo(vext, 2, 0, 1)
    start_halo(video_halo)
    for sender, steps in ((0, (1, 0)), (1, (2, 1, 0))):
        @pl.when(seg == sender)
        def _():
            for step in steps:
                for part in range(2):
                    send_weights(sender, step, part)

    column = lax.broadcasted_iota(jnp.int32, (32, 128), 0)

    def build(ext, high, low, start, stop):
        @pl.loop(start, stop)
        def _(frame):
            base = pl.multiple_of(frame * 128, 128)
            for line in range(6):
                value = ext[frame, line]
                for e in range(3):
                    if e == 0:
                        moved = jnp.where(column == 0, 0.0, pltpu.roll(value, 1, 0))
                    elif e == 2:
                        moved = jnp.where(column == 31, 0.0, pltpu.roll(value, 31, 0))
                    else:
                        moved = value
                    top = moved.astype(BF16)
                    rest = (moved - top.astype(F32)).astype(BF16)
                    for b in range(3):
                        r = line - b
                        if 0 <= r < 4:
                            lanes = slice((b * 3 + e) * 128, (b * 3 + e + 1) * 128)
                            high[pl.ds(base + r * 32, 32), lanes] = top
                            low[pl.ds(base + r * 32, 32), lanes] = rest

    def split(value):
        top = value.astype(BF16)
        return top, (value - top.astype(F32)).astype(BF16)

    def product(high, low, weight, first, step):
        rows = pl.ds(first * 128, 256)
        lines = pl.ds(step * 1152, 1152)
        both = jnp.dot(high[rows, :], weight[lines, :], preferred_element_type=F32)
        rest = jnp.dot(low[rows, :], weight[lines, 0:128], preferred_element_type=F32)
        return both[:, 0:128] + both[:, 128:256] + rest

    def conv_step(high, low, weight, step, first):
        total = product(high, low, weight, step, step)
        if first:
            acc[...] = total
        else:
            acc[...] += total

    def place_grad(g, step, both, rest):
        total = both[:, 0:128] + both[:, 128:256] + rest
        for k in range(9):
            g[:, step * 9 + k] = total[k * 128:(k + 1) * 128].reshape(GROUPS, 8, 128)

    def weight_grad(high, low, g):
        @pl.loop(0, 3)
        def _(step):
            rows = pl.ds(pl.multiple_of(step * 128, 128), 256)
            dims = (((0,), (0,)), ((), ()))
            both = lax.dot_general(high[rows, :], gcat[...], dims, preferred_element_type=F32)
            rest = lax.dot_general(
                low[rows, :], gcat[:, 0:128], dims, preferred_element_type=F32
            )
            place_grad(g, step, both, rest)

    def weight_grad_turned(high, low, g):
        @pl.loop(0, 3)
        def _(step):
            cells = pl.ds(pl.multiple_of(step * 128, 128), 256)
            both = jnp.dot(high[:, cells], gcat[...], preferred_element_type=F32)
            rest = jnp.dot(low[:, cells], gcat[:, 0:128], preferred_element_type=F32)
            place_grad(g, step, both, rest)

    def prepare(start, stop, section):
        @pl.loop(start, stop)
        def _(tap):
            rows = pl.ds(pl.multiple_of(tap * 128, 128), 128)
            value = wboth[section, rows]
            places = [(value, (wc0, wc1)[section], rows)]
            if section == 1:
                flipped = pl.ds(pl.multiple_of((TAPS - 1 - tap) * 128, 128), 128)
                places.append((value.T, wct, flipped))
            for part, ref, place in places:
                top, rest = split(part)
                ref[place, 0:128] = top
                ref[place, 128:256] = rest

    own_w.wait()
    pl.when(seg == 0)(lambda: prepare(0, TAPS, 0))
    pl.when(seg == 1)(lambda: prepare(0, TAPS, 1))

    @pl.when(seg == 0)
    def _():
        for copy, _, gets in help_rows:
            pl.when(gets)(copy.wait_recv)
        build(uext, plh, pll, 0, 2)
        mix[...] = product(plh, pll, wc0, 0, 2)
        help_sum.start()

    take_rows(video_halo)
    take_frames(video_halo)
    build(vext, pvh, pvl, 0, 4)

    latent_halo = halo(lext, 2, 0, 1)

    def encode():
        hidden = acc[...]
        sigmoid = 1.0 / (1.0 + jnp.exp(-hidden))
        slope[...] = sigmoid * (1.0 + hidden * (1.0 - sigmoid))
        lext[2:4, 1:5] = (hidden / (1.0 + jnp.exp(-hidden))).reshape(2, 4, 32, 128)
        start_halo(latent_halo)

    @pl.when(seg == 0)
    def _():
        for step in range(3):
            conv_step(pvh, pvl, wc0, step, step == 0)
        encode()

    @pl.loop(0, 9)
    def _(k):
        lanes = pl.ds(pl.multiple_of(k * 128, 128), 128)
        for source, turned in ((pvh, pth), (pvl, ptl)):
            turned[lanes, :] = source[:, lanes].T

    def take(sender, step):
        await_received(w_got + step, wboth.at[other, 0:576])
        for part in range(2):
            relay_weights(sender, step, part)
        await_received(w_shared + step, wboth.at[other, 0:576])

    @pl.when(seg == 0)
    def _():
        for step in (2, 1, 0):
            take(1, step)
            prepare(step * 9, step * 9 + 9, 1)

    @pl.when(seg == 1)
    def _():
        for step in (1, 0):
            take(0, step)
            prepare(step * 9, step * 9 + 9, 0)
            conv_step(pvh, pvl, wc0, step, step == 1)
        help_sum.wait_recv()
        acc[...] += part_sum[...]
        encode()

    take_rows(latent_halo)
    build(lext, plh, pll, 2, 4)
    conv_step(plh, pll, wc1, 2, True)
    take_frames(latent_halo)
    build(lext, plh, pll, 0, 2)
    for step in (1, 0):
        conv_step(plh, pll, wc1, step, False)
    cot = (acc[...] - vext[2:4, 1:5].reshape(256, 128)) * (65536.0 ** -0.5)
    cext[0:2, 1:5] = cot.reshape(2, 4, 32, 128)
    cot_halo = halo(cext, 0, 2, -1)
    start_halo(cot_halo)
    top, rest = split(cot)
    gcat[:, 0:128] = top
    gcat[:, 128:256] = rest
    weight_grad(plh, pll, g1)

    near = (("tm", x), ("y", y))
    wide = (("y", y), ("tm", x))
    order = (2, 1, 3, 0)
    parts = (slice(0, 4), slice(4, 7))

    def block(h, step, u):
        cut = parts[u]
        return pl.ds(ring(wide[h][1], step) * 7 + cut.start, cut.stop - cut.start)

    class Sum:
        def __init__(self, sec, g, ra):
            self.sec, self.g, self.ra = sec, g, ra
            self.sent = new(sends, 3)
            self.paired = new(receipts, 8)
            self.summed = new(receipts, 8)
            self.widened = new(receipts, 2)

        def start_pair(self):
            for u in range(2):
                for j, step in enumerate(order):
                    for h in range(2):
                        rows = pl.ds((1 - c) * 8 + h * 4, 4)
                        remote(
                            self.g.at[rows, block(h, step, u)],
                            self.ra.at[h, j, :, parts[u]],
                            {"core": 1 - c}, self.sent, self.paired + u * 4 + j,
                        ).start()

        def start_first(self, u):
            cut = parts[u]
            for j, step in enumerate(order):
                await_received(self.paired + u * 4 + j, self.ra.at[:, j, :, cut])
                for h in range(2):
                    taps = block(h, step, u)
                    base = c * 8 + h * 4
                    self.g[pl.ds(base, 4), taps] += self.ra[h, j, :, cut]
                    axis, place = near[h]
                    for d in (2, 1, 3):
                        peer = ring(place, d)
                        remote(
                            self.g.at[base + peer, taps],
                            rb.at[self.sec, h, j, d - 1, cut],
                            {axis: peer}, self.sent + 1, self.summed + u * 4 + j,
                        ).start()

        def start_second(self, u):
            cut = parts[u]
            sec = self.sec
            for j, step in enumerate(order):
                await_received(self.summed + u * 4 + j, rb.at[sec, :, j, :, cut])
                for h in range(2):
                    total = self.g[c * 8 + h * 4 + near[h][1], block(h, step, u)]
                    total += rb[sec, h, j, 0, cut] + rb[sec, h, j, 1, cut] + rb[sec, h, j, 2, cut]
                    if step == 0:
                        tt[sec, h, cut] = total
                    else:
                        sb[sec, h, j, cut] = total
                        axis, place = wide[h]
                        remote(
                            sb.at[sec, h, j, cut], rc.at[sec, h, j, cut],
                            {axis: ring(place, step)}, self.sent + 2, self.widened + u,
                        ).start()

        def start_third(self, u):
            cut = parts[u]
            sec = self.sec
            await_received(self.widened + u, rc.at[sec, :, :, cut])
            for h in range(2):
                tt[sec, h, cut] += rc[sec, h, 0, cut] + rc[sec, h, 1, cut] + rc[sec, h, 2, cut]

            @pl.when(seg != sec)
            def _():
                remote(
                    tt.at[sec, :, cut], rd.at[:, cut], {"segment": other},
                    crossing, crossed + u,
                ).start()

        def start_fourth(self, u):
            cut = parts[u]

            @pl.when(seg == self.sec)
            def _():
                await_received(crossed + u, rd.at[:, cut])
                tt[self.sec, :, cut] += rd[:, cut]
                for d in (2, 1, 3):
                    remote(
                        tt.at[self.sec, :, cut], re.at[d - 1, :, cut], {"zh": ring(zh, d)},
                        stacking, stacked + u,
                    ).start()

        def finish(self):
            await_sent(self.sent, self.ra)
            await_sent(self.sent + 1, rb.at[self.sec])
            await_sent(self.sent + 2, sb.at[self.sec])

    crossing, stacking, crossed, stacked = new(sends), new(sends), new(receipts, 2), new(receipts, 2)
    decoder = Sum(1, g1, ra1)
    encoder = Sum(0, g0, ra0)
    decoder.start_pair()
    decoder.start_first(0)
    decoder.start_first(1)

    take_rows(cot_halo)
    build(cext, pch, pcl, 0, 2)
    conv_step(pch, pcl, wct, 0, True)
    take_frames(cot_halo)
    build(cext, pch, pcl, 2, 4)
    for step in (1, 2):
        conv_step(pch, pcl, wct, step, False)
    top, rest = split(acc[...] * slope[...])
    gcat[:, 0:128] = top
    gcat[:, 128:256] = rest
    weight_grad_turned(pth, ptl, g0)
    encoder.start_pair()
    decoder.start_second(0)
    encoder.start_first(0)
    decoder.start_second(1)
    encoder.start_first(1)
    decoder.start_third(0)
    encoder.start_second(0)
    decoder.start_third(1)
    encoder.start_second(1)
    encoder.start_third(0)
    encoder.start_third(1)
    decoder.start_fourth(0)
    decoder.start_fourth(1)
    encoder.start_fourth(0)
    encoder.start_fourth(1)

    spreading, passing, sharing = new(sends), new(sends), new(sends)
    spread, passed, shared = new(receipts, 6), new(receipts, 3), new(receipts)

    def group(h, e):
        return c * 8 + h * 4 + ring(near[h][1], e)

    def pass_on(h, u, d):
        for e in (2, 1, 3):
            piece = full.at[block(h, -d, u), group(h, 0)]
            axis, place = near[h]
            remote(
                uu.at[h, parts[u]] if d == 0 else piece, piece,
                {axis: ring(place, e)}, passing, passed + e - 1,
            ).start()

    for u, cut in enumerate(parts):
        await_received(stacked + u, re.at[:, :, cut])
        for h in range(2):
            total = tt[seg, h, cut] + re[0, h, cut] + re[1, h, cut] + re[2, h, cut]
            uu[h, cut] = total
            axis, place = wide[h]
            for d in (2, 1, 3):
                remote(
                    uu.at[h, cut], full.at[block(h, 0, u), group(h, 0)],
                    {axis: ring(place, d)}, spreading, spread + u * 3 + d - 1,
                ).start()
    for u, cut in enumerate(parts):
        for h in range(2):
            pass_on(h, u, 0)
            full[block(h, 0, u), group(h, 0)] = uu[h, cut]
    for u, cut in enumerate(parts):
        for d in (1, 3, 2):
            await_received(spread + u * 3 + d - 1, uu.at[:, cut])
            for h in range(2):
                pass_on(h, u, d)
    for e in (0, 1, 3, 2):
        if e > 0:
            await_received(passed + e - 1, full.at[:, 0:2])
        for h in range(2):
            whole = full.at[:, group(h, -e)]
            remote(whole, whole, {"core": 1 - c}, sharing, shared).start()
    await_received(shared, ra0)

    decoder.finish()
    encoder.finish()
    await_sent(crossing, rd)
    await_sent(stacking, re)
    await_sent(spreading, re)
    await_sent(passing, rb.at[0])
    await_sent(sharing, ra0)

    @pl.when(seg == 0)
    def _():
        await_sent(w_sent, wboth.at[0, 0:4 * 288])
        await_sent(w_passed, wboth.at[0, 0:6 * 288])
        for copy, gives, _ in help_rows:
            pl.when(gives)(copy.wait_send)
        help_sum.wait_send()

    @pl.when(seg == 1)
    def _():
        await_sent(w_sent, wboth.at[0, 0:6 * 288])
        await_sent(w_passed, wboth.at[0, 0:4 * 288])

    assert sends[0] <= SENDS and receipts[0] <= RECEIPTS, (sends, receipts)


def write_out(full, out_ref, sems):
    copies = [
        pltpu.make_async_copy(full.at[pl.ds(k * 3, 3)], out_ref.at[pl.ds(k * 3, 3)], sems.at[k])
        for k in range(9)
    ]
    for copy in copies:
        copy.start()
    for copy in copies:
        copy.wait()


def local(video_clips, conv_weights):
    vm = pltpu.VMEM
    ext = vm((4, 6, 32, 128), F32)
    patches = vm((512, 1152), BF16)
    wcat = vm((3456, 256), BF16)
    grads = vm((GROUPS, PAD, 8, 128), F32)
    quarters = vm((2, 4, 4, 7, 8, 128), F32)
    summed = pl.pallas_call(
        kernel,
        out_shape=pltpu.VMEM((PAD, GROUPS, 8, 128), F32),
        in_specs=[pl.BlockSpec(memory_space=pl.ANY)] * 2,
        out_specs=pl.BlockSpec(memory_space=pltpu.VMEM),
        scratch_shapes=[
            ext, ext, ext, vm((2, 6, 32, 128), F32), vm((256, 128), F32), vm((256, 128), F32),
            patches, patches, patches, patches, patches, patches,
            vm((1152, 512), BF16), vm((1152, 512), BF16),
            vm((2, 3456, 128), F32), wcat, wcat, wcat,
            vm((256, 128), F32), vm((256, 128), F32), vm((256, 256), BF16),
            grads, grads, quarters, quarters,
            vm((2, 2, 4, 3, 7, 8, 128), F32),
            vm((2, 2, 3, 7, 8, 128), F32),
            vm((2, 2, 3, 7, 8, 128), F32),
            vm((2, 2, 7, 8, 128), F32),
            vm((2, 7, 8, 128), F32),
            vm((3, 2, 7, 8, 128), F32),
            vm((2, 7, 8, 128), F32),
            pltpu.SemaphoreType.DMA((3,)),
            pltpu.SemaphoreType.DMA((SENDS,)),
            pltpu.SemaphoreType.DMA((RECEIPTS,)),
        ],
        compiler_params=pltpu.CompilerParams(
            collective_id=0, has_side_effects=True, vmem_limit_bytes=60 * 1024 * 1024
        ),
        name="step",
    )(video_clips, conv_weights)
    copied = pl.pallas_call(
        write_out,
        out_shape=jax.ShapeDtypeStruct((TAPS, GROUPS, 8, 128), F32),
        in_specs=[pl.BlockSpec(memory_space=pltpu.VMEM)],
        out_specs=pl.BlockSpec(memory_space=pl.ANY),
        scratch_shapes=[pltpu.SemaphoreType.DMA((9,))],
        name="write_out",
    )(pltpu.with_memory_space_constraint(summed, pltpu.VMEM))
    return copied.reshape(1, TAPS * 128, 128)


def solution(mesh):
    finer = Mesh(
        mesh.devices.reshape(mesh.shape["segment"], mesh.shape["tm"], 4, 4, 2), AXES
    )
    in_specs = (P(None, "tm", ("zh", "y", "core"), None, None), P("segment", None, None))
    return jax.shard_map(
        local, mesh=finer, in_specs=in_specs, out_specs=P("segment", None, None), check_vma=False
    )
```

```python
import jax
import jax.numpy as jnp
from jax import lax
from jax.experimental import pallas as pl
from jax.experimental.pallas import tpu as pltpu
from jax.sharding import Mesh
from jax.sharding import PartitionSpec as P

MESH = pl.DeviceIdType.MESH
AXES = ("segment", "tm", "zh", "y", "core")
F32 = jnp.float32
BF16 = jnp.bfloat16
TAPS = 27
PAD = 28
GROUPS = 16
NEAR_ROWS = 256
FAR_ROWS = 320
EVEN_ROWS = 288
SENDS = 22
RECEIPTS = 79


def kernel(
    vid_ref, w_ref, full,
    vext, lext, cext, uext, mix, part_sum,
    pvh, pvl, plh, pll, pch, pcl, pth, ptl,
    wboth, wc0, wc1, wct,
    acc, slope, gcat,
    g0, g1, ra0, ra1, rb, sb, rc, tt, rd, re, uu,
    local_sem, send_sem, recv_sem,
):
    seg = lax.axis_index("segment")
    x = lax.axis_index("tm")
    zh = lax.axis_index("zh")
    y = lax.axis_index("y")
    c = lax.axis_index("core")
    s = zh * 8 + y * 2 + c
    sends, receipts = [0], [0]

    def new(counter, count=1):
        counter[0] += count
        return counter[0] - count

    def spot(index, **others):
        index = lax.rem(index + 32, 32)
        return {"zh": index // 8, "y": lax.rem(index // 2, 4), "core": lax.rem(index, 2), **others}

    def ring(value, step):
        return lax.rem(value + step + 4, 4)

    other = 1 - seg
    link_b = ring(zh, 2 * seg - 1)

    def remote(src, dst, device, sent=None, received=None):
        sent = new(sends) if sent is None else sent
        received = new(receipts) if received is None else received
        return pltpu.make_async_remote_copy(
            src_ref=src,
            dst_ref=dst,
            send_sem=send_sem.at[sent],
            recv_sem=recv_sem.at[received],
            device_id=device,
            device_id_type=MESH,
        )

    def await_sent(slot, like):
        pltpu.make_async_copy(like, like, send_sem.at[slot]).wait()

    def await_received(slot, like):
        pltpu.make_async_copy(like, like, recv_sem.at[slot]).wait()

    own_w = pltpu.make_async_copy(w_ref.at[0], wboth.at[seg], local_sem.at[0])
    own_v = pltpu.make_async_copy(vid_ref.at[seg], vext.at[2:4, 1:5], local_sem.at[1])
    helped = pltpu.make_async_copy(vid_ref.at[1], uext.at[:, 1:5], local_sem.at[2])
    pl.when(seg == 0)(helped.start)
    own_v.start()
    own_w.start()
    for rim, line in ((s == 0, 0), (s == 31, 5)):
        @pl.when(rim)
        def _():
            uext[:, line] = jnp.zeros((2, 32, 128), F32)

    for ext, edge, far in ((vext, x == 0, 0), (lext, x == 0, 0), (cext, x == 3, 2)):
        @pl.when(edge)
        def _():
            ext[far:far + 2] = jnp.zeros((2, 6, 32, 128), F32)

        for rim, line in ((s == 0, 0), (s == 31, 5)):
            @pl.when(rim)
            def _():
                ext[:, line] = jnp.zeros((4, 32, 128), F32)

    for g in (g0, g1):
        g[:, TAPS] = jnp.zeros((GROUPS, 8, 128), F32)

    barrier = pltpu.get_barrier_semaphore()
    greet = [{"tm": ring(x, d)} for d in (1, 2, 3)]
    greet += [{"y": ring(y, d)} for d in (1, 2, 3)]
    greet += [{"zh": ring(zh, d)} for d in (1, 2, 3)]
    greet += [{"core": 1 - c}, {"segment": other}, {"segment": other, "zh": link_b}]
    greet += [spot(s + 1), spot(s - 1)]
    greet += [spot(s + dy, tm=ring(x, dx)) for dy in (1, -1) for dx in (1, -1)]
    for device in greet:
        pl.semaphore_signal(barrier, inc=1, device_id=device, device_id_type=MESH)
    pl.semaphore_wait(barrier, len(greet))

    shares = ((NEAR_ROWS, FAR_ROWS), (EVEN_ROWS, EVEN_ROWS))

    def quarter(sender, step, part, core):
        count = shares[sender][part]
        return pl.ds(step * 1152 + part * 2 * shares[sender][0] + core * count, count)

    w_sent, w_passed = new(sends), new(sends)
    w_got, w_shared = new(receipts, 3), new(receipts, 3)

    def send_weights(sender, step, part):
        rows = quarter(sender, step, part, c)
        device = {"segment": other} if part == 0 else {"segment": other, "zh": link_b}
        remote(w_ref.at[0, rows], wboth.at[seg, rows], device, w_sent, w_got + step).start()

    def relay_weights(sender, step, part):
        rows = quarter(sender, step, part, c)
        remote(
            wboth.at[other, rows], wboth.at[other, rows], {"core": 1 - c},
            w_passed, w_shared + step,
        ).start()

    halo_sent = new(sends, 6)

    def halo(ext, own, far, shift):
        ahead = {"tm": ring(x, shift)}
        sends_x = (x < 3) if shift == 1 else (x > 0)
        gets_x = (x > 0) if shift == 1 else (x < 3)
        frames, beyond = slice(own, own + 2), slice(far, far + 2)
        inner, outer = 4 - 3 * c, 1 + 3 * c
        up, down = (s < 31), (s > 0)
        edge = jnp.logical_or(jnp.logical_and(c == 1, up), jnp.logical_and(c == 0, down))
        corner = remote(
            ext.at[frames, outer], ext.at[beyond, 5 - 5 * c], spot(s + 2 * c - 1, **ahead),
            halo_sent,
        )
        rest = pl.ds(1 + c, 3)
        moves = {
            "first": (remote(ext.at[frames, inner], ext.at[beyond, inner], ahead, halo_sent + 1), sends_x, gets_x),
            "next": (remote(ext.at[frames, 4], ext.at[frames, 0], spot(s + 1), halo_sent + 2), up, down),
            "last": (remote(ext.at[frames, 1], ext.at[frames, 5], spot(s - 1), halo_sent + 3), down, up),
            "corner": (corner, jnp.logical_and(edge, sends_x), jnp.logical_and(edge, gets_x)),
            "rest": (remote(ext.at[frames, rest], ext.at[beyond, rest], ahead, halo_sent + 4), sends_x, gets_x),
            "pass": (
                remote(ext.at[beyond, inner], ext.at[beyond, 5 * c], {"core": 1 - c}, halo_sent + 5),
                gets_x, gets_x,
            ),
        }
        return moves

    def start_halo(moves):
        for name, (copy, gives, _) in moves.items():
            if name != "pass":
                pl.when(gives)(copy.start)

    def take_rows(moves):
        first, _, gets = moves["first"]

        @pl.when(gets)
        def _():
            first.wait_recv()
            moves["pass"][0].start()

        for name in ("next", "last"):
            copy, _, gets = moves[name]
            pl.when(gets)(copy.wait_recv)

    def take_frames(moves):
        for name in ("corner", "rest", "pass"):
            copy, _, gets = moves[name]
            pl.when(gets)(copy.wait_recv)
        for copy, gives, _ in moves.values():
            pl.when(gives)(copy.wait_send)

    help_rows = (
        (remote(uext.at[:, 4], uext.at[:, 0], spot(s + 1)), s < 31, s > 0),
        (remote(uext.at[:, 1], uext.at[:, 5], spot(s - 1)), s > 0, s < 31),
    )
    help_sum = remote(mix, part_sum, {"segment": other})

    @pl.when(seg == 0)
    def _():
        helped.wait()
        for copy, gives, _ in help_rows:
            pl.when(gives)(copy.start)

    own_v.wait()
    video_halo = halo(vext, 2, 0, 1)
    start_halo(video_halo)
    for sender, steps in ((0, (1, 0)), (1, (2, 1, 0))):
        @pl.when(seg == sender)
        def _():
            for step in steps:
                for part in range(2):
                    send_weights(sender, step, part)

    column = lax.broadcasted_iota(jnp.int32, (32, 128), 0)

    def build(ext, high, low, start, stop):
        @pl.loop(start, stop)
        def _(frame):
            base = pl.multiple_of(frame * 128, 128)
            for line in range(6):
                value = ext[frame, line]
                for e in range(3):
                    if e == 0:
                        moved = jnp.where(column == 0, 0.0, pltpu.roll(value, 1, 0))
                    elif e == 2:
                        moved = jnp.where(column == 31, 0.0, pltpu.roll(value, 31, 0))
                    else:
                        moved = value
                    top = moved.astype(BF16)
                    rest = (moved - top.astype(F32)).astype(BF16)
                    for b in range(3):
                        r = line - b
                        if 0 <= r < 4:
                            lanes = slice((b * 3 + e) * 128, (b * 3 + e + 1) * 128)
                            high[pl.ds(base + r * 32, 32), lanes] = top
                            low[pl.ds(base + r * 32, 32), lanes] = rest

    def split(value):
        top = value.astype(BF16)
        return top, (value - top.astype(F32)).astype(BF16)

    def product(high, low, weight, first, step):
        rows = pl.ds(first * 128, 256)
        lines = pl.ds(step * 1152, 1152)
        both = jnp.dot(high[rows, :], weight[lines, :], preferred_element_type=F32)
        rest = jnp.dot(low[rows, :], weight[lines, 0:128], preferred_element_type=F32)
        return both[:, 0:128] + both[:, 128:256] + rest

    def conv_step(high, low, weight, step, first):
        total = product(high, low, weight, step, step)
        if first:
            acc[...] = total
        else:
            acc[...] += total

    def place_grad(g, step, both, rest):
        total = both[:, 0:128] + both[:, 128:256] + rest
        for k in range(9):
            g[:, step * 9 + k] = total[k * 128:(k + 1) * 128].reshape(GROUPS, 8, 128)

    def weight_grad(high, low, g):
        @pl.loop(0, 3)
        def _(step):
            rows = pl.ds(pl.multiple_of(step * 128, 128), 256)
            dims = (((0,), (0,)), ((), ()))
            both = lax.dot_general(high[rows, :], gcat[...], dims, preferred_element_type=F32)
            rest = lax.dot_general(
                low[rows, :], gcat[:, 0:128], dims, preferred_element_type=F32
            )
            place_grad(g, step, both, rest)

    def weight_grad_turned(high, low, g):
        @pl.loop(0, 3)
        def _(step):
            cells = pl.ds(pl.multiple_of(step * 128, 128), 256)
            both = jnp.dot(high[:, cells], gcat[...], preferred_element_type=F32)
            rest = jnp.dot(low[:, cells], gcat[:, 0:128], preferred_element_type=F32)
            place_grad(g, step, both, rest)

    def prepare(start, stop, section):
        @pl.loop(start, stop)
        def _(tap):
            rows = pl.ds(pl.multiple_of(tap * 128, 128), 128)
            value = wboth[section, rows]
            places = [(value, (wc0, wc1)[section], rows)]
            if section == 1:
                flipped = pl.ds(pl.multiple_of((TAPS - 1 - tap) * 128, 128), 128)
                places.append((value.T, wct, flipped))
            for part, ref, place in places:
                top, rest = split(part)
                ref[place, 0:128] = top
                ref[place, 128:256] = rest

    own_w.wait()
    pl.when(seg == 0)(lambda: prepare(0, TAPS, 0))
    pl.when(seg == 1)(lambda: prepare(0, TAPS, 1))

    @pl.when(seg == 0)
    def _():
        for copy, _, gets in help_rows:
            pl.when(gets)(copy.wait_recv)
        build(uext, plh, pll, 0, 2)
        mix[...] = product(plh, pll, wc0, 0, 2)
        help_sum.start()

    take_rows(video_halo)
    take_frames(video_halo)
    build(vext, pvh, pvl, 0, 4)

    latent_halo = halo(lext, 2, 0, 1)

    def encode():
        hidden = acc[...]
        sigmoid = 1.0 / (1.0 + jnp.exp(-hidden))
        slope[...] = sigmoid * (1.0 + hidden * (1.0 - sigmoid))
        lext[2:4, 1:5] = (hidden / (1.0 + jnp.exp(-hidden))).reshape(2, 4, 32, 128)
        start_halo(latent_halo)

    @pl.when(seg == 0)
    def _():
        for step in range(3):
            conv_step(pvh, pvl, wc0, step, step == 0)
        encode()

    @pl.loop(0, 9)
    def _(k):
        lanes = pl.ds(pl.multiple_of(k * 128, 128), 128)
        for source, turned in ((pvh, pth), (pvl, ptl)):
            turned[lanes, :] = source[:, lanes].T

    def take(sender, step):
        await_received(w_got + step, wboth.at[other, 0:576])
        for part in range(2):
            relay_weights(sender, step, part)
        await_received(w_shared + step, wboth.at[other, 0:576])

    @pl.when(seg == 0)
    def _():
        for step in (2, 1, 0):
            take(1, step)
            prepare(step * 9, step * 9 + 9, 1)

    @pl.when(seg == 1)
    def _():
        for step in (1, 0):
            take(0, step)
            prepare(step * 9, step * 9 + 9, 0)
            conv_step(pvh, pvl, wc0, step, step == 1)
        help_sum.wait_recv()
        acc[...] += part_sum[...]
        encode()

    take_rows(latent_halo)
    build(lext, plh, pll, 2, 4)
    conv_step(plh, pll, wc1, 2, True)
    take_frames(latent_halo)
    build(lext, plh, pll, 0, 2)
    for step in (1, 0):
        conv_step(plh, pll, wc1, step, False)
    cot = (acc[...] - vext[2:4, 1:5].reshape(256, 128)) * (65536.0 ** -0.5)
    cext[0:2, 1:5] = cot.reshape(2, 4, 32, 128)
    cot_halo = halo(cext, 0, 2, -1)
    start_halo(cot_halo)
    top, rest = split(cot)
    gcat[:, 0:128] = top
    gcat[:, 128:256] = rest
    weight_grad(plh, pll, g1)

    near = (("tm", x), ("y", y))
    wide = (("y", y), ("tm", x))
    order = (2, 1, 3, 0)
    parts = (slice(0, 4), slice(4, 7))

    def block(h, step, u):
        cut = parts[u]
        return pl.ds(ring(wide[h][1], step) * 7 + cut.start, cut.stop - cut.start)

    class Sum:
        def __init__(self, sec, g, ra):
            self.sec, self.g, self.ra = sec, g, ra
            self.sent = new(sends, 3)
            self.paired = new(receipts, 8)
            self.summed = new(receipts, 8)
            self.widened = new(receipts, 2)

        def start_pair(self):
            for u in range(2):
                for j, step in enumerate(order):
                    for h in range(2):
                        rows = pl.ds((1 - c) * 8 + h * 4, 4)
                        remote(
                            self.g.at[rows, block(h, step, u)],
                            self.ra.at[h, j, :, parts[u]],
                            {"core": 1 - c}, self.sent, self.paired + u * 4 + j,
                        ).start()

        def start_first(self, u):
            cut = parts[u]
            for j, step in enumerate(order):
                await_received(self.paired + u * 4 + j, self.ra.at[:, j, :, cut])
                for h in range(2):
                    taps = block(h, step, u)
                    base = c * 8 + h * 4
                    self.g[pl.ds(base, 4), taps] += self.ra[h, j, :, cut]
                    axis, place = near[h]
                    for d in (2, 1, 3):
                        peer = ring(place, d)
                        remote(
                            self.g.at[base + peer, taps],
                            rb.at[self.sec, h, j, d - 1, cut],
                            {axis: peer}, self.sent + 1, self.summed + u * 4 + j,
                        ).start()

        def start_second(self, u):
            cut = parts[u]
            sec = self.sec
            for j, step in enumerate(order):
                await_received(self.summed + u * 4 + j, rb.at[sec, :, j, :, cut])
                for h in range(2):
                    total = self.g[c * 8 + h * 4 + near[h][1], block(h, step, u)]
                    total += rb[sec, h, j, 0, cut] + rb[sec, h, j, 1, cut] + rb[sec, h, j, 2, cut]
                    if step == 0:
                        tt[sec, h, cut] = total
                    else:
                        sb[sec, h, j, cut] = total
                        axis, place = wide[h]
                        remote(
                            sb.at[sec, h, j, cut], rc.at[sec, h, j, cut],
                            {axis: ring(place, step)}, self.sent + 2, self.widened + u,
                        ).start()

        def start_third(self, u):
            cut = parts[u]
            sec = self.sec
            await_received(self.widened + u, rc.at[sec, :, :, cut])
            for h in range(2):
                tt[sec, h, cut] += rc[sec, h, 0, cut] + rc[sec, h, 1, cut] + rc[sec, h, 2, cut]

            @pl.when(seg != sec)
            def _():
                remote(
                    tt.at[sec, :, cut], rd.at[:, cut], {"segment": other},
                    crossing, crossed + u,
                ).start()

        def start_fourth(self, u):
            cut = parts[u]

            @pl.when(seg == self.sec)
            def _():
                await_received(crossed + u, rd.at[:, cut])
                tt[self.sec, :, cut] += rd[:, cut]
                for d in (2, 1, 3):
                    remote(
                        tt.at[self.sec, :, cut], re.at[d - 1, :, cut], {"zh": ring(zh, d)},
                        stacking, stacked + u,
                    ).start()

        def finish(self):
            await_sent(self.sent, self.ra)
            await_sent(self.sent + 1, rb.at[self.sec])
            await_sent(self.sent + 2, sb.at[self.sec])

    crossing, stacking, crossed, stacked = new(sends), new(sends), new(receipts, 2), new(receipts, 2)
    decoder = Sum(1, g1, ra1)
    encoder = Sum(0, g0, ra0)
    decoder.start_pair()
    decoder.start_first(0)
    decoder.start_first(1)

    take_rows(cot_halo)
    build(cext, pch, pcl, 0, 2)
    conv_step(pch, pcl, wct, 0, True)
    take_frames(cot_halo)
    build(cext, pch, pcl, 2, 4)
    for step in (1, 2):
        conv_step(pch, pcl, wct, step, False)
    top, rest = split(acc[...] * slope[...])
    gcat[:, 0:128] = top
    gcat[:, 128:256] = rest
    weight_grad_turned(pth, ptl, g0)
    encoder.start_pair()
    decoder.start_second(0)
    encoder.start_first(0)
    decoder.start_second(1)
    encoder.start_first(1)
    decoder.start_third(0)
    encoder.start_second(0)
    decoder.start_third(1)
    encoder.start_second(1)
    encoder.start_third(0)
    encoder.start_third(1)
    decoder.start_fourth(0)
    decoder.start_fourth(1)
    encoder.start_fourth(0)
    encoder.start_fourth(1)

    spreading, passing, sharing = new(sends), new(sends), new(sends)
    spread, passed, shared = new(receipts, 6), new(receipts, 3), new(receipts)

    def group(h, e):
        return c * 8 + h * 4 + ring(near[h][1], e)

    def pass_on(h, u, d):
        for e in (2, 1, 3):
            piece = full.at[block(h, -d, u), group(h, 0)]
            axis, place = near[h]
            remote(
                uu.at[h, parts[u]] if d == 0 else piece, piece,
                {axis: ring(place, e)}, passing, passed + e - 1,
            ).start()

    for u, cut in enumerate(parts):
        await_received(stacked + u, re.at[:, :, cut])
        for h in range(2):
            total = tt[seg, h, cut] + re[0, h, cut] + re[1, h, cut] + re[2, h, cut]
            uu[h, cut] = total
            axis, place = wide[h]
            for d in (2, 1, 3):
                remote(
                    uu.at[h, cut], full.at[block(h, 0, u), group(h, 0)],
                    {axis: ring(place, d)}, spreading, spread + u * 3 + d - 1,
                ).start()
    for u, cut in enumerate(parts):
        for h in range(2):
            pass_on(h, u, 0)
            full[block(h, 0, u), group(h, 0)] = uu[h, cut]
    for u, cut in enumerate(parts):
        for d in (1, 3, 2):
            await_received(spread + u * 3 + d - 1, uu.at[:, cut])
            for h in range(2):
                pass_on(h, u, d)
    for e in (0, 1, 3, 2):
        if e > 0:
            await_received(passed + e - 1, full.at[:, 0:2])
        for h in range(2):
            whole = full.at[:, group(h, -e)]
            remote(whole, whole, {"core": 1 - c}, sharing, shared).start()
    await_received(shared, ra0)

    decoder.finish()
    encoder.finish()
    await_sent(crossing, rd)
    await_sent(stacking, re)
    await_sent(spreading, re)
    await_sent(passing, rb.at[0])
    await_sent(sharing, ra0)

    @pl.when(seg == 0)
    def _():
        await_sent(w_sent, wboth.at[0, 0:4 * 288])
        await_sent(w_passed, wboth.at[0, 0:6 * 288])
        for copy, gives, _ in help_rows:
            pl.when(gives)(copy.wait_send)
        help_sum.wait_send()

    @pl.when(seg == 1)
    def _():
        await_sent(w_sent, wboth.at[0, 0:6 * 288])
        await_sent(w_passed, wboth.at[0, 0:4 * 288])

    assert sends[0] <= SENDS and receipts[0] <= RECEIPTS, (sends, receipts)


def write_out(full, out_ref, sems):
    copies = [
        pltpu.make_async_copy(full.at[pl.ds(k * 3, 3)], out_ref.at[pl.ds(k * 3, 3)], sems.at[k])
        for k in range(9)
    ]
    for copy in copies:
        copy.start()
    for copy in copies:
        copy.wait()


def local(video_clips, conv_weights):
    vm = pltpu.VMEM
    ext = vm((4, 6, 32, 128), F32)
    patches = vm((512, 1152), BF16)
    wcat = vm((3456, 256), BF16)
    grads = vm((GROUPS, PAD, 8, 128), F32)
    quarters = vm((2, 4, 4, 7, 8, 128), F32)
    summed = pl.pallas_call(
        kernel,
        out_shape=pltpu.VMEM((PAD, GROUPS, 8, 128), F32),
        in_specs=[pl.BlockSpec(memory_space=pl.ANY)] * 2,
        out_specs=pl.BlockSpec(memory_space=pltpu.VMEM),
        scratch_shapes=[
            ext, ext, ext, vm((2, 6, 32, 128), F32), vm((256, 128), F32), vm((256, 128), F32),
            patches, patches, patches, patches, patches, patches,
            vm((1152, 512), BF16), vm((1152, 512), BF16),
            vm((2, 3456, 128), F32), wcat, wcat, wcat,
            vm((256, 128), F32), vm((256, 128), F32), vm((256, 256), BF16),
            grads, grads, quarters, quarters,
            vm((2, 2, 4, 3, 7, 8, 128), F32),
            vm((2, 2, 3, 7, 8, 128), F32),
            vm((2, 2, 3, 7, 8, 128), F32),
            vm((2, 2, 7, 8, 128), F32),
            vm((2, 7, 8, 128), F32),
            vm((3, 2, 7, 8, 128), F32),
            vm((2, 7, 8, 128), F32),
            pltpu.SemaphoreType.DMA((3,)),
            pltpu.SemaphoreType.DMA((SENDS,)),
            pltpu.SemaphoreType.DMA((RECEIPTS,)),
        ],
        compiler_params=pltpu.CompilerParams(
            collective_id=0, has_side_effects=True, vmem_limit_bytes=60 * 1024 * 1024
        ),
        name="step",
    )(video_clips, conv_weights)
    copied = pl.pallas_call(
        write_out,
        out_shape=jax.ShapeDtypeStruct((TAPS, GROUPS, 8, 128), F32),
        in_specs=[pl.BlockSpec(memory_space=pltpu.VMEM)],
        out_specs=pl.BlockSpec(memory_space=pl.ANY),
        scratch_shapes=[pltpu.SemaphoreType.DMA((9,))],
        name="write_out",
    )(pltpu.with_memory_space_constraint(summed, pltpu.VMEM))
    return copied.reshape(1, TAPS * 128, 128)


def solution(mesh):
    finer = Mesh(
        mesh.devices.reshape(mesh.shape["segment"], mesh.shape["tm"], 4, 4, 2), AXES
    )
    in_specs = (P(None, "tm", ("zh", "y", "core"), None, None), P("segment", None, None))
    return jax.shard_map(
        local, mesh=finer, in_specs=in_specs, out_specs=P("segment", None, None), check_vma=False
    )
```
